32 devices in a mesh: seq: 4 (over x, core), clip: 8 (over z, y).
Axes of the slice: x: 2, y: 2, z: 4, core: 2. Of those that a mesh axis runs over, the one named last changes fastest.
Arguments:
- x_vis: bfloat16 [24, 157, 768], P('clip'), may hold values from -6 to 6
- vis_pos: int32 [24, 157], P('clip'), may hold values from 0 to 1567, as said below
- w_proj: bfloat16 [768, 384], replicated, may hold values from -0.21875 to 0.21875
- b_proj: float32 [384], replicated, may hold values from -3 to 3
- mask_token: float32 [384], replicated, may hold values from -4 to 4
- ln1_gain: float32 [384], replicated, may hold values from 0.25 to 1.75
- ln1_bias: float32 [384], replicated, may hold values from -2 to 2
- w_qkv: bfloat16 [384, 1152], replicated, may hold values from -0.3125 to 0.3125
- q_bias: float32 [384], replicated, may hold values from -2 to 2
- v_bias: float32 [384], replicated, may hold values from -3 to 3
- w_out: bfloat16 [384, 384], replicated, may hold values from -4 to 4
- b_out: float32 [384], replicated, may hold values from -2 to 2
- ln2_gain: float32 [384], replicated, may hold values from 0.25 to 1.75
- ln2_bias: float32 [384], replicated, may hold values from -2 to 2
- w_fc1: bfloat16 [384, 1536], replicated, may hold values from -0.3125 to 0.3125
- b_fc1: float32 [1536], replicated, may hold values from -3 to 3
- w_fc2: bfloat16 [1536, 384], replicated, may hold values from -0.15625 to 0.15625
- b_fc2: float32 [384], replicated, may hold values from -2 to 2
- cotangent: bfloat16 [24, 1568, 384], P('clip', 'seq'), may hold values from -6 to 6
Outputs:
- output: bfloat16 [24, 1568, 384], P('clip', 'seq')
- grad_x: float32 [24, 157, 768], P('clip')
- grad_w_proj: float32 [768, 384], replicated
- grad_b_proj: float32 [384], replicated
- grad_mask: float32 [384], replicated
- grad_ln1_gain: float32 [384], replicated
- grad_ln1_bias: float32 [384], replicated
- grad_w_qkv: float32 [384, 1152], replicated
- grad_q_bias: float32 [384], replicated
- grad_v_bias: float32 [384], replicated
- grad_w_out: float32 [384, 384], replicated
- grad_b_out: float32 [384], replicated
- grad_ln2_gain: float32 [384], replicated
- grad_ln2_bias: float32 [384], replicated
- grad_w_fc1: float32 [384, 1536], replicated
- grad_b_fc1: float32 [1536], replicated
- grad_w_fc2: float32 [1536, 384], replicated
- grad_b_fc2: float32 [384], replicated
- trust: float32 [4], replicated
- trust_qkv: float32 [1], replicated
The draws below stay inside these ranges and needn't reach their ends.
Inputs may be any that keep to these rules, and one draw needn't show every extreme that they name: `vis_pos`: each clip's 157 visible positions, in rising order, all different.
All inputs are finite; a program needn't handle non-finite values.
Results may differ from the reference program's by a relative error of at most 0.01.
Values may be sent and summed in bfloat16 or wider, within the bound.
No kernel may reach another device: no remote copies, remote signals or barrier semaphores. Data moves between devices by JAX's collectives and lax.ppermute only.
A program may use at most 256 MiB of HBM per device.

```python
import jax
import jax.numpy as jnp
from jax import lax

DIN = 768
D = 384
HEADS = 6
HEAD = 64
FF = 1536
LEN = 1568
VIS = 157
CLIPS = 24


def draw_vis_pos(key, part):
    clip_keys = jax.random.split(key, CLIPS)
    shuffled = jax.vmap(lambda single: jax.random.permutation(single, LEN))(clip_keys)
    return jnp.sort(shuffled[:, :VIS], axis=1).astype(jnp.int32)


def level_of(rng, shape, cuts, smallest, largest):
    def one(dim, parts):
        steps = jax.random.uniform(jax.random.fold_in(jax.random.fold_in(rng, 6), dim), (parts,), jnp.float32, smallest / len(cuts), largest / len(cuts))
        return jnp.repeat(jnp.exp(steps), shape[dim] // parts).reshape((-1,) + (1,) * (len(shape) - dim - 1))

    loudness = one(*cuts[0])
    for cut in cuts[1:]:
        loudness = loudness * one(*cut)
    return loudness


def noise(key, shape, scale, bound, shards=(), kind=jnp.bfloat16):
    entries = scale * jax.random.normal(key, shape, jnp.float32)
    if shards:
        entries = entries * level_of(key, shape, shards, -0.22, 0.18)
    return jnp.clip(entries, -bound, bound).astype(kind)


def setup_inputs(seed: int = 0) -> dict:
    splits = jax.random.split(jax.random.key(seed), 20)
    return {
        "x_vis": noise(splits[0], (CLIPS, VIS, DIN), 1.0, 6.0, ((0, 8),)),
        "vis_pos": draw_vis_pos(jax.random.fold_in(splits[19], 71), 0),
        "w_proj": noise(splits[2], (DIN, D), DIN ** -0.5, 0.21875),
        "b_proj": noise(splits[3], (D,), 0.5, 3.0, (), jnp.float32),
        "mask_token": noise(splits[4], (D,), 1.0, 4.0, (), jnp.float32),
        "ln1_gain": jnp.clip(1.0 + 0.15 * jax.random.normal(splits[5], (D,), jnp.float32), 0.25, 1.75),
        "ln1_bias": noise(splits[6], (D,), 0.3, 2.0, (), jnp.float32),
        "w_qkv": noise(splits[7], (D, 3 * D), D ** -0.5, 0.3125),
        "q_bias": noise(splits[8], (D,), 0.3, 2.0, (), jnp.float32),
        "v_bias": noise(splits[9], (D,), 0.5, 3.0, (), jnp.float32),
        "w_out": noise(splits[10], (D, D), 2 ** -0.5, 4.0),
        "b_out": noise(splits[11], (D,), 0.3, 2.0, (), jnp.float32),
        "ln2_gain": jnp.clip(1.0 + 0.15 * jax.random.normal(splits[12], (D,), jnp.float32), 0.25, 1.75),
        "ln2_bias": noise(splits[13], (D,), 0.3, 2.0, (), jnp.float32),
        "w_fc1": noise(splits[14], (D, FF), D ** -0.5, 0.3125),
        "b_fc1": noise(splits[15], (FF,), 0.5, 3.0, (), jnp.float32),
        "w_fc2": noise(splits[16], (FF, D), FF ** -0.5, 0.15625),
        "b_fc2": noise(splits[17], (D,), 0.3, 2.0, (), jnp.float32),
        "cotangent": noise(splits[18], (CLIPS, LEN, D), 1.0, 6.0, ((0, 8), (1, 4))),
    }


@jax.custom_vjp
def low(v):
    return lax.optimization_barrier(v.astype(jnp.bfloat16)).astype(jnp.float32)

@jax.custom_vjp
def low_back(v):
    return v

def low_keep(v):
    return (low(v), None)

def low_pass(kept, grad):
    return (grad,)

def back_keep(v):
    return (v, None)

def back_low(kept, grad):
    return (low(grad),)
low.defvjp(low_keep, low_pass)
low_back.defvjp(back_keep, back_low)
exact_prec = lax.Precision.HIGHEST

def matmul(left, right):
    return jnp.dot(left, right, precision=exact_prec, preferred_element_type=jnp.float32)

def sinusoid(length, columns):
    positions = jnp.arange(length, dtype=jnp.float32)[:, None]
    column = jnp.arange(columns, dtype=jnp.int32)
    exponent = (2 * (column // 2)).astype(jnp.float32) / columns
    angles = positions / jnp.power(10000.0, exponent)[None, :]
    return jnp.where((column % 2)[None, :] == 0, jnp.sin(angles), jnp.cos(angles))

def layer_norm(inputs, gain_vec, shift_vec):
    average = lax.optimization_barrier(jnp.mean(inputs, axis=-1, keepdims=True))
    centered = inputs - average
    variance = lax.optimization_barrier(jnp.mean(centered * centered, axis=-1, keepdims=True))
    return centered * lax.rsqrt(variance + 1e-05) * gain_vec + shift_vec

def forward_clip(params, inputs, places):
    w_proj, b_proj, mask_token, ln1_gain, ln1_bias, w_qkv, q_bias, v_bias, w_out, b_out, ln2_gain, ln2_bias, w_fc1, b_fc1, w_fc2, b_fc2 = params
    projected = low_back(matmul(inputs, w_proj) + b_proj)
    onehot = (places[None, :] == jnp.arange(LEN, dtype=jnp.int32)[:, None]).astype(jnp.float32)
    visible = lax.optimization_barrier(jnp.sum(onehot, axis=1, keepdims=True))
    embedded = matmul(onehot, projected) + (1.0 - visible) * mask_token + sinusoid(LEN, D)
    normed = low(layer_norm(embedded, ln1_gain, ln1_bias))
    qkv_mixed = matmul(normed, w_qkv)
    queries = low(low_back(qkv_mixed[:, :D] + q_bias))
    keys_all = low(low_back(qkv_mixed[:, D:2 * D]))
    values_all = low(low_back(qkv_mixed[:, 2 * D:] + v_bias))
    q_heads = queries.reshape(LEN, HEADS, HEAD)
    k_heads = keys_all.reshape(LEN, HEADS, HEAD)
    v_heads = values_all.reshape(LEN, HEADS, HEAD)
    scores = low_back(jnp.einsum('qhe,khe->hqk', q_heads, k_heads, precision=exact_prec) * HEAD ** (-0.5))
    attn_probs = low(jax.nn.softmax(scores, axis=-1))
    attended = jnp.einsum('hqk,khe->qhe', attn_probs, v_heads, precision=exact_prec).reshape(LEN, D)
    attended = low(low_back(attended))
    branch = low_back(matmul(attended, w_out) + b_out)
    middle = embedded + branch
    normed2 = low(layer_norm(middle, ln2_gain, ln2_bias))
    hidden_pre = low_back(matmul(normed2, w_fc1) + b_fc1)
    hidden = low(jax.nn.gelu(hidden_pre, approximate=False))
    return middle + matmul(hidden, w_fc2) + b_fc2

def reference(x_vis, vis_pos, w_proj, b_proj, mask_token, ln1_gain, ln1_bias, w_qkv, q_bias, v_bias, w_out, b_out, ln2_gain, ln2_bias, w_fc1, b_fc1, w_fc2, b_fc2, cotangent):
    params = tuple((tensor.astype(jnp.float32) for tensor in (w_proj, b_proj, mask_token, ln1_gain, ln1_bias, w_qkv, q_bias, v_bias, w_out, b_out, ln2_gain, ln2_bias, w_fc1, b_fc1, w_fc2, b_fc2)))
    initial = tuple((jnp.zeros_like(tensor) for tensor in params))

    def one_clip(totals, sliced):
        inputs, places, upstream = sliced

        def closed(weights_in, inputs_in):
            return forward_clip(weights_in, inputs_in, places)
        result, pullback = jax.vjp(closed, params, inputs.astype(jnp.float32))
        grad_params, grad_inputs = pullback(upstream.astype(jnp.float32))
        totals = tuple((first + second for first, second in zip(totals, grad_params)))
        return (totals, (result.astype(jnp.bfloat16), grad_inputs))
    totals, (outputs, grad_inputs) = lax.scan(one_clip, initial, (x_vis, vis_pos, cotangent))
    trust_all = jnp.stack([jnp.sqrt(jnp.mean(params[position] ** 2)) / jnp.sqrt(jnp.mean(totals[position] ** 2) + 1e-06) for position in (0, 5, 8, 12, 14)])
    trust = jnp.concatenate([trust_all[:1], trust_all[2:]])
    trust_qkv = trust_all[1:2]
    return (outputs, grad_inputs, totals[0], totals[1], totals[2], totals[3], totals[4], totals[5], totals[6], totals[7], totals[8], totals[9], totals[10], totals[11], totals[12], totals[13], totals[14], totals[15], trust, trust_qkv)
```

```python
import functools

import jax
import jax.numpy as jnp
import numpy as np
from jax import lax
from jax.experimental import pallas as pl
from jax.experimental.pallas import tpu as pltpu
from jax.sharding import PartitionSpec as P

D = 384
HEADS = 6
HEAD = 64
PAIRS = 3
PAIR = 128
FF = 1536
DIN = 768
LEN = 1568
FC_ROWS = 3584
QKV_ROWS = 2048
STEP = 112
AXES = ("seq", "clip")
VMEM = 60 * 1024 * 1024

bf16 = jnp.bfloat16
f32 = jnp.float32


def dot(left, right):
    return lax.dot_general(
        left, right, (((1,), (0,)), ((), ())), preferred_element_type=f32
    )


def dot_rt(left, right):
    return lax.dot_general(
        left, right, (((1,), (1,)), ((), ())), preferred_element_type=f32
    )


def dot_lt(left, right):
    return lax.dot_general(
        left, right, (((0,), (0,)), ((), ())), preferred_element_type=f32
    )


def split3(value):
    high = value.astype(bf16)
    rest = value - high.astype(f32)
    middle = rest.astype(bf16)
    low = (rest - middle.astype(f32)).astype(bf16)
    return high, middle, low


def sinusoid_table(length, columns):
    positions = np.arange(length, dtype=np.float64)[:, None]
    column = np.arange(columns)
    angles = positions / np.power(10000.0, (2 * (column // 2)) / columns)[None, :]
    return np.where((column % 2)[None, :] == 0, np.sin(angles), np.cos(angles)).astype(np.float32)


def forward_kernel(
    start_ref,
    x_ref,
    pos_ref,
    table_ref,
    w_proj_ref,
    b_proj_ref,
    mask_ref,
    gain1_ref,
    bias1_ref,
    w_qkv_ref,
    q_bias_ref,
    v_bias_ref,
    w_out_ref,
    b_out_ref,
    gain2_ref,
    bias2_ref,
    w_fc1_ref,
    b_fc1_ref,
    w_fc2_ref,
    b_fc2_ref,
    cot_ref,
    out_ref,
    p_ref,
    q_ref,
    k_ref,
    v_ref,
    normed_ref,
    xhat_ref,
    rstd_ref,
    gs_ref,
    extra_ref,
    gmid_ref,
    flat_ref,
    emb_s,
    att_s,
    linv_s,
    *,
    rows,
):
    clip = pl.program_id(0)
    phase = pl.program_id(1)
    lane = lax.broadcasted_iota(jnp.int32, (1, PAIR), 1)

    @pl.when(jnp.logical_and(clip == 0, phase == 0))
    def _():
        flat_ref[...] = jnp.zeros_like(flat_ref)

    @pl.when(phase == 0)
    def _():
        projected = dot(x_ref[0], w_proj_ref[...]) + b_proj_ref[...][None, :]
        high, middle, low = split3(projected - mask_ref[...][None, :])
        row = lax.broadcasted_iota(jnp.int32, (LEN, 1), 0)
        onehot = (row == pos_ref[0]).astype(f32).astype(bf16)
        emb_s[...] = (
            (table_ref[...].reshape(LEN, D) + mask_ref[...][None, :]) + dot(onehot, low) + dot(onehot, middle)
        ) + dot(onehot, high)

        def norm_rows(step, carry):
            at = pl.ds(pl.multiple_of(step * STEP, STEP), STEP)
            value = emb_s[at, :]
            centered = value - jnp.mean(value, axis=1, keepdims=True)
            rstd = lax.rsqrt(jnp.mean(centered * centered, axis=1, keepdims=True) + 1e-05)
            xhat = centered * rstd
            xhat_ref[0, at, :] = xhat.astype(bf16)
            normed_ref[0, at, :] = (xhat * gain1_ref[...][None, :] + bias1_ref[...][None, :]).astype(bf16)
            rstd_ref[0, at, :] = rstd
            return carry

        lax.fori_loop(0, LEN // STEP, norm_rows, 0)
        normed = normed_ref[0]
        k_ref[0] = dot(normed, w_qkv_ref[:, D : 2 * D]).astype(bf16)
        v_ref[0] = (dot(normed, w_qkv_ref[:, 2 * D :]) + v_bias_ref[...][None, :]).astype(bf16)
        q_ref[0] = (dot(normed[:rows], w_qkv_ref[:, :D]) + q_bias_ref[...][None, :]).astype(bf16)

    @pl.when(jnp.logical_and(phase >= 1, phase <= PAIRS))
    def _():
        at = pl.ds(pl.multiple_of((phase - 1) * PAIR, PAIR), PAIR)
        query = q_ref[0, :, at]
        key = k_ref[0, :, at]
        value = jnp.concatenate([v_ref[0, :, at], jnp.ones((LEN, PAIR), bf16)], axis=1)
        parts = []
        for head in range(2):
            own = (lane < HEAD) if head == 0 else (lane >= HEAD)
            scores = dot_rt(jnp.where(own, query, jnp.zeros_like(query)), key)
            largest = jnp.max(scores, axis=1, keepdims=True)
            weights = jnp.exp2((scores - largest) * (HEAD**-0.5 * np.log2(np.e))).astype(bf16)
            p_ref[0, head] = weights
            parts.append(dot(weights, value))
        sums = jnp.where(lane < HEAD, parts[0][:, PAIR:], parts[1][:, PAIR:])
        inverse = 1.0 / sums
        linv_s[:, at] = inverse
        att_s[:, at] = jnp.where(lane < HEAD, parts[0][:, :PAIR], parts[1][:, :PAIR]) * inverse

    @pl.when(phase == PAIRS + 1)
    def _():
        att = att_s[...]
        attended = att.astype(bf16)
        middle = emb_s[:rows, :] + (dot(attended, w_out_ref[...]) + b_out_ref[...][None, :])
        centered = middle - jnp.mean(middle, axis=1, keepdims=True)
        rstd = lax.rsqrt(jnp.mean(centered * centered, axis=1, keepdims=True) + 1e-05)
        xhat = centered * rstd
        normed2 = (xhat * gain2_ref[...][None, :] + bias2_ref[...][None, :]).astype(bf16)
        cot = cot_ref[0]
        cot_f = cot.astype(f32)
        output = middle + b_fc2_ref[...][None, :]
        grad_normed = jnp.zeros((rows, D), f32)
        width = 256
        for block in range(FF // width):
            at = slice(block * width, (block + 1) * width)
            pre = dot(normed2, w_fc1_ref[:, at]) + b_fc1_ref[at][None, :]
            cdf = 0.5 + 0.5 * lax.erf(pre * np.float32(0.5**0.5))
            hidden = (pre * cdf).astype(bf16)
            output = output + dot(hidden, w_fc2_ref[at, :])
            flat_ref[at, :] += dot_lt(hidden, cot)
            slope = cdf + pre * (jnp.exp2(pre * pre * (-0.5 * np.log2(np.e))) * ((2 * np.pi) ** -0.5))
            grad_pre = dot_rt(cot, w_fc2_ref[at, :]) * slope
            grad_pre_b = grad_pre.astype(bf16)
            col_sum = jnp.sum(grad_pre_b.astype(f32), axis=0, keepdims=True)
            grad_w = dot_lt(normed2, grad_pre_b)
            for piece in range(width // PAIR):
                col = block * width + piece * PAIR
                first = FF + D + (col // D) * D
                lanes = slice(col % D, col % D + PAIR)
                src = slice(piece * PAIR, (piece + 1) * PAIR)
                flat_ref[first : first + D, lanes] += grad_w[:, src]
                vec_row = 2 * FF + D + col // D
                flat_ref[vec_row : vec_row + 1, lanes] += col_sum[:, src]
            grad_normed = grad_normed + dot_rt(grad_pre_b, w_fc1_ref[:, at])
        out_ref[0] = output.astype(bf16)
        base = 2 * FF + D + 4
        flat_ref[base : base + 1, :] += jnp.sum(cot_f, axis=0, keepdims=True)
        flat_ref[base + 1 : base + 2, :] += jnp.sum(grad_normed * xhat, axis=0, keepdims=True)
        flat_ref[base + 2 : base + 3, :] += jnp.sum(grad_normed, axis=0, keepdims=True)
        scaled = grad_normed * gain2_ref[...][None, :]
        grad_middle = cot_f + rstd * (
            scaled
            - jnp.mean(scaled, axis=1, keepdims=True)
            - xhat * jnp.mean(scaled * xhat, axis=1, keepdims=True)
        )
        gmid_ref[0] = grad_middle
        grad_branch = grad_middle.astype(bf16)
        flat_ref[base + 3 : base + 4, :] += jnp.sum(
            grad_branch.astype(f32), axis=0, keepdims=True
        )
        flat_ref[FF : FF + D, :] += dot_lt(attended, grad_branch)
        grad_att = dot_rt(grad_branch, w_out_ref[...]).astype(bf16).astype(f32)
        grad_s = (grad_att * linv_s[...]).astype(bf16)
        gs_ref[0] = grad_s
        product = grad_s.astype(f32) * att
        for pair in range(PAIRS):
            piece = product[:, pair * PAIR : (pair + 1) * PAIR]
            for head in range(2):
                own = (lane < HEAD) if head == 0 else (lane >= HEAD)
                inner = -jnp.sum(jnp.where(own, piece, 0.0), axis=1, keepdims=True)
                high, middle3, low = split3(inner)
                filled = jnp.where(
                    lane == 0,
                    high.astype(f32),
                    jnp.where(
                        lane == 1,
                        middle3.astype(f32),
                        jnp.where(lane == 2, low.astype(f32), 0.0),
                    ),
                )
                first = (2 * pair + head) * PAIR
                extra_ref[0, :, first : first + PAIR] = filled.astype(bf16)


def backward_kernel(
    start_ref,
    q_ref,
    k_ref,
    v_ref,
    gs_ref,
    extra_ref,
    p_ref,
    normed_ref,
    xhat_ref,
    rstd_ref,
    gmid_ref,
    x_ref,
    pos_ref,
    w_qkv_ref,
    gain1_ref,
    flat_ref,
    gproj_ref,
    dq_s,
    dk_s,
    dv_s,
    gn_s,
    own_s,
    high_s,
    low_s,
    *,
    rows,
):
    clip = pl.program_id(0)
    phase = pl.program_id(1)
    lane = lax.broadcasted_iota(jnp.int32, (1, PAIR), 1)

    @pl.when(jnp.logical_and(clip == 0, phase == 0))
    def _():
        flat_ref[...] = jnp.zeros_like(flat_ref)

    @pl.when(phase < PAIRS)
    def _():
        at = pl.ds(pl.multiple_of(phase * PAIR, PAIR), PAIR)
        query = q_ref[0, :, at] * jnp.asarray(HEAD**-0.5, bf16)
        key = k_ref[0, :, at]
        value = jnp.concatenate([v_ref[0, :, at], jnp.ones((LEN, PAIR), bf16)], axis=1)
        grad = gs_ref[0, :, at]
        queries, keys, values = [], [], []
        for head in range(2):
            own = (lane < HEAD) if head == 0 else (lane >= HEAD)
            where = pl.ds(pl.multiple_of(phase * (2 * PAIR) + head * PAIR, PAIR), PAIR)
            left = jnp.concatenate(
                [jnp.where(own, grad, jnp.zeros_like(grad)), extra_ref[0, :, where]], axis=1
            )
            weights = p_ref[0, head]
            grad_scores = (weights.astype(f32) * dot_rt(left, value)).astype(bf16)
            queries.append(dot(grad_scores, key))
            keys.append(dot_lt(grad_scores, query))
            values.append(dot_lt(weights, grad))
        dq_s[:, at] = (
            jnp.where(lane < HEAD, queries[0], queries[1]) * (HEAD**-0.5)
        ).astype(bf16)
        dk_s[:, at] = jnp.where(lane < HEAD, keys[0], keys[1]).astype(bf16)
        dv_s[:, at] = jnp.where(lane < HEAD, values[0], values[1]).astype(bf16)

    @pl.when(phase == PAIRS)
    def _():
        normed = normed_ref[0]
        grad_q = dq_s[...]
        grad_k = dk_s[...]
        grad_v = dv_s[...]
        flat_ref[:D, :] += dot_lt(normed[:rows], grad_q)
        flat_ref[D : 2 * D, :] += dot_lt(normed, grad_k)
        flat_ref[2 * D : 3 * D, :] += dot_lt(normed, grad_v)
        base = 3 * D + DIN
        ones = jnp.ones((8, LEN), bf16)
        flat_ref[base + 4 : base + 5, :] += dot(ones[:, :rows], grad_q)[:1]
        flat_ref[base + 5 : base + 6, :] += dot(ones, grad_v)[:1]
        gn_s[...] = dot_rt(grad_k, w_qkv_ref[:, D : 2 * D]) + dot_rt(
            grad_v, w_qkv_ref[:, 2 * D :]
        )
        gn_s[:rows, :] += dot_rt(grad_q, w_qkv_ref[:, :D])
        own_s[:rows, :] = gmid_ref[0]
        own_s[rows:, :] = jnp.zeros_like(own_s[rows:, :])

        def norm_rows(step, carry, with_own):
            at = pl.ds(pl.multiple_of(step * STEP, STEP), STEP)
            sum_gain, sum_bias, sum_emb = carry
            value = gn_s[at, :]
            xhat = xhat_ref[0, at, :].astype(f32)
            sum_bias = sum_bias + jnp.sum(value, axis=0, keepdims=True)
            sum_gain = sum_gain + jnp.sum(value * xhat, axis=0, keepdims=True)
            scaled = value * gain1_ref[...][None, :]
            grad = rstd_ref[0, at, :] * (
                scaled
                - jnp.mean(scaled, axis=1, keepdims=True)
                - xhat * jnp.mean(scaled * xhat, axis=1, keepdims=True)
            )
            if with_own:
                grad = grad + own_s[at, :]
            sum_emb = sum_emb + jnp.sum(grad, axis=0, keepdims=True)
            high = grad.astype(bf16)
            high_s[at, :] = high
            low_s[at, :] = (grad - high.astype(f32)).astype(bf16)
            return sum_gain, sum_bias, sum_emb

        zero = jnp.zeros((1, D), f32)
        own_steps = own_s.shape[0] // STEP
        carry = lax.fori_loop(
            0, own_steps, functools.partial(norm_rows, with_own=True), (zero, zero, zero)
        )
        sum_gain, sum_bias, sum_emb = lax.fori_loop(
            own_steps, LEN // STEP, functools.partial(norm_rows, with_own=False), carry
        )
        column = lax.broadcasted_iota(jnp.int32, (1, LEN), 1)
        onehot = (pos_ref[0] == column).astype(f32).astype(bf16)
        grad_proj = dot(onehot, high_s[...]) + dot(onehot, low_s[...])
        gproj_ref[0] = grad_proj
        sum_proj = jnp.sum(grad_proj, axis=0, keepdims=True)
        flat_ref[base : base + 1, :] += sum_proj
        flat_ref[base + 1 : base + 2, :] += sum_emb - sum_proj
        flat_ref[base + 2 : base + 3, :] += sum_gain
        flat_ref[base + 3 : base + 4, :] += sum_bias
        flat_ref[3 * D : 3 * D + DIN, :] += dot_lt(x_ref[0], grad_proj.astype(bf16))


def whole(shape):
    return pl.BlockSpec(
        shape, lambda c, h, s: (0,) * len(shape), pipeline_mode=pl.Buffered(1)
    )


def per_clip(*shape):
    return pl.BlockSpec((1,) + shape, lambda c, h, s: (c,) + (0,) * len(shape))


def run_forward(start, x_vis, local_pos, table, params, cotangent, rows):
    clips, visible, _ = x_vis.shape
    (
        w_proj,
        b_proj,
        mask_token,
        ln1_gain,
        ln1_bias,
        w_qkv,
        q_bias,
        v_bias,
        w_out,
        b_out,
        ln2_gain,
        ln2_bias,
        w_fc1,
        b_fc1,
        w_fc2,
        b_fc2,
    ) = params
    arrays = [
        (w_proj, (DIN, D)),
        (b_proj, (D,)),
        (mask_token, (D,)),
        (ln1_gain, (D,)),
        (ln1_bias, (D,)),
        (w_qkv, (D, 3 * D)),
        (q_bias, (D,)),
        (v_bias, (D,)),
        (w_out, (D, D)),
        (b_out, (D,)),
        (ln2_gain, (D,)),
        (ln2_bias, (D,)),
        (w_fc1, (D, FF)),
        (b_fc1, (FF,)),
        (w_fc2, (FF, D)),
        (b_fc2, (D,)),
    ]
    shape = jax.ShapeDtypeStruct
    return pl.pallas_call(
        functools.partial(forward_kernel, rows=rows),
        grid_spec=pltpu.PrefetchScalarGridSpec(
            num_scalar_prefetch=1,
            grid=(clips, PAIRS + 2),
            in_specs=[
                per_clip(visible, DIN),
                per_clip(1, visible),
                pl.BlockSpec(
                    (pl.Element(LEN // 8), pl.Element(8), pl.Element(D)),
                    lambda c, h, s: (s[0], 0, 0),
                ),
            ]
            + [whole(size) for _, size in arrays]
            + [per_clip(rows, D)],
            out_specs=[
                per_clip(rows, D),
                pl.BlockSpec(
                    (1, 2, rows, LEN),
                    lambda c, h, s: (c, jnp.clip(h - 1, 0, PAIRS - 1), 0, 0),
                ),
                per_clip(rows, D),
                per_clip(LEN, D),
                per_clip(LEN, D),
                per_clip(LEN, D),
                per_clip(LEN, D),
                per_clip(LEN, 1),
                per_clip(rows, D),
                per_clip(rows, HEADS * PAIR),
                per_clip(rows, D),
                whole((FC_ROWS, D)),
            ],
            scratch_shapes=[
                pltpu.VMEM((LEN, D), f32),
                pltpu.VMEM((rows, D), f32),
                pltpu.VMEM((rows, D), f32),
            ],
        ),
        out_shape=[
            shape((clips, rows, D), bf16),
            shape((clips, HEADS, rows, LEN), bf16),
            shape((clips, rows, D), bf16),
            shape((clips, LEN, D), bf16),
            shape((clips, LEN, D), bf16),
            shape((clips, LEN, D), bf16),
            shape((clips, LEN, D), bf16),
            shape((clips, LEN, 1), f32),
            shape((clips, rows, D), bf16),
            shape((clips, rows, HEADS * PAIR), bf16),
            shape((clips, rows, D), f32),
            shape((FC_ROWS, D), f32),
        ],
        compiler_params=pltpu.CompilerParams(
            dimension_semantics=("arbitrary", "arbitrary"), vmem_limit_bytes=VMEM
        ),
        name="forward_clip",
    )(
        start,
        x_vis,
        local_pos[:, None, :],
        table,
        *[value for value, _ in arrays],
        cotangent,
    )


def run_backward(start, saved, x_vis, local_pos, w_qkv, ln1_gain, rows):
    clips, visible, _ = x_vis.shape
    query, key, value, grads, extra, weights, normed, xhat, rstd, gmid = saved
    own_rows = -(-rows // STEP) * STEP
    shape = jax.ShapeDtypeStruct
    return pl.pallas_call(
        functools.partial(backward_kernel, rows=rows),
        grid_spec=pltpu.PrefetchScalarGridSpec(
            num_scalar_prefetch=1,
            grid=(clips, PAIRS + 1),
            in_specs=[
                per_clip(rows, D),
                per_clip(LEN, D),
                per_clip(LEN, D),
                per_clip(rows, D),
                per_clip(rows, HEADS * PAIR),
                pl.BlockSpec(
                    (1, 2, rows, LEN),
                    lambda c, h, s: (c, jnp.minimum(h, PAIRS - 1), 0, 0),
                ),
                per_clip(LEN, D),
                per_clip(LEN, D),
                per_clip(LEN, 1),
                per_clip(rows, D),
                per_clip(visible, DIN),
                per_clip(visible, 1),
                whole((D, 3 * D)),
                whole((D,)),
            ],
            out_specs=[whole((QKV_ROWS, D)), per_clip(visible, D)],
            scratch_shapes=[
                pltpu.VMEM((rows, D), bf16),
                pltpu.VMEM((LEN, D), bf16),
                pltpu.VMEM((LEN, D), bf16),
                pltpu.VMEM((LEN, D), f32),
                pltpu.VMEM((own_rows, D), f32),
                pltpu.VMEM((LEN, D), bf16),
                pltpu.VMEM((LEN, D), bf16),
            ],
        ),
        out_shape=[shape((QKV_ROWS, D), f32), shape((clips, visible, D), f32)],
        compiler_params=pltpu.CompilerParams(
            dimension_semantics=("arbitrary", "arbitrary"), vmem_limit_bytes=VMEM
        ),
        name="backward_clip",
    )(
        start,
        query,
        key,
        value,
        grads,
        extra,
        weights,
        normed,
        xhat,
        rstd,
        gmid,
        x_vis,
        local_pos[:, :, None],
        w_qkv,
        ln1_gain,
    )


def exchange_stages(seq_size, clip_size):
    def seq_bit(s, c):
        return (s >> 1) & 1

    def clip_bit(s, c):
        return c & 1

    def core(s, c):
        return s & 1

    stages = [(core, lambda s, c: (s ^ 1, c))]
    stages.append(
        (
            lambda s, c: seq_bit(s, c) * (1 - core(s, c)) + clip_bit(s, c) * core(s, c),
            lambda s, c: (s ^ 2, c) if s & 1 == 0 else (s, c ^ 1),
        )
    )
    stages.append(
        (
            lambda s, c: clip_bit(s, c) * (1 - core(s, c)) + seq_bit(s, c) * core(s, c),
            lambda s, c: (s, c ^ 1) if s & 1 == 0 else (s ^ 2, c),
        )
    )
    for bit in range(1, clip_size.bit_length() - 1):
        stages.append(
            (
                lambda s, c, bit=bit: (c >> bit) & 1,
                lambda s, c, bit=bit: (s, c ^ (1 << bit)),
            )
        )
    result = []
    for bit_of, partner in stages:
        pairs = []
        for s in range(seq_size):
            for c in range(clip_size):
                other = partner(s, c)
                pairs.append((s * clip_size + c, other[0] * clip_size + other[1]))
        result.append((bit_of, pairs))
    return result


def sum_everywhere(flat):
    seq_size = lax.axis_size("seq")
    clip_size = lax.axis_size("clip")
    s = lax.axis_index("seq")
    c = lax.axis_index("clip")
    stages = exchange_stages(seq_size, clip_size)
    data = flat
    for bit_of, pairs in stages:
        half = data.shape[0] // 2
        bit = bit_of(s, c)
        sent = lax.dynamic_slice_in_dim(data, (1 - bit) * half, half, 0).astype(bf16)
        kept = lax.dynamic_slice_in_dim(data, bit * half, half, 0)
        data = kept + lax.ppermute(sent, AXES, pairs).astype(f32)
    data = data.astype(bf16)
    for bit_of, pairs in stages[::-1]:
        bit = bit_of(s, c)
        other = lax.ppermute(data, AXES, pairs)
        data = jnp.where(
            bit == 0, jnp.concatenate([data, other]), jnp.concatenate([other, data])
        )
    return data.astype(f32)


def sum_over_seq(value):
    s = lax.axis_index("seq")
    core_pairs = [(0, 1), (1, 0), (2, 3), (3, 2)]
    chip_pairs = [(0, 2), (2, 0), (1, 3), (3, 1)]
    half = value.shape[0] // 2
    bit = s & 1
    sent = lax.dynamic_slice_in_dim(value, (1 - bit) * half, half, 0).astype(bf16)
    kept = lax.dynamic_slice_in_dim(value, bit * half, half, 0)
    part = (kept + lax.ppermute(sent, "seq", core_pairs).astype(f32)).astype(bf16)
    other = lax.ppermute(part, "seq", chip_pairs)
    part = (part.astype(f32) + other.astype(f32)).astype(bf16)
    other = lax.ppermute(part, "seq", core_pairs)
    return jnp.where(bit == 0, jnp.concatenate([part, other]), jnp.concatenate([other, part]))


def shards(x_vis, vis_pos, *rest):
    params, cotangent = rest[:-1], rest[-1]
    w_proj, ln1_gain, w_qkv = params[0], params[3], params[5]
    rows = LEN // lax.axis_size("seq")
    clips, visible, _ = x_vis.shape
    first = lax.axis_index("seq") * rows
    local_pos = jnp.where(vis_pos >= first, vis_pos - first, vis_pos - first + LEN)
    table = sinusoid_table(LEN, D)
    table = jnp.asarray(np.concatenate([table, table[: LEN - rows]]).reshape(-1, 8, D))
    start = jnp.reshape(first // 8, (1,)).astype(jnp.int32)
    output, weights, query, key, value, normed, xhat, rstd, grads, extra, gmid, flat_fc = (
        run_forward(start, x_vis, local_pos, table, params, cotangent, rows)
    )
    saved = (query, key, value, grads, extra, weights, normed, xhat, rstd, gmid)
    flat_qkv, grad_proj = run_backward(start, saved, x_vis, local_pos, w_qkv, ln1_gain, rows)

    fc = sum_everywhere(flat_fc)
    qkv = sum_everywhere(flat_qkv)
    count = clips * visible
    padded = -(-count // 32) * 32
    stacked = jnp.pad(grad_proj.reshape(count, D), ((0, padded - count), (0, 0)))
    grad_projected = sum_over_seq(stacked)[:count]
    grad_x = lax.dot_general(
        grad_projected, w_proj, (((1,), (1,)), ((), ())), preferred_element_type=f32
    ).reshape(clips, visible, DIN)

    grad_w_qkv = jnp.concatenate([qkv[:D], qkv[D : 2 * D], qkv[2 * D : 3 * D]], axis=1)
    grad_w_proj = qkv[3 * D : 3 * D + DIN]
    base = 3 * D + DIN
    grad_b_proj, grad_mask, grad_ln1_gain, grad_ln1_bias, grad_q_bias, grad_v_bias = [
        qkv[base + number] for number in range(6)
    ]
    grad_w_fc2 = fc[:FF]
    grad_w_out = fc[FF : FF + D]
    grad_w_fc1 = jnp.concatenate(
        [fc[FF + D + number * D : FF + 2 * D + number * D] for number in range(4)], axis=1
    )
    base = 2 * FF + D
    grad_b_fc1 = fc[base : base + 4].reshape(FF)
    grad_b_fc2, grad_ln2_gain, grad_ln2_bias, grad_b_out = [
        fc[base + 4 + number] for number in range(4)
    ]

    def ratio(weight, grad):
        return jnp.sqrt(jnp.mean(weight.astype(f32) ** 2)) / jnp.sqrt(jnp.mean(grad**2) + 1e-06)

    trust = jnp.stack(
        [
            ratio(w_proj, grad_w_proj),
            ratio(params[8], grad_w_out),
            ratio(params[12], grad_w_fc1),
            ratio(params[14], grad_w_fc2),
        ]
    )
    trust_qkv = ratio(w_qkv, grad_w_qkv).reshape(1)
    return (
        output,
        grad_x,
        grad_w_proj,
        grad_b_proj,
        grad_mask,
        grad_ln1_gain,
        grad_ln1_bias,
        grad_w_qkv,
        grad_q_bias,
        grad_v_bias,
        grad_w_out,
        grad_b_out,
        grad_ln2_gain,
        grad_ln2_bias,
        grad_w_fc1,
        grad_b_fc1,
        grad_w_fc2,
        grad_b_fc2,
        trust,
        trust_qkv,
    )


def solution(mesh):
    return jax.shard_map(
        shards,
        mesh=mesh,
        in_specs=(P("clip", None, None), P("clip", None))
        + (P(),) * 16
        + (P("clip", "seq", None),),
        out_specs=(P("clip", "seq", None), P("clip", None, None)) + (P(),) * 18,
        check_vma=False,
    )
```

```python
import functools

import jax
import jax.numpy as jnp
import numpy as np
from jax import lax
from jax.experimental import pallas as pl
from jax.experimental.pallas import tpu as pltpu
from jax.sharding import PartitionSpec as P

D = 384
HEADS = 6
HEAD = 64
PAIRS = 3
PAIR = 128
FF = 1536
DIN = 768
SLOT = 160
LEN = 1568
STEP = 112
BLOCK = 256
BLOCKS = FF // BLOCK
FC_USED = 10392
QKV_USED = 5784
AXES = ("seq", "clip")
VMEM = 60 * 1024 * 1024

bf16 = jnp.bfloat16
f32 = jnp.float32


def dot(left, right):
    return lax.dot_general(
        left, right, (((1,), (0,)), ((), ())), preferred_element_type=f32
    )


def dot_rt(left, right):
    return lax.dot_general(
        left, right, (((1,), (1,)), ((), ())), preferred_element_type=f32
    )


def dot_lt(left, right):
    return lax.dot_general(
        left, right, (((0,), (0,)), ((), ())), preferred_element_type=f32
    )


def split3(value):
    high = value.astype(bf16)
    rest = value - high.astype(f32)
    middle = rest.astype(bf16)
    low = (rest - middle.astype(f32)).astype(bf16)
    return high, middle, low


def sinusoid_table(length, columns):
    positions = np.arange(length, dtype=np.float64)[:, None]
    column = np.arange(columns)
    angles = positions / np.power(10000.0, (2 * (column // 2)) / columns)[None, :]
    return np.where((column % 2)[None, :] == 0, np.sin(angles), np.cos(angles)).astype(np.float32)


def own_lanes(head):
    lane = lax.broadcasted_iota(jnp.int32, (1, PAIR), 1)
    return (lane < HEAD) if head == 0 else (lane >= HEAD)


def column_sums(value):
    return jnp.sum(value, axis=0, keepdims=True)


def square_sum(weight):
    columns = weight.shape[1]
    total = column_sums(weight.astype(f32) ** 2)
    result = total[:, :PAIR]
    for first in range(PAIR, columns, PAIR):
        result = result + total[:, first : first + PAIR]
    return result


def lane_mean(value):
    return jnp.mean(value, axis=1, keepdims=True)


def forward_kernel(
    start_ref,
    x_ref,
    pos_ref,
    table_ref,
    w_proj_ref,
    b_proj_ref,
    mask_ref,
    gain1_ref,
    bias1_ref,
    w_qkv_ref,
    q_bias_ref,
    v_bias_ref,
    w_out_ref,
    b_out_ref,
    gain2_ref,
    bias2_ref,
    w_fc1_ref,
    b_fc1_ref,
    w_fc2_ref,
    b_fc2_ref,
    cot_ref,
    out_ref,
    gs_ref,
    extra_ref,
    gmid_ref,
    kept_ref,
    sent_ref,
    norms_ref,
    p_hbm,
    q_hbm,
    k_hbm,
    v_hbm,
    normed_hbm,
    xhat_hbm,
    rstd_hbm,
    p_s,
    q_s,
    k_s,
    v_s,
    normed_s,
    xhat_s,
    rstd_s,
    emb_s,
    own_s,
    att_s,
    linv_s,
    attended_s,
    middle_s,
    xhat2_s,
    rstd2_s,
    normed2_s,
    gn_s,
    vec_s,
    flat_s,
    sems,
    p_sems,
    *,
    rows,
    clips,
):
    step = pl.program_id(0)
    per = PAIRS + 1
    clip = jnp.minimum(lax.div(step, per), clips - 1)
    phase = step - clip * per
    half = kept_ref.shape[0]

    def saves(number):
        pairs = [
            (q_s, q_hbm),
            (k_s, k_hbm),
            (v_s, v_hbm),
            (normed_s, normed_hbm),
            (xhat_s, xhat_hbm),
            (rstd_s, rstd_hbm),
        ]
        return [
            pltpu.make_async_copy(source, target.at[number], sems.at[index])
            for index, (source, target) in enumerate(pairs)
        ]

    def p_save(number):
        slot = lax.rem(number, 2)
        at = lax.div(number, PAIRS)
        pair = lax.rem(number, PAIRS)
        return pltpu.make_async_copy(
            p_s.at[slot], p_hbm.at[at, pl.ds(2 * pair, 2)], p_sems.at[slot]
        )

    @pl.when(phase == 0)
    def _():
        @pl.when(clip > 0)
        def _():
            for copy in saves(clip - 1):
                copy.wait()

        projected = dot(x_ref[0], w_proj_ref[...]) + b_proj_ref[...][None, :]
        high, middle, low = split3(projected - mask_ref[...][None, :])
        row = lax.broadcasted_iota(jnp.int32, (LEN, 1), 0)
        onehot = (row == pos_ref[0]).astype(f32).astype(bf16)
        emb_s[...] = (
            (table_ref[...].reshape(LEN, D) + mask_ref[...][None, :])
            + dot(onehot, low)
            + dot(onehot, middle)
        ) + dot(onehot, high)

        def norm_rows(number, carry):
            at = pl.ds(pl.multiple_of(number * STEP, STEP), STEP)
            value = emb_s[at, :]
            centered = value - lane_mean(value)
            rstd = lax.rsqrt(lane_mean(centered * centered) + 1e-05)
            xhat = centered * rstd
            xhat_s[at, :] = xhat.astype(bf16)
            normed_s[at, :] = (xhat * gain1_ref[...][None, :] + bias1_ref[...][None, :]).astype(
                bf16
            )
            rstd_s[at, :] = rstd
            return carry

        lax.fori_loop(0, LEN // STEP, norm_rows, 0)
        own_s[pl.ds(pl.multiple_of(clip * rows, 8), rows), :] = emb_s[:rows, :]
        normed = normed_s[...]
        k_s[...] = dot(normed, w_qkv_ref[:, D : 2 * D]).astype(bf16)
        v_s[...] = (dot(normed, w_qkv_ref[:, 2 * D :]) + v_bias_ref[...][None, :]).astype(bf16)
        q_s[...] = (dot(normed[:rows], w_qkv_ref[:, :D]) + q_bias_ref[...][None, :]).astype(bf16)
        for copy in saves(clip):
            copy.start()

        @pl.when(clip == 0)
        def _():
            norms_ref[0:1, :] = square_sum(w_proj_ref[...])
            norms_ref[1:2, :] = square_sum(w_out_ref[...])
            norms_ref[2:4, :] = jnp.zeros((2, PAIR), f32)
            norms_ref[4:5, :] = square_sum(w_qkv_ref[...])

    @pl.when(jnp.logical_and(phase >= 1, phase < per))
    def _():
        number = clip * PAIRS + phase - 1
        slot = lax.rem(number, 2)

        @pl.when(number >= 2)
        def _():
            p_save(number - 2).wait()

        at = pl.ds(pl.multiple_of((phase - 1) * PAIR, PAIR), PAIR)
        query = q_s[:, at]
        key = k_s[:, at]
        value = jnp.concatenate([v_s[:, at], jnp.ones((LEN, PAIR), bf16)], axis=1)
        parts = []
        for head in range(2):
            scores = dot_rt(jnp.where(own_lanes(head), query, jnp.zeros_like(query)), key)
            largest = jnp.max(scores, axis=1, keepdims=True)
            weights = jnp.exp2((scores - largest) * (HEAD**-0.5 * np.log2(np.e))).astype(bf16)
            p_s[slot, head] = weights
            parts.append(dot(weights, value))
        first = own_lanes(0)
        inverse = 1.0 / jnp.where(first, parts[0][:, PAIR:], parts[1][:, PAIR:])
        group = pl.ds(pl.multiple_of(clip * rows, 8), rows)
        linv_s[group, at] = inverse
        att_s[group, at] = jnp.where(first, parts[0][:, :PAIR], parts[1][:, :PAIR]) * inverse
        p_save(number).start()

    @pl.when(step == clips * per)
    def _():
        for copy in saves(clips - 1):
            copy.wait()
        p_save(clips * PAIRS - 2).wait()
        p_save(clips * PAIRS - 1).wait()
        attended = att_s[...].astype(bf16)
        attended_s[...] = attended
        middle = own_s[...] + (dot(attended, w_out_ref[...]) + b_out_ref[...][None, :])
        centered = middle - lane_mean(middle)
        rstd = lax.rsqrt(lane_mean(centered * centered) + 1e-05)
        xhat = centered * rstd
        xhat2_s[...] = xhat
        rstd2_s[...] = rstd
        normed2_s[...] = (xhat * gain2_ref[...][None, :] + bias2_ref[...][None, :]).astype(bf16)
        middle_s[...] = middle + b_fc2_ref[...][None, :]
        gn_s[...] = jnp.zeros_like(gn_s)
        flat_s[FC_USED - 24 :, :] = jnp.zeros_like(flat_s[FC_USED - 24 :, :])

    @pl.when(step >= clips * per)
    def _():
        block = step - clips * per
        normed2 = normed2_s[...]
        cot = cot_ref[...]
        w_fc1 = w_fc1_ref[...]
        w_fc2 = w_fc2_ref[...]
        norms_ref[2:3, :] += square_sum(w_fc1)
        norms_ref[3:4, :] += square_sum(w_fc2)
        pre = dot(normed2, w_fc1) + b_fc1_ref[...][None, :]
        cdf = 0.5 + 0.5 * lax.erf(pre * np.float32(0.5**0.5))
        hidden = (pre * cdf).astype(bf16)
        slope = cdf + pre * (
            jnp.exp2(pre * pre * (-0.5 * np.log2(np.e))) * ((2 * np.pi) ** -0.5)
        )
        grad_pre = dot_rt(cot, w_fc2) * slope
        grad_pre_b = grad_pre.astype(bf16)
        middle_s[...] += dot(hidden, w_fc2)
        gn_s[...] += dot_rt(grad_pre_b, w_fc1)
        grad_w2 = dot_lt(hidden, cot).astype(bf16)
        for column in range(D // PAIR):
            first = FF * PAIRS + column * FF + block * BLOCK
            flat_s[pl.ds(pl.multiple_of(first, 16), BLOCK), :] = grad_w2[
                :, column * PAIR : (column + 1) * PAIR
            ]
        grad_w1 = dot_lt(normed2, grad_pre_b).astype(bf16)
        sums = column_sums(grad_pre_b.astype(f32))
        for piece in range(BLOCK // PAIR):
            lanes = slice(piece * PAIR, (piece + 1) * PAIR)
            number = block * (BLOCK // PAIR) + piece
            flat_s[pl.ds(pl.multiple_of(number * D, 16), D), :] = grad_w1[:, lanes]
            row = 8 * lax.rem(number, PAIRS) + lax.div(number, PAIRS)
            vec_s[pl.ds(row, 1), :] = sums[:, lanes]

    @pl.when(step == clips * per + BLOCKS - 1)
    def _():
        out_ref[...] = middle_s[...].astype(bf16)
        cot_f = cot_ref[...].astype(f32)
        grad_normed = gn_s[...]
        xhat = xhat2_s[...]
        scaled = grad_normed * gain2_ref[...][None, :]
        grad_middle = cot_f + rstd2_s[...] * (
            scaled - lane_mean(scaled) - xhat * lane_mean(scaled * xhat)
        )
        gmid_ref[...] = grad_middle
        grad_branch = grad_middle.astype(bf16)
        vectors = [
            column_sums(cot_f),
            column_sums(grad_normed * xhat),
            column_sums(grad_normed),
            column_sums(grad_branch.astype(f32)),
        ]
        grad_out = dot_lt(attended_s[...], grad_branch).astype(bf16)
        for column in range(D // PAIR):
            lanes = slice(column * PAIR, (column + 1) * PAIR)
            first = 2 * FF * PAIRS + column * D
            flat_s[first : first + D, :] = grad_out[:, lanes]
            for number, vector in enumerate(vectors):
                row = 8 * column + 4 + number
                vec_s[row : row + 1, :] = vector[:, lanes]
        flat_s[FC_USED - 24 : FC_USED, :] = vec_s[...].astype(bf16)
        bit = start_ref[1]
        kept_ref[...] = flat_s[pl.ds(pl.multiple_of(bit * half, 16), half), :]
        sent_ref[...] = flat_s[pl.ds(pl.multiple_of((1 - bit) * half, 16), half), :]
        grad_att = dot_rt(grad_branch, w_out_ref[...]).astype(bf16).astype(f32)
        grad_s = (grad_att * linv_s[...]).astype(bf16)
        gs_ref[...] = grad_s
        product = grad_s.astype(f32) * att_s[...]
        lane = lax.broadcasted_iota(jnp.int32, (1, PAIR), 1)
        packed = jnp.zeros((clips * rows, PAIR), f32)
        for pair in range(PAIRS):
            piece = product[:, pair * PAIR : (pair + 1) * PAIR]
            for head in range(2):
                inner = -jnp.sum(
                    jnp.where(own_lanes(head), piece, 0.0), axis=1, keepdims=True
                )
                for index, term in enumerate(split3(inner)):
                    at = 3 * (2 * pair + head) + index
                    packed = jnp.where(lane == at, term.astype(f32), packed)
        extra_ref[...] = packed.astype(bf16)


def backward_kernel(
    start_ref,
    q_ref,
    k_ref,
    v_ref,
    gs_ref,
    extra_ref,
    p_ref,
    x_ref,
    pos_ref,
    w_qkv_ref,
    gain1_ref,
    normed_hbm,
    xhat_hbm,
    rstd_hbm,
    gmid_hbm,
    *rest,
    rows,
    base,
    count,
    last,
):
    if last:
        acc_hbm, kept_ref, sent_ref, proj_kept_ref, proj_sent_ref = rest[:5]
        acc_s, total_sem = rest[5:7]
        scratch = rest[7:]
    else:
        acc_s, proj_kept_ref, proj_sent_ref = rest[:3]
        scratch = rest[3:]
    (normed_s, xhat_s, rstd_s, own_s, dq_s, dkv_s, gn_s, high_s, low_s, proj_s, sems) = scratch
    per = PAIRS + 1
    step = pl.program_id(0)
    clip = lax.div(step, per)
    phase = step - clip * per
    lane = lax.broadcasted_iota(jnp.int32, (1, PAIR), 1)

    def loads():
        at = base + clip
        pairs = [
            (normed_hbm.at[at], normed_s),
            (xhat_hbm.at[at], xhat_s),
            (rstd_hbm.at[at], rstd_s),
            (gmid_hbm.at[pl.ds(pl.multiple_of(at * rows, 8), rows)], own_s.at[pl.ds(0, rows)]),
        ]
        return [
            pltpu.make_async_copy(source, target, sems.at[index])
            for index, (source, target) in enumerate(pairs)
        ]

    @pl.when(phase == 0)
    def _():
        for copy in loads():
            copy.start()

    @pl.when(step == 0)
    def _():
        own_s[rows:, :] = jnp.zeros_like(own_s[rows:, :])
        if last:
            pltpu.make_async_copy(acc_hbm, acc_s, total_sem).start()
        else:
            acc_s[...] = jnp.zeros_like(acc_s)

    @pl.when(phase < PAIRS)
    def _():
        at = pl.ds(pl.multiple_of(phase * PAIR, PAIR), PAIR)
        query = q_ref[0, :, at] * jnp.asarray(HEAD**-0.5, bf16)
        key = k_ref[0, :, at]
        value = jnp.concatenate([v_ref[0, :, at], jnp.ones((LEN, PAIR), bf16)], axis=1)
        grad = gs_ref[:, at]
        extra = extra_ref[...]
        queries, keys, values = [], [], []
        for head in range(2):
            first = 3 * (2 * phase + head)
            inner = jnp.logical_and(lane >= first, lane < first + 3)
            left = jnp.concatenate(
                [
                    jnp.where(own_lanes(head), grad, jnp.zeros_like(grad)),
                    jnp.where(inner, extra, jnp.zeros_like(extra)),
                ],
                axis=1,
            )
            weights = p_ref[0, head]
            grad_scores = (weights.astype(f32) * dot_rt(left, value)).astype(bf16)
            queries.append(dot(grad_scores, key))
            keys.append(dot_lt(grad_scores, query))
            values.append(dot_lt(weights, grad))
        side = own_lanes(0)
        dq_s[:, at] = (jnp.where(side, queries[0], queries[1]) * (HEAD**-0.5)).astype(bf16)
        dkv_s[:, at] = jnp.where(side, keys[0], keys[1]).astype(bf16)
        at = pl.ds(pl.multiple_of(phase * PAIR + D, PAIR), PAIR)
        dkv_s[:, at] = jnp.where(side, values[0], values[1]).astype(bf16)

    @pl.when(phase == PAIRS)
    def _():
        for copy in loads():
            copy.wait()
        if last:
            @pl.when(step == PAIRS)
            def _():
                pltpu.make_async_copy(acc_hbm, acc_s, total_sem).wait()

        normed = normed_s[...]
        grad_q = dq_s[...]
        grad_kv = dkv_s[...]
        gn_s[...] = dot_rt(grad_kv, w_qkv_ref[:, D:])
        gn_s[:rows, :] += dot_rt(grad_q, w_qkv_ref[:, :D])
        part_q = dot_lt(normed[:rows], grad_q)
        part_kv = dot_lt(normed, grad_kv)
        for index in range(PAIRS):
            acc_s[index * D : (index + 1) * D, :] += part_q[:, index * PAIR : (index + 1) * PAIR]
        for index in range(2 * PAIRS):
            first = (PAIRS + index) * D
            acc_s[first : first + D, :] += part_kv[:, index * PAIR : (index + 1) * PAIR]
        ones = jnp.ones((8, LEN), bf16)
        sum_q = dot(ones[:, :rows], grad_q)[:1]
        sum_v = dot(ones, grad_kv[:, D:])[:1]

        def norm_rows(number, carry, with_own):
            at = pl.ds(pl.multiple_of(number * STEP, STEP), STEP)
            sum_gain, sum_bias, sum_emb = carry
            value = gn_s[at, :]
            xhat = xhat_s[at, :].astype(f32)
            sum_bias = sum_bias + column_sums(value)
            sum_gain = sum_gain + column_sums(value * xhat)
            scaled = value * gain1_ref[...][None, :]
            grad = rstd_s[at, :] * (
                scaled - lane_mean(scaled) - xhat * lane_mean(scaled * xhat)
            )
            if with_own:
                grad = grad + own_s[at, :]
            sum_emb = sum_emb + column_sums(grad)
            high = grad.astype(bf16)
            high_s[at, :] = high
            low_s[at, :] = (grad - high.astype(f32)).astype(bf16)
            return sum_gain, sum_bias, sum_emb

        zero = jnp.zeros((1, D), f32)
        own_steps = own_s.shape[0] // STEP
        carry = lax.fori_loop(
            0, own_steps, functools.partial(norm_rows, with_own=True), (zero, zero, zero)
        )
        sum_gain, sum_bias, sum_emb = lax.fori_loop(
            own_steps, LEN // STEP, functools.partial(norm_rows, with_own=False), carry
        )
        column = lax.broadcasted_iota(jnp.int32, (1, LEN), 1)
        onehot = (pos_ref[0] == column).astype(f32).astype(bf16)
        grad_proj = dot(onehot, high_s[...]) + dot(onehot, low_s[...])
        proj_s[...] = grad_proj
        bit = start_ref[1]
        part = SLOT // 2
        proj_kept_ref[0] = proj_s[pl.ds(pl.multiple_of(bit * part, 8), part), :]
        proj_sent_ref[0] = proj_s[
            pl.ds(pl.multiple_of((1 - bit) * part, 8), part), :
        ].astype(bf16)
        sum_proj = column_sums(grad_proj)
        vectors = [sum_proj, sum_emb - sum_proj, sum_gain, sum_bias, sum_q, sum_v]
        weight = dot_lt(x_ref[0], grad_proj[: x_ref.shape[1]].astype(bf16))
        for index in range(D // PAIR):
            lanes = slice(index * PAIR, (index + 1) * PAIR)
            first = 3 * PAIRS * D + index * DIN
            acc_s[first : first + DIN, :] += weight[:, lanes]
            first = 3 * PAIRS * D + PAIRS * DIN + 8 * index
            for number, vector in enumerate(vectors):
                acc_s[first + number : first + number + 1, :] += vector[:, lanes]

    if last:

        @pl.when(step == count * per - 1)
        def _():
            bit = start_ref[1]
            half = kept_ref.shape[0]
            kept_ref[...] = acc_s[pl.ds(pl.multiple_of(bit * half, 8), half), :]
            sent_ref[...] = acc_s[pl.ds(pl.multiple_of((1 - bit) * half, 8), half), :].astype(
                bf16
            )


def place(target, lanes, source, parts, total):
    for side, where, at, size in parts:
        value = source(side, where, size).astype(f32)
        target[at : at + size, lanes] = value
        if total is not None:
            square = jnp.sum((value * value).reshape(size // 8, 8, PAIR), axis=0)
            total = square if total is False else total + square
    return total


def split_rows(first, count, half):
    result = []
    done = 0
    while done < count:
        side, inside = divmod(first + done, half)
        length = min(count - done, half - inside)
        result.append((side, inside, done, length))
        done += length
    return result


def lanes_of(index):
    return slice(index * PAIR, (index + 1) * PAIR)


def whole_mean(total, size):
    value = jnp.sum(jnp.sum(total, axis=1, keepdims=True), axis=0, keepdims=True)
    return value / size


def assemble_fc_kernel(
    start_ref,
    mine_ref,
    other_ref,
    w_out_ref,
    w_fc1_ref,
    w_fc2_ref,
    b_out_ref,
    gain_ref,
    bias_ref,
    b_fc1_ref,
    b_fc2_ref,
    mean_ref,
):
    half = mine_ref.shape[0]

    def body(halves):
        def source(side, where, size):
            return halves[side][where : where + size, :]

        total = False
        for index in range(PAIRS):
            parts = split_rows(2 * FF * PAIRS + index * D, D, half)
            total = place(w_out_ref, lanes_of(index), source, parts, total)
        mean_out = whole_mean(total, D * D)
        total = False
        for index in range(FF // PAIR):
            parts = split_rows(index * D, D, half)
            total = place(w_fc1_ref, lanes_of(index), source, parts, total)
        mean_fc1 = whole_mean(total, D * FF)
        total = False
        for index in range(PAIRS):
            parts = split_rows(FF * PAIRS + index * FF, FF, half)
            total = place(w_fc2_ref, lanes_of(index), source, parts, total)
        mean_fc2 = whole_mean(total, FF * D)
        first = 2 * FF * PAIRS + PAIRS * D - half
        vectors = source(1, first, 24).astype(f32)
        for index in range(PAIRS):
            lanes = lanes_of(index)
            for number in range(4):
                b_fc1_ref[number * D + index * PAIR : number * D + (index + 1) * PAIR] = vectors[
                    8 * index + number
                ]
            for number, target in enumerate([b_fc2_ref, gain_ref, bias_ref, b_out_ref]):
                target[lanes] = vectors[8 * index + 4 + number]
        row = lax.broadcasted_iota(jnp.int32, (8, PAIR), 0)
        mean_ref[...] = jnp.where(
            row == 1, mean_out, jnp.where(row == 2, mean_fc1, mean_fc2)
        )

    bit = start_ref[1]

    @pl.when(bit == 0)
    def _():
        body((mine_ref, other_ref))

    @pl.when(bit == 1)
    def _():
        body((other_ref, mine_ref))


def assemble_qkv_kernel(
    start_ref,
    mine_ref,
    other_ref,
    norms_ref,
    mean_ref,
    w_proj_ref,
    w_qkv_ref,
    b_proj_ref,
    mask_ref,
    gain_ref,
    bias_ref,
    q_bias_ref,
    v_bias_ref,
    trust_ref,
    trust_qkv_ref,
):
    half = mine_ref.shape[0]

    def body(halves):
        def source(side, where, size):
            return halves[side][where : where + size, :]

        total = False
        for index in range(PAIRS):
            parts = split_rows(3 * PAIRS * D + index * DIN, DIN, half)
            total = place(w_proj_ref, lanes_of(index), source, parts, total)
        mean_proj = whole_mean(total, DIN * D)
        total = False
        for index in range(3 * PAIRS):
            parts = split_rows(index * D, D, half)
            total = place(w_qkv_ref, lanes_of(index), source, parts, total)
        mean_qkv = whole_mean(total, D * 3 * D)
        vectors = source(1, 3 * PAIRS * D + PAIRS * DIN - half, 24).astype(f32)
        targets = [b_proj_ref, mask_ref, gain_ref, bias_ref, q_bias_ref, v_bias_ref]
        for index in range(PAIRS):
            for number, target in enumerate(targets):
                target[lanes_of(index)] = vectors[8 * index + number]
        lane = lax.broadcasted_iota(jnp.int32, (1, PAIR), 1)
        means = [mean_proj, mean_ref[1:2], mean_ref[2:3], mean_ref[3:4], mean_qkv]
        sums = jnp.sum(norms_ref[...], axis=1, keepdims=True)
        sizes = [DIN * D, D * D, D * FF, FF * D, D * 3 * D]
        grads = jnp.ones((1, PAIR), f32)
        weights = jnp.ones((1, PAIR), f32)
        for index, (mean, size) in enumerate(zip(means, sizes)):
            grads = jnp.where(lane == index, mean, grads)
            weights = jnp.where(lane == index, sums[index : index + 1] / size, weights)
        ratios = jnp.sqrt(weights) / jnp.sqrt(grads + 1e-06)
        trust_ref[...] = ratios[0, :4]
        trust_qkv_ref[...] = ratios[0, 4:5]

    bit = start_ref[1]

    @pl.when(bit == 0)
    def _():
        body((mine_ref, other_ref))

    @pl.when(bit == 1)
    def _():
        body((other_ref, mine_ref))


def whole(shape):
    return pl.BlockSpec(shape, lambda i, s: (0,) * len(shape), pipeline_mode=pl.Buffered(1))


def shape_of(shape, dtype):
    return jax.ShapeDtypeStruct(shape, dtype)


def kernel_call(kernel, grid, in_specs, out_specs, out_shape, scratch, name, cost, args):
    return pl.pallas_call(
        kernel,
        grid_spec=pltpu.PrefetchScalarGridSpec(
            num_scalar_prefetch=1,
            grid=grid,
            in_specs=in_specs,
            out_specs=out_specs,
            scratch_shapes=scratch,
        ),
        out_shape=out_shape,
        compiler_params=pltpu.CompilerParams(
            dimension_semantics=("arbitrary",), vmem_limit_bytes=VMEM
        ),
        cost_estimate=pl.CostEstimate(
            flops=cost[0], bytes_accessed=cost[1], transcendentals=cost[2]
        ),
        name=name,
    )(*args)


def run_forward(start, x_vis, local_pos, table, params, cotangent, rows, half):
    clips, visible, _ = x_vis.shape
    (
        w_proj,
        b_proj,
        mask_token,
        ln1_gain,
        ln1_bias,
        w_qkv,
        q_bias,
        v_bias,
        w_out,
        b_out,
        ln2_gain,
        ln2_bias,
        w_fc1,
        b_fc1,
        w_fc2,
        b_fc2,
    ) = params
    per = PAIRS + 1
    steps = clips * per

    def clip_at(i):
        return jnp.minimum(lax.div(i, per), clips - 1)

    def block_at(i):
        return jnp.maximum(i - steps, 0)

    tokens = clips * rows
    any_space = pl.BlockSpec(memory_space=pl.ANY)
    vector = whole((D,))
    in_specs = [
        pl.BlockSpec((1, visible, DIN), lambda i, s: (clip_at(i), 0, 0)),
        pl.BlockSpec((1, 1, visible), lambda i, s: (clip_at(i), 0, 0)),
        pl.BlockSpec(
            (pl.Element(LEN // 8), pl.Element(8), pl.Element(D)), lambda i, s: (s[0], 0, 0)
        ),
        whole((DIN, D)),
        vector,
        vector,
        vector,
        vector,
        whole((D, 3 * D)),
        vector,
        vector,
        whole((D, D)),
        vector,
        vector,
        vector,
        pl.BlockSpec((D, BLOCK), lambda i, s: (0, block_at(i))),
        pl.BlockSpec((BLOCK,), lambda i, s: (block_at(i),)),
        pl.BlockSpec((BLOCK, D), lambda i, s: (block_at(i), 0)),
        vector,
        whole((tokens, D)),
    ]
    out_specs = [
        whole((tokens, D)),
        whole((tokens, D)),
        whole((tokens, PAIR)),
        whole((tokens, D)),
        whole((half, PAIR)),
        whole((half, PAIR)),
        whole((8, PAIR)),
    ] + [any_space] * 7
    out_shape = [
        shape_of((tokens, D), bf16),
        shape_of((tokens, D), bf16),
        shape_of((tokens, PAIR), bf16),
        shape_of((tokens, D), f32),
        shape_of((half, PAIR), bf16),
        shape_of((half, PAIR), bf16),
        shape_of((8, PAIR), f32),
        shape_of((clips, HEADS, rows, LEN), bf16),
        shape_of((clips, rows, D), bf16),
        shape_of((clips, LEN, D), bf16),
        shape_of((clips, LEN, D), bf16),
        shape_of((clips, LEN, D), bf16),
        shape_of((clips, LEN, D), bf16),
        shape_of((clips, LEN, 1), f32),
    ]
    scratch = [
        pltpu.VMEM((2, 2, rows, LEN), bf16),
        pltpu.VMEM((rows, D), bf16),
        pltpu.VMEM((LEN, D), bf16),
        pltpu.VMEM((LEN, D), bf16),
        pltpu.VMEM((LEN, D), bf16),
        pltpu.VMEM((LEN, D), bf16),
        pltpu.VMEM((LEN, 1), f32),
        pltpu.VMEM((LEN, D), f32),
        pltpu.VMEM((tokens, D), f32),
        pltpu.VMEM((tokens, D), f32),
        pltpu.VMEM((tokens, D), f32),
        pltpu.VMEM((tokens, D), bf16),
        pltpu.VMEM((tokens, D), f32),
        pltpu.VMEM((tokens, D), f32),
        pltpu.VMEM((tokens, 1), f32),
        pltpu.VMEM((tokens, D), bf16),
        pltpu.VMEM((tokens, D), f32),
        pltpu.VMEM((24, PAIR), f32),
        pltpu.VMEM((2 * half, PAIR), bf16),
        pltpu.SemaphoreType.DMA((6,)),
        pltpu.SemaphoreType.DMA((2,)),
    ]
    return kernel_call(
        functools.partial(forward_kernel, rows=rows, clips=clips),
        (steps + BLOCKS,),
        in_specs,
        out_specs,
        out_shape,
        scratch,
        "forward",
        (40_000_000_000, 60_000_000, 13_000_000),
        (
            start,
            x_vis,
            local_pos[:, None, :],
            table,
            w_proj,
            b_proj,
            mask_token,
            ln1_gain,
            ln1_bias,
            w_qkv,
            q_bias,
            v_bias,
            w_out,
            b_out,
            ln2_gain,
            ln2_bias,
            w_fc1,
            b_fc1,
            w_fc2,
            b_fc2,
            cotangent.reshape(tokens, D),
        ),
    )


def run_backward(start, saved, x_vis, padded_pos, w_qkv, ln1_gain, rows, half, base, count, acc):
    query, key, value, grads, extra, weights, normed, xhat, rstd, gmid = saved
    _, visible, _ = x_vis.shape
    per = PAIRS + 1
    last = acc is not None
    own_rows = -(-rows // STEP) * STEP
    any_space = pl.BlockSpec(memory_space=pl.ANY)

    def at(i):
        return base + lax.div(i, per)

    def block(*shape):
        return pl.BlockSpec((1,) + shape, lambda i, s: (at(i),) + (0,) * len(shape))

    proj_spec = pl.BlockSpec((1, SLOT // 2, D), lambda i, s: (lax.div(i, per), 0, 0))
    proj_shapes = [
        shape_of((count, SLOT // 2, D), f32),
        shape_of((count, SLOT // 2, D), bf16),
    ]
    in_specs = [
        block(rows, D),
        block(LEN, D),
        block(LEN, D),
        pl.BlockSpec((rows, D), lambda i, s: (at(i), 0)),
        pl.BlockSpec((rows, PAIR), lambda i, s: (at(i), 0)),
        pl.BlockSpec(
            (1, 2, rows, LEN),
            lambda i, s: (at(i), jnp.minimum(lax.rem(i, per), PAIRS - 1), 0, 0),
        ),
        block(visible, DIN),
        block(SLOT, 1),
        whole((D, 3 * D)),
        whole((D,)),
    ] + [any_space] * 4
    args = [
        start,
        query,
        key,
        value,
        grads,
        extra,
        weights,
        x_vis,
        padded_pos[:, :, None],
        w_qkv,
        ln1_gain,
        normed,
        xhat,
        rstd,
        gmid,
    ]
    scratch = [
        pltpu.VMEM((LEN, D), bf16),
        pltpu.VMEM((LEN, D), bf16),
        pltpu.VMEM((LEN, 1), f32),
        pltpu.VMEM((own_rows, D), f32),
        pltpu.VMEM((rows, D), bf16),
        pltpu.VMEM((LEN, 2 * D), bf16),
        pltpu.VMEM((LEN, D), f32),
        pltpu.VMEM((LEN, D), bf16),
        pltpu.VMEM((LEN, D), bf16),
        pltpu.VMEM((SLOT, D), f32),
        pltpu.SemaphoreType.DMA((4,)),
    ]
    if last:
        in_specs.append(any_space)
        args.append(acc)
        out_specs = [whole((half, PAIR)), whole((half, PAIR)), proj_spec, proj_spec]
        out_shape = [shape_of((half, PAIR), f32), shape_of((half, PAIR), bf16)] + proj_shapes
        scratch = [pltpu.VMEM((2 * half, PAIR), f32), pltpu.SemaphoreType.DMA] + scratch
    else:
        out_specs = [whole((2 * half, PAIR)), proj_spec, proj_spec]
        out_shape = [shape_of((2 * half, PAIR), f32)] + proj_shapes
    return kernel_call(
        functools.partial(backward_kernel, rows=rows, base=base, count=count, last=last),
        (count * per,),
        in_specs,
        out_specs,
        out_shape,
        scratch,
        "backward",
        (16_000_000_000 * count, 20_000_000 * count, 0),
        tuple(args),
    )


def run_assemble_fc(start, mine, other):
    half = mine.shape[0]
    shapes = [(D, D), (D, FF), (FF, D), (D,), (D,), (D,), (FF,), (D,), (8, PAIR)]
    return kernel_call(
        assemble_fc_kernel,
        (1,),
        [whole((half, PAIR)), whole((half, PAIR))],
        [whole(size) for size in shapes],
        [shape_of(size, f32) for size in shapes],
        [],
        "assemble_fc",
        (10_000_000, 8_000_000, 0),
        (start, mine, other),
    )


def run_assemble_qkv(start, mine, other, norms, means):
    half = mine.shape[0]
    shapes = [(DIN, D), (D, 3 * D), (D,), (D,), (D,), (D,), (D,), (D,), (4,), (1,)]
    return kernel_call(
        assemble_qkv_kernel,
        (1,),
        [whole((half, PAIR)), whole((half, PAIR)), whole((8, PAIR)), whole((8, PAIR))],
        [whole(size) for size in shapes],
        [shape_of(size, f32) for size in shapes],
        [],
        "assemble_qkv",
        (10_000_000, 5_000_000, 0),
        (start, mine, other, norms, means),
    )


def add_received(kept, received):
    return kept.astype(f32) + received.astype(f32)


def shards(x_vis, vis_pos, *rest):
    params, cotangent = rest[:-1], rest[-1]
    w_proj, ln1_gain, w_qkv = params[0], params[3], params[5]
    seq_size = lax.axis_size("seq")
    clip_size = lax.axis_size("clip")
    groups = seq_size * clip_size // 2
    rows = LEN // seq_size
    clips, visible, _ = x_vis.shape
    members = [
        [s * clip_size + c for s in range(core, seq_size, 2) for c in range(clip_size)]
        for core in range(2)
    ]

    def chunk_rows(used):
        return -(-used // (32 * groups)) * 16

    core_pairs = [(s, s ^ 1) for s in range(seq_size)]
    chip_pairs = [(s, s ^ 2) for s in range(seq_size)]

    def across_core(value):
        return lax.ppermute(value, "seq", core_pairs)

    def swap(value):
        chunks = value.reshape(groups, -1, PAIR)
        return lax.all_to_all(chunks, AXES, 0, 0, axis_index_groups=members)

    def spread(chunks):
        total = jnp.sum(chunks.astype(f32), axis=0).astype(bf16)
        return jnp.broadcast_to(total[None], chunks.shape)

    fc_chunk = chunk_rows(FC_USED)
    qkv_chunk = chunk_rows(QKV_USED)
    qkv_half = qkv_chunk * groups
    seq_index = lax.axis_index("seq")
    bit = seq_index & 1
    first = seq_index * rows
    local_pos = jnp.where(vis_pos >= first, vis_pos - first, vis_pos - first + LEN)
    padded_pos = jnp.pad(local_pos, ((0, 0), (0, SLOT - visible)), constant_values=-1)
    table = sinusoid_table(LEN, D)
    table = jnp.asarray(np.concatenate([table, table[: LEN - rows]]).reshape(-1, 8, D))
    start = jnp.stack([first // 8, bit]).astype(jnp.int32)

    (
        output,
        grads,
        extra,
        gmid,
        kept,
        sent,
        norms,
        weights,
        query,
        key,
        value,
        normed,
        xhat,
        rstd,
    ) = run_forward(start, x_vis, local_pos, table, params, cotangent, rows, fc_chunk * groups)
    fc = add_received(kept, across_core(sent)).astype(bf16)
    fc, query = lax.optimization_barrier((fc, query))
    fc = swap(fc)
    saved = (query, key, value, grads, extra, weights, normed, xhat, rstd, gmid)
    acc, proj_kept0, proj_sent0 = run_backward(
        start, saved, x_vis, padded_pos, w_qkv, ln1_gain, rows, qkv_half, 0, clips - 1, None
    )
    fc, acc = lax.optimization_barrier((spread(fc), acc))
    fc = swap(fc).reshape(groups * fc_chunk, PAIR)
    kept, sent, proj_kept1, proj_sent1 = run_backward(
        start, saved, x_vis, padded_pos, w_qkv, ln1_gain, rows, qkv_half, clips - 1, 1, acc
    )
    qkv = add_received(kept, across_core(sent)).astype(bf16)
    fc, qkv = lax.optimization_barrier((fc, qkv))
    qkv = swap(qkv)
    w_out_g, w_fc1_g, w_fc2_g, b_out_g, gain2_g, bias2_g, b_fc1_g, b_fc2_g, means = (
        run_assemble_fc(start, fc, across_core(fc))
    )
    proj_kept = jnp.concatenate([proj_kept0, proj_kept1])
    proj_sent = jnp.concatenate([proj_sent0, proj_sent1])
    part = add_received(proj_kept, across_core(proj_sent)).astype(bf16)
    part = add_received(part, lax.ppermute(part, "seq", chip_pairs)).astype(bf16)
    qkv, means, part = lax.optimization_barrier((spread(qkv), means, part))
    qkv = swap(qkv).reshape(groups * qkv_chunk, PAIR)
    other = across_core(part)
    grad_projected = jnp.where(
        bit == 0,
        jnp.concatenate([part, other], axis=1),
        jnp.concatenate([other, part], axis=1),
    )[:, :visible]
    grad_x = lax.dot_general(
        grad_projected, w_proj, (((2,), (1,)), ((), ())), preferred_element_type=f32
    )
    (
        w_proj_g,
        w_qkv_g,
        b_proj_g,
        mask_g,
        gain1_g,
        bias1_g,
        q_bias_g,
        v_bias_g,
        trust,
        trust_qkv,
    ) = run_assemble_qkv(start, qkv, across_core(qkv), norms, means)
    return (
        output.reshape(clips, rows, D),
        grad_x,
        w_proj_g,
        b_proj_g,
        mask_g,
        gain1_g,
        bias1_g,
        w_qkv_g,
        q_bias_g,
        v_bias_g,
        w_out_g,
        b_out_g,
        gain2_g,
        bias2_g,
        w_fc1_g,
        b_fc1_g,
        w_fc2_g,
        b_fc2_g,
        trust,
        trust_qkv,
    )


def solution(mesh):
    return jax.shard_map(
        shards,
        mesh=mesh,
        in_specs=(P("clip", None, None), P("clip", None))
        + (P(),) * 16
        + (P("clip", "seq", None),),
        out_specs=(P("clip", "seq", None), P("clip", None, None)) + (P(),) * 18,
        check_vma=False,
    )
```

```python
import functools

import jax
import jax.numpy as jnp
import numpy as np
from jax import lax
from jax.experimental import pallas as pl
from jax.experimental.pallas import tpu as pltpu
from jax.sharding import PartitionSpec as P

D = 384
HEADS = 6
HEAD = 64
PAIRS = 3
PAIR = 128
FF = 1536
DIN = 768
SLOT = 160
LEN = 1568
STEP = 112
BLOCK = 256
BLOCKS = FF // BLOCK
SLOTS = 4
UNROLL_F = True
UNROLL_M = True
UNROLL_B = False
FC_USED = 10392
QKV_USED = 5784
AXES = ("seq", "clip")
VMEM = 60 * 1024 * 1024

bf16 = jnp.bfloat16
f32 = jnp.float32


def dot(left, right):
    return lax.dot_general(
        left, right, (((1,), (0,)), ((), ())), preferred_element_type=f32
    )


def dot_rt(left, right):
    return lax.dot_general(
        left, right, (((1,), (1,)), ((), ())), preferred_element_type=f32
    )


def dot_lt(left, right):
    return lax.dot_general(
        left, right, (((0,), (0,)), ((), ())), preferred_element_type=f32
    )


def split3(value):
    high = value.astype(bf16)
    rest = value - high.astype(f32)
    middle = rest.astype(bf16)
    low = (rest - middle.astype(f32)).astype(bf16)
    return high, middle, low


def sinusoid_table(length, columns):
    positions = np.arange(length, dtype=np.float64)[:, None]
    column = np.arange(columns)
    angles = positions / np.power(10000.0, (2 * (column // 2)) / columns)[None, :]
    return np.where((column % 2)[None, :] == 0, np.sin(angles), np.cos(angles)).astype(np.float32)


def own_lanes(head):
    lane = lax.broadcasted_iota(jnp.int32, (1, PAIR), 1)
    return (lane < HEAD) if head == 0 else (lane >= HEAD)


def column_sums(value):
    return jnp.sum(value, axis=0, keepdims=True)


def square_sum(weight):
    columns = weight.shape[1]
    total = column_sums(weight.astype(f32) ** 2)
    result = total[:, :PAIR]
    for first in range(PAIR, columns, PAIR):
        result = result + total[:, first : first + PAIR]
    return result


def lane_mean(value):
    return jnp.mean(value, axis=1, keepdims=True)


def forward_kernel(
    start_ref,
    x_ref,
    pos_ref,
    table_ref,
    w_proj_ref,
    b_proj_ref,
    mask_ref,
    gain1_ref,
    bias1_ref,
    w_qkv_ref,
    q_bias_ref,
    v_bias_ref,
    b_out_ref,
    gain2_ref,
    bias2_ref,
    b_fc1_ref,
    b_fc2_ref,
    w_out_hbm,
    w_fc1_hbm,
    w_fc2_hbm,
    cot_hbm,
    gs_ref,
    extra_ref,
    norms_ref,
    out_hbm,
    gmid_hbm,
    kept_hbm,
    sent_hbm,
    p_hbm,
    q_hbm,
    k_hbm,
    v_hbm,
    normed_hbm,
    xhat_hbm,
    rstd_hbm,
    p_s,
    q_s,
    k_s,
    v_s,
    normed_s,
    xhat_s,
    rstd_s,
    emb_s,
    middle_s,
    att_s,
    linv_s,
    attended_s,
    xhat2_s,
    rstd2_s,
    normed2_s,
    gn_s,
    vec_s,
    flat_s,
    out_s,
    w_out_s,
    w_fc1_s,
    w_fc2_s,
    cot_s,
    b_fc1_s,
    save_sems,
    p_sems,
    load_sems,
    end_sems,
    *,
    rows,
    clips,
):
    step = pl.program_id(0)
    half = kept_hbm.shape[0]

    def loads():
        pairs = [
            (w_out_hbm, w_out_s),
            (w_fc1_hbm, w_fc1_s),
            (w_fc2_hbm, w_fc2_s),
            (cot_hbm, cot_s),
        ]
        return [
            pltpu.make_async_copy(source, target, load_sems.at[index])
            for index, (source, target) in enumerate(pairs)
        ]

    def saves(number):
        pairs = [
            (q_s, q_hbm),
            (k_s, k_hbm),
            (v_s, v_hbm),
            (normed_s, normed_hbm),
            (xhat_s, xhat_hbm),
            (rstd_s, rstd_hbm),
        ]
        return [
            pltpu.make_async_copy(source, target.at[number], save_sems.at[index])
            for index, (source, target) in enumerate(pairs)
        ]

    def p_save(number):
        slot = lax.rem(number, SLOTS)
        at = lax.div(number, PAIRS)
        pair = lax.rem(number, PAIRS)
        return pltpu.make_async_copy(
            p_s.at[slot], p_hbm.at[at, pl.ds(2 * pair, 2)], p_sems.at[slot]
        )

    @pl.when(step == 0)
    def _():
        for copy in loads():
            copy.start()

    @pl.when(jnp.logical_and(step > 0, step < clips))
    def _():
        for copy in saves(step - 1):
            copy.wait()
        for number in range(PAIRS - 1):
            p_save(PAIRS * (step - 1) + number).wait()

    @pl.when(jnp.logical_and(step > 1, step < clips))
    def _():
        p_save(PAIRS * (step - 1) - 1).wait()

    @pl.when(step < clips)
    def _():
        projected = dot(x_ref[0], w_proj_ref[...]) + b_proj_ref[...][None, :]
        high, middle, low = split3(projected - mask_ref[...][None, :])
        row = lax.broadcasted_iota(jnp.int32, (LEN, 1), 0)
        onehot = (row == pos_ref[0]).astype(f32).astype(bf16)[:, : x_ref.shape[1]]
        emb_s[...] = (
            (table_ref[...].reshape(LEN, D) + mask_ref[...][None, :])
            + dot(onehot, low)
            + dot(onehot, middle)
        ) + dot(onehot, high)
        for number in range(LEN // STEP):
            at = slice(number * STEP, (number + 1) * STEP)
            value = emb_s[at, :]
            centered = value - lane_mean(value)
            rstd = lax.rsqrt(lane_mean(centered * centered) + 1e-05)
            xhat = centered * rstd
            xhat_s[at, :] = xhat.astype(bf16)
            normed_s[at, :] = (xhat * gain1_ref[...][None, :] + bias1_ref[...][None, :]).astype(
                bf16
            )
            rstd_s[at, :] = rstd
        group = pl.ds(pl.multiple_of(step * rows, 8), rows)
        middle_s[group, :] = emb_s[:rows, :]
        normed = normed_s[...]
        k_s[...] = dot(normed, w_qkv_ref[:, D : 2 * D]).astype(bf16)
        v_s[...] = (dot(normed, w_qkv_ref[:, 2 * D :]) + v_bias_ref[...][None, :]).astype(bf16)
        q_s[...] = (dot(normed[:rows], w_qkv_ref[:, :D]) + q_bias_ref[...][None, :]).astype(bf16)
        for copy in saves(step):
            copy.start()

        def attend(pair, carry):
            number = step * PAIRS + pair
            slot = lax.rem(number, SLOTS)
            at = pl.ds(pl.multiple_of(pair * PAIR, PAIR), PAIR)
            query = q_s[:, at]
            key = k_s[:, at]
            value = jnp.concatenate([v_s[:, at], jnp.ones((LEN, PAIR), bf16)], axis=1)
            parts = []
            for head in range(2):
                scores = dot_rt(jnp.where(own_lanes(head), query, jnp.zeros_like(query)), key)
                largest = jnp.max(scores, axis=1, keepdims=True)
                weights = jnp.exp2(
                    (scores - largest) * (HEAD**-0.5 * np.log2(np.e))
                ).astype(bf16)
                p_s[slot, head] = weights
                parts.append(dot(weights, value))
            first = own_lanes(0)
            inverse = 1.0 / jnp.where(first, parts[0][:, PAIR:], parts[1][:, PAIR:])
            linv_s[group, at] = inverse
            att_s[group, at] = jnp.where(first, parts[0][:, :PAIR], parts[1][:, :PAIR]) * inverse
            p_save(number).start()
            return carry

        lax.fori_loop(0, PAIRS, attend, 0, unroll=UNROLL_F)

    @pl.when(step == 0)
    def _():
        norms_ref[...] = jnp.zeros_like(norms_ref)
        norms_ref[0:1, :] = square_sum(w_proj_ref[...])
        norms_ref[4:5, :] = square_sum(w_qkv_ref[...])
        b_fc1_s[...] = b_fc1_ref[...][None, :]

    @pl.when(step == clips)
    def _():
        for copy in loads():
            copy.wait()
        attended = att_s[...].astype(bf16)
        attended_s[...] = attended
        middle = middle_s[...] + (dot(attended, w_out_s[...]) + b_out_ref[...][None, :])
        centered = middle - lane_mean(middle)
        rstd = lax.rsqrt(lane_mean(centered * centered) + 1e-05)
        xhat = centered * rstd
        xhat2_s[...] = xhat
        rstd2_s[...] = rstd
        normed2_s[...] = (xhat * gain2_ref[...][None, :] + bias2_ref[...][None, :]).astype(bf16)
        middle_s[...] = middle + b_fc2_ref[...][None, :]
        gn_s[...] = jnp.zeros_like(gn_s)
        norms_ref[1:2, :] = square_sum(w_out_s[...])
        norms_ref[2:3, :] = square_sum(w_fc1_s[...])
        norms_ref[3:4, :] = square_sum(w_fc2_s[...])
        flat_s[FC_USED - 24 :, :] = jnp.zeros_like(flat_s[FC_USED - 24 :, :])

        def hidden_block(block, carry):
            normed2 = normed2_s[...]
            cot = cot_s[...]
            at = pl.ds(pl.multiple_of(block * BLOCK, BLOCK), BLOCK)
            w_fc1 = w_fc1_s[:, at]
            w_fc2 = w_fc2_s[at, :]
            pre = dot(normed2, w_fc1) + b_fc1_s[:, at]
            cdf = 0.5 + 0.5 * lax.erf(pre * np.float32(0.5**0.5))
            hidden = (pre * cdf).astype(bf16)
            slope = cdf + pre * (
                jnp.exp2(pre * pre * (-0.5 * np.log2(np.e))) * ((2 * np.pi) ** -0.5)
            )
            grad_pre = dot_rt(cot, w_fc2) * slope
            grad_pre_b = grad_pre.astype(bf16)
            middle_s[...] += dot(hidden, w_fc2)
            gn_s[...] += dot_rt(grad_pre_b, w_fc1)
            grad_w2 = dot_lt(hidden, cot).astype(bf16)
            for column in range(D // PAIR):
                first = FF * PAIRS + column * FF + block * BLOCK
                flat_s[pl.ds(pl.multiple_of(first, 16), BLOCK), :] = grad_w2[
                    :, column * PAIR : (column + 1) * PAIR
                ]
            grad_w1 = dot_lt(normed2, grad_pre_b).astype(bf16)
            sums = column_sums(grad_pre_b.astype(f32))
            for piece in range(BLOCK // PAIR):
                lanes = slice(piece * PAIR, (piece + 1) * PAIR)
                number = block * (BLOCK // PAIR) + piece
                flat_s[pl.ds(pl.multiple_of(number * D, 16), D), :] = grad_w1[:, lanes]
                row = 8 * lax.rem(number, PAIRS) + lax.div(number, PAIRS)
                vec_s[pl.ds(row, 1), :] = sums[:, lanes]
            return carry

        lax.fori_loop(0, BLOCKS, hidden_block, 0, unroll=UNROLL_M)
        out_s[...] = middle_s[...].astype(bf16)
        ends = [pltpu.make_async_copy(out_s, out_hbm, end_sems.at[0])]
        ends[0].start()
        cot_f = cot_s[...].astype(f32)
        grad_normed = gn_s[...]
        xhat = xhat2_s[...]
        scaled = grad_normed * gain2_ref[...][None, :]
        grad_middle = cot_f + rstd2_s[...] * (
            scaled - lane_mean(scaled) - xhat * lane_mean(scaled * xhat)
        )
        middle_s[...] = grad_middle
        ends.append(pltpu.make_async_copy(middle_s, gmid_hbm, end_sems.at[1]))
        ends[1].start()
        grad_branch = grad_middle.astype(bf16)
        vectors = [
            column_sums(cot_f),
            column_sums(grad_normed * xhat),
            column_sums(grad_normed),
            column_sums(grad_branch.astype(f32)),
        ]
        grad_out = dot_lt(attended_s[...], grad_branch).astype(bf16)
        for column in range(D // PAIR):
            lanes = slice(column * PAIR, (column + 1) * PAIR)
            first = 2 * FF * PAIRS + column * D
            flat_s[first : first + D, :] = grad_out[:, lanes]
            for number, vector in enumerate(vectors):
                row = 8 * column + 4 + number
                vec_s[row : row + 1, :] = vector[:, lanes]
        flat_s[FC_USED - 24 : FC_USED, :] = vec_s[...].astype(bf16)
        bit = start_ref[1]
        for index, (side, target) in enumerate([(bit, kept_hbm), (1 - bit, sent_hbm)]):
            copy = pltpu.make_async_copy(
                flat_s.at[pl.ds(pl.multiple_of(side * half, 16), half)],
                target,
                end_sems.at[2 + index],
            )
            copy.start()
            ends.append(copy)
        grad_att = dot_rt(grad_branch, w_out_s[...]).astype(bf16).astype(f32)
        grad_s = (grad_att * linv_s[...]).astype(bf16)
        gs_ref[...] = grad_s
        product = grad_s.astype(f32) * att_s[...]
        lane = lax.broadcasted_iota(jnp.int32, (1, PAIR), 1)
        packed = jnp.zeros((clips * rows, PAIR), f32)
        for pair in range(PAIRS):
            piece = product[:, pair * PAIR : (pair + 1) * PAIR]
            for head in range(2):
                inner = -jnp.sum(
                    jnp.where(own_lanes(head), piece, 0.0), axis=1, keepdims=True
                )
                for index, term in enumerate(split3(inner)):
                    at = 3 * (2 * pair + head) + index
                    packed = jnp.where(lane == at, term.astype(f32), packed)
        extra_ref[...] = packed.astype(bf16)
        for copy in ends + saves(clips - 1):
            copy.wait()
        for number in range(PAIRS * clips - PAIRS - 1, PAIRS * clips):
            p_save(number).wait()


def backward_kernel(
    start_ref,
    q_ref,
    k_ref,
    v_ref,
    gs_ref,
    extra_ref,
    x_ref,
    pos_ref,
    w_qkv_ref,
    gain1_ref,
    p_hbm,
    normed_hbm,
    xhat_hbm,
    rstd_hbm,
    gmid_hbm,
    *rest,
    rows,
    base,
    count,
    last,
):
    if last:
        acc_hbm, kept_ref, sent_ref, proj_kept_ref, proj_sent_ref = rest[:5]
        acc_s, total_sem = rest[5:7]
        scratch = rest[7:]
    else:
        acc_s, proj_kept_ref, proj_sent_ref = rest[:3]
        scratch = rest[3:]
    (p_s, normed_s, xhat_s, rstd_s, own_s, dq_s, dkv_s, gn_s, high_s, low_s, proj_s) = scratch[:-2]
    sems, p_sems = scratch[-2:]
    clip = pl.program_id(0)
    lane = lax.broadcasted_iota(jnp.int32, (1, PAIR), 1)

    def loads():
        at = base + clip
        pairs = [
            (normed_hbm.at[at], normed_s),
            (xhat_hbm.at[at], xhat_s),
            (rstd_hbm.at[at], rstd_s),
            (gmid_hbm.at[pl.ds(pl.multiple_of(at * rows, 8), rows)], own_s.at[pl.ds(0, rows)]),
        ]
        return [
            pltpu.make_async_copy(source, target, sems.at[index])
            for index, (source, target) in enumerate(pairs)
        ]

    def p_load(number):
        at = lax.div(number, PAIRS)
        pair = lax.rem(number, PAIRS)
        slot = lax.rem(number, 2 * PAIRS)
        return pltpu.make_async_copy(
            p_hbm.at[base + at, pl.ds(2 * pair, 2)], p_s.at[slot], p_sems.at[slot]
        )

    @pl.when(clip == 0)
    def _():
        for pair in range(PAIRS):
            p_load(pair).start()

    for copy in loads():
        copy.start()

    @pl.when(clip == 0)
    def _():
        own_s[rows:, :] = jnp.zeros_like(own_s[rows:, :])
        if last:
            pltpu.make_async_copy(acc_hbm, acc_s, total_sem).start()
        else:
            acc_s[...] = jnp.zeros_like(acc_s)

    def attend_back(phase, carry):
        number = clip * PAIRS + phase
        slot = lax.rem(number, 2 * PAIRS)
        p_load(number).wait()
        at = pl.ds(pl.multiple_of(phase * PAIR, PAIR), PAIR)
        query = q_ref[0, :, at] * jnp.asarray(HEAD**-0.5, bf16)
        key = k_ref[0, :, at]
        value = jnp.concatenate([v_ref[0, :, at], jnp.ones((LEN, PAIR), bf16)], axis=1)
        grad = gs_ref[:, at]
        extra = extra_ref[...]
        queries, keys, values = [], [], []
        for head in range(2):
            first = 3 * (2 * phase + head)
            inner = jnp.logical_and(lane >= first, lane < first + 3)
            left = jnp.concatenate(
                [
                    jnp.where(own_lanes(head), grad, jnp.zeros_like(grad)),
                    jnp.where(inner, extra, jnp.zeros_like(extra)),
                ],
                axis=1,
            )
            weights = p_s[slot, head]
            grad_scores = (weights.astype(f32) * dot_rt(left, value)).astype(bf16)
            queries.append(dot(grad_scores, key))
            keys.append(dot_lt(grad_scores, query))
            values.append(dot_lt(weights, grad))
        side = own_lanes(0)
        dq_s[:, at] = (jnp.where(side, queries[0], queries[1]) * (HEAD**-0.5)).astype(bf16)
        dkv_s[:, at] = jnp.where(side, keys[0], keys[1]).astype(bf16)
        at = pl.ds(pl.multiple_of(phase * PAIR + D, PAIR), PAIR)
        dkv_s[:, at] = jnp.where(side, values[0], values[1]).astype(bf16)
        return carry

    lax.fori_loop(0, PAIRS, attend_back, 0, unroll=UNROLL_B)

    @pl.when(clip + 1 < count)
    def _():
        for pair in range(PAIRS):
            p_load(PAIRS * (clip + 1) + pair).start()

    for copy in loads():
        copy.wait()
    if last:

        @pl.when(clip == 0)
        def _():
            pltpu.make_async_copy(acc_hbm, acc_s, total_sem).wait()

    if True:

        normed = normed_s[...]
        grad_q = dq_s[...]
        grad_kv = dkv_s[...]
        gn_s[...] = dot_rt(grad_kv, w_qkv_ref[:, D:])
        gn_s[:rows, :] += dot_rt(grad_q, w_qkv_ref[:, :D])
        part_q = dot_lt(normed[:rows], grad_q)
        part_kv = dot_lt(normed, grad_kv)
        for index in range(PAIRS):
            acc_s[index * D : (index + 1) * D, :] += part_q[:, index * PAIR : (index + 1) * PAIR]
        for index in range(2 * PAIRS):
            first = (PAIRS + index) * D
            acc_s[first : first + D, :] += part_kv[:, index * PAIR : (index + 1) * PAIR]
        ones = jnp.ones((8, LEN), bf16)
        sum_q = dot(ones[:, :rows], grad_q)[:1]
        sum_v = dot(ones, grad_kv[:, D:])[:1]

        def norm_rows(number, carry, with_own):
            at = pl.ds(pl.multiple_of(number * STEP, STEP), STEP)
            sum_gain, sum_bias, sum_emb = carry
            value = gn_s[at, :]
            xhat = xhat_s[at, :].astype(f32)
            sum_bias = sum_bias + column_sums(value)
            sum_gain = sum_gain + column_sums(value * xhat)
            scaled = value * gain1_ref[...][None, :]
            grad = rstd_s[at, :] * (
                scaled - lane_mean(scaled) - xhat * lane_mean(scaled * xhat)
            )
            if with_own:
                grad = grad + own_s[at, :]
            sum_emb = sum_emb + column_sums(grad)
            high = grad.astype(bf16)
            high_s[at, :] = high
            low_s[at, :] = (grad - high.astype(f32)).astype(bf16)
            return sum_gain, sum_bias, sum_emb

        zero = jnp.zeros((1, D), f32)
        own_steps = own_s.shape[0] // STEP
        carry = lax.fori_loop(
            0, own_steps, functools.partial(norm_rows, with_own=True), (zero, zero, zero), unroll=True
        )
        sum_gain, sum_bias, sum_emb = lax.fori_loop(
            own_steps, LEN // STEP, functools.partial(norm_rows, with_own=False), carry, unroll=True
        )
        row = lax.broadcasted_iota(jnp.int32, (LEN, 1), 0)
        onehot = (row == pos_ref[0]).astype(f32).astype(bf16)
        grad_proj = dot_lt(onehot, high_s[...]) + dot_lt(onehot, low_s[...])
        proj_s[...] = grad_proj
        bit = start_ref[1]
        part = SLOT // 2
        proj_kept_ref[0] = proj_s[pl.ds(pl.multiple_of(bit * part, 8), part), :]
        proj_sent_ref[0] = proj_s[
            pl.ds(pl.multiple_of((1 - bit) * part, 8), part), :
        ].astype(bf16)
        sum_proj = column_sums(grad_proj)
        vectors = [sum_proj, sum_emb - sum_proj, sum_gain, sum_bias, sum_q, sum_v]
        weight = dot_lt(x_ref[0], grad_proj[: x_ref.shape[1]].astype(bf16))
        for index in range(D // PAIR):
            lanes = slice(index * PAIR, (index + 1) * PAIR)
            first = 3 * PAIRS * D + index * DIN
            acc_s[first : first + DIN, :] += weight[:, lanes]
            first = 3 * PAIRS * D + PAIRS * DIN + 8 * index
            for number, vector in enumerate(vectors):
                acc_s[first + number : first + number + 1, :] += vector[:, lanes]

    if last:

        @pl.when(clip == count - 1)
        def _():
            bit = start_ref[1]
            half = kept_ref.shape[0]
            kept_ref[...] = acc_s[pl.ds(pl.multiple_of(bit * half, 8), half), :]
            sent_ref[...] = acc_s[pl.ds(pl.multiple_of((1 - bit) * half, 8), half), :].astype(
                bf16
            )


def place(target, lanes, source, parts, total):
    for side, where, at, size in parts:
        value = source(side, where, size).astype(f32)
        target[at : at + size, lanes] = value
        if total is not None:
            square = jnp.sum((value * value).reshape(size // 8, 8, PAIR), axis=0)
            total = square if total is False else total + square
    return total


def split_rows(first, count, half):
    result = []
    done = 0
    while done < count:
        side, inside = divmod(first + done, half)
        length = min(count - done, half - inside)
        result.append((side, inside, done, length))
        done += length
    return result


def lanes_of(index):
    return slice(index * PAIR, (index + 1) * PAIR)


def whole_mean(total, size):
    value = jnp.sum(jnp.sum(total, axis=1, keepdims=True), axis=0, keepdims=True)
    return value / size


def assemble_fc_kernel(
    start_ref,
    mine_ref,
    other_ref,
    w_out_ref,
    w_fc1_ref,
    w_fc2_ref,
    b_out_ref,
    gain_ref,
    bias_ref,
    b_fc1_ref,
    b_fc2_ref,
    mean_ref,
):
    half = mine_ref.shape[0]

    def body(halves):
        def source(side, where, size):
            return halves[side][where : where + size, :]

        total = False
        for index in range(PAIRS):
            parts = split_rows(2 * FF * PAIRS + index * D, D, half)
            total = place(w_out_ref, lanes_of(index), source, parts, total)
        mean_out = whole_mean(total, D * D)
        total = False
        for index in range(FF // PAIR):
            parts = split_rows(index * D, D, half)
            total = place(w_fc1_ref, lanes_of(index), source, parts, total)
        mean_fc1 = whole_mean(total, D * FF)
        total = False
        for index in range(PAIRS):
            parts = split_rows(FF * PAIRS + index * FF, FF, half)
            total = place(w_fc2_ref, lanes_of(index), source, parts, total)
        mean_fc2 = whole_mean(total, FF * D)
        first = 2 * FF * PAIRS + PAIRS * D - half
        vectors = source(1, first, 24).astype(f32)
        for index in range(PAIRS):
            lanes = lanes_of(index)
            for number in range(4):
                b_fc1_ref[number * D + index * PAIR : number * D + (index + 1) * PAIR] = vectors[
                    8 * index + number
                ]
            for number, target in enumerate([b_fc2_ref, gain_ref, bias_ref, b_out_ref]):
                target[lanes] = vectors[8 * index + 4 + number]
        row = lax.broadcasted_iota(jnp.int32, (8, PAIR), 0)
        mean_ref[...] = jnp.where(
            row == 1, mean_out, jnp.where(row == 2, mean_fc1, mean_fc2)
        )

    bit = start_ref[1]

    @pl.when(bit == 0)
    def _():
        body((mine_ref, other_ref))

    @pl.when(bit == 1)
    def _():
        body((other_ref, mine_ref))


def assemble_qkv_kernel(
    start_ref,
    *refs,
    far,
    chunk,
):
    planes = refs[:8]
    (
        norms_ref,
        mean_ref,
        w_proj_ref,
        w_qkv_ref,
        b_proj_ref,
        mask_ref,
        gain_ref,
        bias_ref,
        q_bias_ref,
        v_bias_ref,
        trust_ref,
        trust_qkv_ref,
        full_s,
        sems,
    ) = refs[8:]
    half = 4 * far * chunk
    bit = start_ref[1]
    copies = []
    for side in range(2):
        for plane in range(4):
            for line in range(far):
                place_at = jnp.bitwise_xor(start_ref[2], plane * far + line) * chunk
                place_at = place_at + (bit if side == 0 else 1 - bit) * half
                copies.append(
                    pltpu.make_async_copy(
                        planes[4 * side + plane].at[pl.ds(line * chunk, chunk)],
                        full_s.at[pl.ds(pl.multiple_of(place_at, 16), chunk)],
                        sems.at[len(copies)],
                    )
                )
    for copy in copies:
        copy.start()
    for copy in copies:
        copy.wait()

    def source(side, where, size):
        return full_s[where : where + size, :]

    total = False
    for index in range(PAIRS):
        parts = [(0, 3 * PAIRS * D + index * DIN, 0, DIN)]
        total = place(w_proj_ref, lanes_of(index), source, parts, total)
    mean_proj = whole_mean(total, DIN * D)
    total = False
    for index in range(3 * PAIRS):
        parts = [(0, index * D, 0, D)]
        total = place(w_qkv_ref, lanes_of(index), source, parts, total)
    mean_qkv = whole_mean(total, D * 3 * D)
    vectors = source(0, 3 * PAIRS * D + PAIRS * DIN, 24).astype(f32)
    targets = [b_proj_ref, mask_ref, gain_ref, bias_ref, q_bias_ref, v_bias_ref]
    for index in range(PAIRS):
        for number, target in enumerate(targets):
            target[lanes_of(index)] = vectors[8 * index + number]
    lane = lax.broadcasted_iota(jnp.int32, (1, PAIR), 1)
    means = [mean_proj, mean_ref[1:2], mean_ref[2:3], mean_ref[3:4], mean_qkv]
    sums = jnp.sum(norms_ref[...], axis=1, keepdims=True)
    sizes = [DIN * D, D * D, D * FF, FF * D, D * 3 * D]
    grads = jnp.ones((1, PAIR), f32)
    weights = jnp.ones((1, PAIR), f32)
    for index, (mean, size) in enumerate(zip(means, sizes)):
        grads = jnp.where(lane == index, mean, grads)
        weights = jnp.where(lane == index, sums[index : index + 1] / size, weights)
    ratios = jnp.sqrt(weights) / jnp.sqrt(grads + 1e-06)
    trust_ref[...] = ratios[0, :4]
    trust_qkv_ref[...] = ratios[0, 4:5]


def whole(shape):
    return pl.BlockSpec(shape, lambda i, s: (0,) * len(shape), pipeline_mode=pl.Buffered(1))


def shape_of(shape, dtype):
    return jax.ShapeDtypeStruct(shape, dtype)


def kernel_call(kernel, grid, in_specs, out_specs, out_shape, scratch, name, cost, args):
    return pl.pallas_call(
        kernel,
        grid_spec=pltpu.PrefetchScalarGridSpec(
            num_scalar_prefetch=1,
            grid=grid,
            in_specs=in_specs,
            out_specs=out_specs,
            scratch_shapes=scratch,
        ),
        out_shape=out_shape,
        compiler_params=pltpu.CompilerParams(
            dimension_semantics=("arbitrary",), vmem_limit_bytes=VMEM
        ),
        cost_estimate=pl.CostEstimate(
            flops=cost[0], bytes_accessed=cost[1], transcendentals=cost[2]
        ),
        name=name,
    )(*args)


def run_forward(start, x_vis, padded_pos, table, params, cotangent, rows, half):
    clips, visible, _ = x_vis.shape
    (
        w_proj,
        b_proj,
        mask_token,
        ln1_gain,
        ln1_bias,
        w_qkv,
        q_bias,
        v_bias,
        w_out,
        b_out,
        ln2_gain,
        ln2_bias,
        w_fc1,
        b_fc1,
        w_fc2,
        b_fc2,
    ) = params
    tokens = clips * rows
    any_space = pl.BlockSpec(memory_space=pl.ANY)
    vector = whole((D,))

    def clip_at(i):
        return jnp.minimum(i, clips - 1)

    in_specs = [
        pl.BlockSpec((1, visible, DIN), lambda i, s: (clip_at(i), 0, 0)),
        pl.BlockSpec((1, 1, SLOT), lambda i, s: (clip_at(i), 0, 0)),
        pl.BlockSpec(
            (pl.Element(LEN // 8), pl.Element(8), pl.Element(D)),
            lambda i, s: (s[0], 0, 0),
            pipeline_mode=pl.Buffered(1),
        ),
        whole((DIN, D)),
        vector,
        vector,
        vector,
        vector,
        whole((D, 3 * D)),
        vector,
        vector,
        vector,
        vector,
        vector,
        whole((FF,)),
        vector,
    ] + [any_space] * 4
    out_specs = [whole((tokens, D)), whole((tokens, PAIR)), whole((8, PAIR))] + [any_space] * 11
    out_shape = [
        shape_of((tokens, D), bf16),
        shape_of((tokens, PAIR), bf16),
        shape_of((8, PAIR), f32),
        shape_of((tokens, D), bf16),
        shape_of((tokens, D), f32),
        shape_of((half, PAIR), bf16),
        shape_of((half, PAIR), bf16),
        shape_of((clips, HEADS, rows, LEN), bf16),
        shape_of((clips, rows, D), bf16),
        shape_of((clips, LEN, D), bf16),
        shape_of((clips, LEN, D), bf16),
        shape_of((clips, LEN, D), bf16),
        shape_of((clips, LEN, D), bf16),
        shape_of((clips, LEN, 1), f32),
    ]
    scratch = [
        pltpu.VMEM((SLOTS, 2, rows, LEN), bf16),
        pltpu.VMEM((rows, D), bf16),
        pltpu.VMEM((LEN, D), bf16),
        pltpu.VMEM((LEN, D), bf16),
        pltpu.VMEM((LEN, D), bf16),
        pltpu.VMEM((LEN, D), bf16),
        pltpu.VMEM((LEN, 1), f32),
        pltpu.VMEM((LEN, D), f32),
        pltpu.VMEM((tokens, D), f32),
        pltpu.VMEM((tokens, D), f32),
        pltpu.VMEM((tokens, D), f32),
        pltpu.VMEM((tokens, D), bf16),
        pltpu.VMEM((tokens, D), f32),
        pltpu.VMEM((tokens, 1), f32),
        pltpu.VMEM((tokens, D), bf16),
        pltpu.VMEM((tokens, D), f32),
        pltpu.VMEM((24, PAIR), f32),
        pltpu.VMEM((2 * half, PAIR), bf16),
        pltpu.VMEM((tokens, D), bf16),
        pltpu.VMEM((D, D), bf16),
        pltpu.VMEM((D, FF), bf16),
        pltpu.VMEM((FF, D), bf16),
        pltpu.VMEM((tokens, D), bf16),
        pltpu.VMEM((1, FF), f32),
        pltpu.SemaphoreType.DMA((6,)),
        pltpu.SemaphoreType.DMA((SLOTS,)),
        pltpu.SemaphoreType.DMA((4,)),
        pltpu.SemaphoreType.DMA((4,)),
    ]
    return kernel_call(
        functools.partial(forward_kernel, rows=rows, clips=clips),
        (clips + 1,),
        in_specs,
        out_specs,
        out_shape,
        scratch,
        "forward",
        (40_000_000_000, 60_000_000, 13_000_000),
        (
            start,
            x_vis,
            padded_pos,
            table,
            w_proj,
            b_proj,
            mask_token,
            ln1_gain,
            ln1_bias,
            w_qkv,
            q_bias,
            v_bias,
            b_out,
            ln2_gain,
            ln2_bias,
            b_fc1,
            b_fc2,
            w_out,
            w_fc1,
            w_fc2,
            cotangent.reshape(tokens, D),
        ),
    )


def run_backward(start, saved, x_vis, padded_pos, w_qkv, ln1_gain, rows, half, base, count, acc):
    query, key, value, grads, extra, weights, normed, xhat, rstd, gmid = saved
    _, visible, _ = x_vis.shape
    last = acc is not None
    own_rows = -(-rows // STEP) * STEP
    any_space = pl.BlockSpec(memory_space=pl.ANY)

    def at(i):
        return base + i

    def block(*shape):
        return pl.BlockSpec((1,) + shape, lambda i, s: (at(i),) + (0,) * len(shape))

    proj_spec = pl.BlockSpec((1, SLOT // 2, D), lambda i, s: (i, 0, 0))
    proj_shapes = [
        shape_of((count, SLOT // 2, D), f32),
        shape_of((count, SLOT // 2, D), bf16),
    ]
    in_specs = [
        block(rows, D),
        block(LEN, D),
        block(LEN, D),
        pl.BlockSpec((rows, D), lambda i, s: (at(i), 0)),
        pl.BlockSpec((rows, PAIR), lambda i, s: (at(i), 0)),
        block(visible, DIN),
        block(1, SLOT),
        whole((D, 3 * D)),
        whole((D,)),
    ] + [any_space] * 5
    args = [
        start,
        query,
        key,
        value,
        grads,
        extra,
        x_vis,
        padded_pos,
        w_qkv,
        ln1_gain,
        weights,
        normed,
        xhat,
        rstd,
        gmid,
    ]
    scratch = [
        pltpu.VMEM((2 * PAIRS, 2, rows, LEN), bf16),
        pltpu.VMEM((LEN, D), bf16),
        pltpu.VMEM((LEN, D), bf16),
        pltpu.VMEM((LEN, 1), f32),
        pltpu.VMEM((own_rows, D), f32),
        pltpu.VMEM((rows, D), bf16),
        pltpu.VMEM((LEN, 2 * D), bf16),
        pltpu.VMEM((LEN, D), f32),
        pltpu.VMEM((LEN, D), bf16),
        pltpu.VMEM((LEN, D), bf16),
        pltpu.VMEM((SLOT, D), f32),
        pltpu.SemaphoreType.DMA((4,)),
        pltpu.SemaphoreType.DMA((2 * PAIRS,)),
    ]
    if last:
        in_specs.append(any_space)
        args.append(acc)
        out_specs = [whole((half, PAIR)), whole((half, PAIR)), proj_spec, proj_spec]
        out_shape = [shape_of((half, PAIR), f32), shape_of((half, PAIR), bf16)] + proj_shapes
        scratch = [pltpu.VMEM((2 * half, PAIR), f32), pltpu.SemaphoreType.DMA] + scratch
    else:
        out_specs = [whole((2 * half, PAIR)), proj_spec, proj_spec]
        out_shape = [shape_of((2 * half, PAIR), f32)] + proj_shapes
    return kernel_call(
        functools.partial(backward_kernel, rows=rows, base=base, count=count, last=last),
        (count,),
        in_specs,
        out_specs,
        out_shape,
        scratch,
        "backward",
        (16_000_000_000 * count, 20_000_000 * count, 0),
        tuple(args),
    )


def run_assemble_fc(start, mine, other):
    half = mine.shape[0]
    shapes = [(D, D), (D, FF), (FF, D), (D,), (D,), (D,), (FF,), (D,), (8, PAIR)]
    return kernel_call(
        assemble_fc_kernel,
        (1,),
        [whole((half, PAIR)), whole((half, PAIR))],
        [whole(size) for size in shapes],
        [shape_of(size, f32) for size in shapes],
        [],
        "assemble_fc",
        (10_000_000, 8_000_000, 0),
        (start, mine, other),
    )


def run_assemble_qkv(start, planes, norms, means, far, chunk):
    any_space = pl.BlockSpec(memory_space=pl.ANY)
    shapes = [(DIN, D), (D, 3 * D), (D,), (D,), (D,), (D,), (D,), (D,), (4,), (1,)]
    return kernel_call(
        functools.partial(assemble_qkv_kernel, far=far, chunk=chunk),
        (1,),
        [any_space] * 8 + [whole((8, PAIR)), whole((8, PAIR))],
        [whole(size) for size in shapes],
        [shape_of(size, f32) for size in shapes],
        [
            pltpu.VMEM((8 * far * chunk, PAIR), bf16),
            pltpu.SemaphoreType.DMA((8 * far,)),
        ],
        "assemble_qkv",
        (10_000_000, 5_000_000, 0),
        (start, *planes, norms, means),
    )


def add_received(kept, received):
    return kept.astype(f32) + received.astype(f32)


def shards(x_vis, vis_pos, *rest):
    params, cotangent = rest[:-1], rest[-1]
    w_proj, ln1_gain, w_qkv = params[0], params[3], params[5]
    seq_size = lax.axis_size("seq")
    clip_size = lax.axis_size("clip")
    groups = seq_size * clip_size // 2
    rows = LEN // seq_size
    clips, visible, _ = x_vis.shape
    far = clip_size // 2
    members = [
        [
            s * clip_size + 2 * high + low
            for s in range(core, seq_size, 2)
            for low in range(2)
            for high in range(far)
        ]
        for core in range(2)
    ]

    def chunk_rows(used):
        return -(-used // (32 * groups)) * 16

    core_pairs = [(s, s ^ 1) for s in range(seq_size)]
    chip_pairs = [(s, s ^ 2) for s in range(seq_size)]

    def across_core(value):
        return lax.ppermute(value, "seq", core_pairs)

    def swap(value):
        chunks = value.reshape(groups, -1, PAIR)
        return lax.all_to_all(chunks, AXES, 0, 0, axis_index_groups=members)

    def total_of(chunks):
        return jnp.sum(chunks.astype(f32), axis=0).astype(bf16)

    def spread(chunk, size):
        return jnp.broadcast_to(chunk[None], (size,) + chunk.shape)

    def across(value, seq_change, low_change, high_change):
        pairs = []
        for s in range(seq_size):
            for c in range(clip_size):
                other = (s ^ (2 * seq_change)) * clip_size + (c ^ (2 * high_change + low_change))
                pairs.append((s * clip_size + c, other))
        return lax.ppermute(value, AXES, pairs)

    def gather(chunk):
        size = 1
        while size < far:
            count = min(4, far // size)
            chunk = jnp.concatenate(
                [chunk] + [across(chunk, 0, 0, size * k) for k in range(1, count)]
            )
            size *= count
        return [chunk] + [across(chunk, k >> 1, k & 1, 0) for k in (1, 2, 3)]

    fc_chunk = chunk_rows(FC_USED)
    qkv_chunk = chunk_rows(QKV_USED)
    qkv_half = qkv_chunk * groups
    seq_index = lax.axis_index("seq")
    bit = seq_index & 1
    first = seq_index * rows
    local_pos = jnp.where(vis_pos >= first, vis_pos - first, vis_pos - first + LEN)
    padded_pos = jnp.pad(local_pos, ((0, 0), (0, SLOT - visible)), constant_values=-1)[:, None, :]
    table = sinusoid_table(LEN, D)
    table = jnp.asarray(np.concatenate([table, table[: LEN - rows]]).reshape(-1, 8, D))
    clip_index = lax.axis_index("clip")
    number = ((seq_index >> 1) * 2 + (clip_index & 1)) * far + (clip_index >> 1)
    start = jnp.stack([first // 8, bit, number]).astype(jnp.int32)

    (
        grads,
        extra,
        norms,
        output,
        gmid,
        kept,
        sent,
        weights,
        query,
        key,
        value,
        normed,
        xhat,
        rstd,
    ) = run_forward(start, x_vis, padded_pos, table, params, cotangent, rows, fc_chunk * groups)
    fc = add_received(kept, across_core(sent)).astype(bf16)
    fc, query = lax.optimization_barrier((fc, query))
    fc = swap(fc)
    saved = (query, key, value, grads, extra, weights, normed, xhat, rstd, gmid)
    acc, proj_kept0, proj_sent0 = run_backward(
        start, saved, x_vis, padded_pos, w_qkv, ln1_gain, rows, qkv_half, 0, clips - 1, None
    )
    fc, acc = lax.optimization_barrier((spread(total_of(fc), groups), acc))
    fc = swap(fc).reshape(groups * fc_chunk, PAIR)
    kept, sent, proj_kept1, proj_sent1 = run_backward(
        start, saved, x_vis, padded_pos, w_qkv, ln1_gain, rows, qkv_half, clips - 1, 1, acc
    )
    qkv = add_received(kept, across_core(sent)).astype(bf16)
    fc, qkv = lax.optimization_barrier((fc, qkv))
    qkv = swap(qkv)
    w_out_g, w_fc1_g, w_fc2_g, b_out_g, gain2_g, bias2_g, b_fc1_g, b_fc2_g, means = (
        run_assemble_fc(start, fc, across_core(fc))
    )
    qkv, means = lax.optimization_barrier((total_of(qkv), means))
    planes = gather(qkv)
    planes += [across_core(plane) for plane in planes]
    proj_kept = jnp.concatenate([proj_kept0, proj_kept1])
    proj_sent = jnp.concatenate([proj_sent0, proj_sent1])
    part = add_received(proj_kept, across_core(proj_sent)).astype(bf16)
    part = add_received(part, lax.ppermute(part, "seq", chip_pairs)).astype(bf16)
    other = across_core(part)
    grad_projected = jnp.where(
        bit == 0,
        jnp.concatenate([part, other], axis=1),
        jnp.concatenate([other, part], axis=1),
    )[:, :visible]
    grad_x = lax.dot_general(
        grad_projected, w_proj, (((2,), (1,)), ((), ())), preferred_element_type=f32
    )
    (
        w_proj_g,
        w_qkv_g,
        b_proj_g,
        mask_g,
        gain1_g,
        bias1_g,
        q_bias_g,
        v_bias_g,
        trust,
        trust_qkv,
    ) = run_assemble_qkv(start, planes, norms, means, far, qkv_chunk)
    return (
        output.reshape(clips, rows, D),
        grad_x,
        w_proj_g,
        b_proj_g,
        mask_g,
        gain1_g,
        bias1_g,
        w_qkv_g,
        q_bias_g,
        v_bias_g,
        w_out_g,
        b_out_g,
        gain2_g,
        bias2_g,
        w_fc1_g,
        b_fc1_g,
        w_fc2_g,
        b_fc2_g,
        trust,
        trust_qkv,
    )


def solution(mesh):
    return jax.shard_map(
        shards,
        mesh=mesh,
        in_specs=(P("clip", None, None), P("clip", None))
        + (P(),) * 16
        + (P("clip", "seq", None),),
        out_specs=(P("clip", "seq", None), P("clip", None, None)) + (P(),) * 18,
        check_vma=False,
    )
```

```python
import functools

import jax
import jax.numpy as jnp
import numpy as np
from jax import lax
from jax.experimental import pallas as pl
from jax.experimental.pallas import tpu as pltpu
from jax.sharding import PartitionSpec as P

D = 384
HEADS = 6
HEAD = 64
PAIRS = 3
PAIR = 128
FF = 1536
DIN = 768
SLOT = 160
LEN = 1568
STEP = 112
BLOCK = 256
BLOCKS = FF // BLOCK
SLOTS = 4
UNROLL_F = True
UNROLL_M = False
UNROLL_B = False
FC_USED = 10392
QKV_USED = 5784
AXES = ("seq", "clip")
VMEM = 60 * 1024 * 1024

bf16 = jnp.bfloat16
f32 = jnp.float32


def dot(left, right):
    return lax.dot_general(
        left, right, (((1,), (0,)), ((), ())), preferred_element_type=f32
    )


def dot_rt(left, right):
    return lax.dot_general(
        left, right, (((1,), (1,)), ((), ())), preferred_element_type=f32
    )


def dot_lt(left, right):
    return lax.dot_general(
        left, right, (((0,), (0,)), ((), ())), preferred_element_type=f32
    )


def split3(value):
    high = value.astype(bf16)
    rest = value - high.astype(f32)
    middle = rest.astype(bf16)
    low = (rest - middle.astype(f32)).astype(bf16)
    return high, middle, low


def sinusoid_table(length, columns):
    positions = np.arange(length, dtype=np.float64)[:, None]
    column = np.arange(columns)
    angles = positions / np.power(10000.0, (2 * (column // 2)) / columns)[None, :]
    return np.where((column % 2)[None, :] == 0, np.sin(angles), np.cos(angles)).astype(np.float32)


def row_loop(total, body, carry, unroll=False):
    full = total // STEP

    def at_step(number, carry):
        return body(pl.ds(pl.multiple_of(number * STEP, STEP), STEP), carry)

    carry = lax.fori_loop(0, full, at_step, carry, unroll=unroll)
    if total % STEP:
        carry = body(pl.ds(full * STEP, total % STEP), carry)
    return carry


def own_lanes(head):
    lane = lax.broadcasted_iota(jnp.int32, (1, PAIR), 1)
    return (lane < HEAD) if head == 0 else (lane >= HEAD)


def column_sums(value):
    return jnp.sum(value, axis=0, keepdims=True)


def square_sum(ref):
    rows, columns = ref.shape
    size = 64

    def add(number, total):
        piece = ref[pl.ds(pl.multiple_of(number * size, size), size), :].astype(f32)
        sums = column_sums(piece * piece)
        for first in range(0, columns, PAIR):
            total = total + sums[:, first : first + PAIR]
        return total

    return lax.fori_loop(0, rows // size, add, jnp.zeros((1, PAIR), f32))


def lane_mean(value):
    return jnp.mean(value, axis=1, keepdims=True)


def forward_kernel(
    start_ref,
    x_ref,
    pos_ref,
    table_ref,
    w_proj_ref,
    b_proj_ref,
    mask_ref,
    gain1_ref,
    bias1_ref,
    w_qkv_ref,
    q_bias_ref,
    v_bias_ref,
    b_out_ref,
    gain2_ref,
    bias2_ref,
    b_fc1_ref,
    b_fc2_ref,
    w_out_hbm,
    w_fc1_hbm,
    w_fc2_hbm,
    cot_hbm,
    gs_ref,
    extra_ref,
    norms_ref,
    out_hbm,
    gmid_hbm,
    kept_hbm,
    sent_hbm,
    p_hbm,
    q_hbm,
    k_hbm,
    v_hbm,
    normed_hbm,
    xhat_hbm,
    rstd_hbm,
    p_s,
    q_s,
    k_s,
    v_s,
    normed_s,
    xhat_s,
    rstd_s,
    emb_s,
    middle_s,
    att_s,
    linv_s,
    attended_s,
    xhat2_s,
    rstd2_s,
    normed2_s,
    gn_s,
    vec_s,
    flat_s,
    out_s,
    w_out_s,
    w_fc1_s,
    w_fc2_s,
    cot_s,
    b_fc1_s,
    save_sems,
    p_sems,
    load_sems,
    end_sems,
    *,
    rows,
    clips,
):
    step = pl.program_id(0)
    half = kept_hbm.shape[0]

    def loads():
        pairs = [
            (w_out_hbm, w_out_s),
            (w_fc1_hbm, w_fc1_s),
            (w_fc2_hbm, w_fc2_s),
            (cot_hbm, cot_s),
        ]
        return [
            pltpu.make_async_copy(source, target, load_sems.at[index])
            for index, (source, target) in enumerate(pairs)
        ]

    def saves(number):
        pairs = [
            (q_s, q_hbm),
            (k_s, k_hbm),
            (v_s, v_hbm),
            (normed_s, normed_hbm),
            (xhat_s, xhat_hbm),
            (rstd_s, rstd_hbm),
        ]
        return [
            pltpu.make_async_copy(source, target.at[number], save_sems.at[index])
            for index, (source, target) in enumerate(pairs)
        ]

    def p_save(number):
        slot = lax.rem(number, SLOTS)
        at = lax.div(number, PAIRS)
        pair = lax.rem(number, PAIRS)
        return pltpu.make_async_copy(
            p_s.at[slot], p_hbm.at[at, pl.ds(2 * pair, 2)], p_sems.at[slot]
        )

    @pl.when(step == 0)
    def _():
        for copy in loads():
            copy.start()

    @pl.when(jnp.logical_and(step > 0, step < clips))
    def _():
        for copy in saves(step - 1):
            copy.wait()
        for number in range(PAIRS - 1):
            p_save(PAIRS * (step - 1) + number).wait()

    @pl.when(jnp.logical_and(step > 1, step < clips))
    def _():
        p_save(PAIRS * (step - 1) - 1).wait()

    @pl.when(step < clips)
    def _():
        projected = dot(x_ref[0], w_proj_ref[...]) + b_proj_ref[...][None, :]
        high, middle, low = split3(projected - mask_ref[...][None, :])
        row = lax.broadcasted_iota(jnp.int32, (LEN, 1), 0)
        onehot = (row == pos_ref[0]).astype(f32).astype(bf16)[:, : x_ref.shape[1]]
        emb_s[...] = (
            (table_ref[...].reshape(LEN, D) + mask_ref[...][None, :])
            + dot(onehot, low)
            + dot(onehot, middle)
        ) + dot(onehot, high)
        for number in range(LEN // STEP):
            at = slice(number * STEP, (number + 1) * STEP)
            value = emb_s[at, :]
            centered = value - lane_mean(value)
            rstd = lax.rsqrt(lane_mean(centered * centered) + 1e-05)
            xhat = centered * rstd
            xhat_s[at, :] = xhat.astype(bf16)
            normed_s[at, :] = (xhat * gain1_ref[...][None, :] + bias1_ref[...][None, :]).astype(
                bf16
            )
            rstd_s[at, :] = rstd
        group = pl.ds(pl.multiple_of(step * rows, 8), rows)
        middle_s[group, :] = emb_s[:rows, :]
        normed = normed_s[...]
        k_s[...] = dot(normed, w_qkv_ref[:, D : 2 * D]).astype(bf16)
        v_s[...] = (dot(normed, w_qkv_ref[:, 2 * D :]) + v_bias_ref[...][None, :]).astype(bf16)
        q_s[...] = (dot(normed[:rows], w_qkv_ref[:, :D]) + q_bias_ref[...][None, :]).astype(bf16)
        for copy in saves(step):
            copy.start()

        def attend(pair, carry):
            number = step * PAIRS + pair
            slot = lax.rem(number, SLOTS)
            at = pl.ds(pl.multiple_of(pair * PAIR, PAIR), PAIR)
            query = q_s[:, at]
            key = k_s[:, at]
            value = jnp.concatenate([v_s[:, at], jnp.ones((LEN, PAIR), bf16)], axis=1)
            parts = []
            for head in range(2):
                scores = dot_rt(jnp.where(own_lanes(head), query, jnp.zeros_like(query)), key)
                largest = jnp.max(scores, axis=1, keepdims=True)
                weights = jnp.exp2(
                    (scores - largest) * (HEAD**-0.5 * np.log2(np.e))
                ).astype(bf16)
                p_s[slot, head] = weights
                parts.append(dot(weights, value))
            first = own_lanes(0)
            inverse = 1.0 / jnp.where(first, parts[0][:, PAIR:], parts[1][:, PAIR:])
            linv_s[group, at] = inverse
            att_s[group, at] = jnp.where(first, parts[0][:, :PAIR], parts[1][:, :PAIR]) * inverse
            p_save(number).start()
            return carry

        lax.fori_loop(0, PAIRS, attend, 0, unroll=UNROLL_F)

    @pl.when(step == 0)
    def _():
        norms_ref[...] = jnp.zeros_like(norms_ref)
        norms_ref[0:1, :] = square_sum(w_proj_ref)
        norms_ref[4:5, :] = square_sum(w_qkv_ref)
        b_fc1_s[...] = b_fc1_ref[...][None, :]

    @pl.when(step == clips)
    def _():
        for copy in loads():
            copy.wait()
        attended_s[...] = att_s[...].astype(bf16)
        gn_s[...] = dot(attended_s[...], w_out_s[...])

        def norm_middle(at, carry):
            middle = middle_s[at, :] + (gn_s[at, :] + b_out_ref[...][None, :])
            centered = middle - lane_mean(middle)
            rstd = lax.rsqrt(lane_mean(centered * centered) + 1e-05)
            xhat = centered * rstd
            xhat2_s[at, :] = xhat
            rstd2_s[at, :] = rstd
            normed2_s[at, :] = (
                xhat * gain2_ref[...][None, :] + bias2_ref[...][None, :]
            ).astype(bf16)
            middle_s[at, :] = middle + b_fc2_ref[...][None, :]
            gn_s[at, :] = jnp.zeros(middle.shape, f32)
            return carry

        row_loop(clips * rows, norm_middle, 0, unroll=2)
        norms_ref[1:2, :] = square_sum(w_out_s)
        norms_ref[2:3, :] = square_sum(w_fc1_s)
        norms_ref[3:4, :] = square_sum(w_fc2_s)
        flat_s[FC_USED - 24 :, :] = jnp.zeros_like(flat_s[FC_USED - 24 :, :])

        def hidden_block(block, carry):
            normed2 = normed2_s[...]
            cot = cot_s[...]
            at = pl.ds(pl.multiple_of(block * BLOCK, BLOCK), BLOCK)
            w_fc1 = w_fc1_s[:, at]
            w_fc2 = w_fc2_s[at, :]
            pre = dot(normed2, w_fc1) + b_fc1_s[:, at]
            cdf = 0.5 + 0.5 * lax.erf(pre * np.float32(0.5**0.5))
            hidden = (pre * cdf).astype(bf16)
            slope = cdf + pre * (
                jnp.exp2(pre * pre * (-0.5 * np.log2(np.e))) * ((2 * np.pi) ** -0.5)
            )
            grad_pre = dot_rt(cot, w_fc2) * slope
            grad_pre_b = grad_pre.astype(bf16)
            middle_s[...] += dot(hidden, w_fc2)
            gn_s[...] += dot_rt(grad_pre_b, w_fc1)
            grad_w2 = dot_lt(hidden, cot).astype(bf16)
            for column in range(D // PAIR):
                first = FF * PAIRS + column * FF + block * BLOCK
                flat_s[pl.ds(pl.multiple_of(first, 16), BLOCK), :] = grad_w2[
                    :, column * PAIR : (column + 1) * PAIR
                ]
            grad_w1 = dot_lt(normed2, grad_pre_b).astype(bf16)
            sums = column_sums(grad_pre_b.astype(f32))
            for piece in range(BLOCK // PAIR):
                lanes = slice(piece * PAIR, (piece + 1) * PAIR)
                number = block * (BLOCK // PAIR) + piece
                flat_s[pl.ds(pl.multiple_of(number * D, 16), D), :] = grad_w1[:, lanes]
                row = 8 * lax.rem(number, PAIRS) + lax.div(number, PAIRS)
                vec_s[pl.ds(row, 1), :] = sums[:, lanes]
            return carry

        lax.fori_loop(0, BLOCKS, hidden_block, 0, unroll=UNROLL_M)
        out_s[...] = middle_s[...].astype(bf16)
        ends = [pltpu.make_async_copy(out_s, out_hbm, end_sems.at[0])]
        ends[0].start()

        def norm_back(at, carry):
            cot_f = cot_s[at, :].astype(f32)
            grad_normed = gn_s[at, :]
            xhat = xhat2_s[at, :]
            scaled = grad_normed * gain2_ref[...][None, :]
            grad_middle = cot_f + rstd2_s[at, :] * (
                scaled - lane_mean(scaled) - xhat * lane_mean(scaled * xhat)
            )
            middle_s[at, :] = grad_middle
            grad_branch = grad_middle.astype(bf16)
            normed2_s[at, :] = grad_branch
            terms = [cot_f, grad_normed * xhat, grad_normed, grad_branch.astype(f32)]
            return tuple(total + column_sums(term) for total, term in zip(carry, terms))

        zero = jnp.zeros((1, D), f32)
        vectors = row_loop(clips * rows, norm_back, (zero,) * 4, unroll=2)
        ends.append(pltpu.make_async_copy(middle_s, gmid_hbm, end_sems.at[1]))
        ends[1].start()
        grad_branch = normed2_s[...]
        grad_out = dot_lt(attended_s[...], grad_branch).astype(bf16)
        for column in range(D // PAIR):
            lanes = slice(column * PAIR, (column + 1) * PAIR)
            first = 2 * FF * PAIRS + column * D
            flat_s[first : first + D, :] = grad_out[:, lanes]
            for number, vector in enumerate(vectors):
                row = 8 * column + 4 + number
                vec_s[row : row + 1, :] = vector[:, lanes]
        flat_s[FC_USED - 24 : FC_USED, :] = vec_s[...].astype(bf16)
        bit = start_ref[1]
        for index, (side, target) in enumerate([(bit, kept_hbm), (1 - bit, sent_hbm)]):
            copy = pltpu.make_async_copy(
                flat_s.at[pl.ds(pl.multiple_of(side * half, 16), half)],
                target,
                end_sems.at[2 + index],
            )
            copy.start()
            ends.append(copy)
        gn_s[...] = dot_rt(grad_branch, w_out_s[...])

        def inner_products(at, carry):
            grad_att = gn_s[at, :].astype(bf16).astype(f32)
            grad_s = (grad_att * linv_s[at, :]).astype(bf16)
            gs_ref[at, :] = grad_s
            product = grad_s.astype(f32) * att_s[at, :]
            lane = lax.broadcasted_iota(jnp.int32, (1, PAIR), 1)
            packed = jnp.zeros((product.shape[0], PAIR), f32)
            for pair in range(PAIRS):
                piece = product[:, pair * PAIR : (pair + 1) * PAIR]
                for head in range(2):
                    inner = -jnp.sum(
                        jnp.where(own_lanes(head), piece, 0.0), axis=1, keepdims=True
                    )
                    for index, term in enumerate(split3(inner)):
                        where = 3 * (2 * pair + head) + index
                        packed = jnp.where(lane == where, term.astype(f32), packed)
            extra_ref[at, :] = packed.astype(bf16)
            return carry

        row_loop(clips * rows, inner_products, 0, unroll=2)
        for copy in ends + saves(clips - 1):
            copy.wait()
        for number in range(PAIRS * clips - PAIRS - 1, PAIRS * clips):
            p_save(number).wait()


def backward_kernel(
    start_ref,
    q_ref,
    k_ref,
    v_ref,
    gs_ref,
    extra_ref,
    x_ref,
    pos_ref,
    w_qkv_ref,
    gain1_ref,
    p_hbm,
    normed_hbm,
    xhat_hbm,
    rstd_hbm,
    gmid_hbm,
    *rest,
    rows,
    base,
    count,
    last,
):
    if last:
        acc_hbm, kept_ref, sent_ref, proj_kept_ref, proj_sent_ref = rest[:5]
        acc_s, total_sem = rest[5:7]
        scratch = rest[7:]
    else:
        acc_s, proj_kept_ref, proj_sent_ref = rest[:3]
        scratch = rest[3:]
    (p_s, normed_s, xhat_s, rstd_s, own_s, dq_s, dkv_s, gn_s, high_s, low_s, proj_s) = scratch[:-2]
    sems, p_sems = scratch[-2:]
    clip = pl.program_id(0)
    lane = lax.broadcasted_iota(jnp.int32, (1, PAIR), 1)

    def loads():
        at = base + clip
        pairs = [
            (normed_hbm.at[at], normed_s),
            (xhat_hbm.at[at], xhat_s),
            (rstd_hbm.at[at], rstd_s),
            (gmid_hbm.at[pl.ds(pl.multiple_of(at * rows, 8), rows)], own_s.at[pl.ds(0, rows)]),
        ]
        return [
            pltpu.make_async_copy(source, target, sems.at[index])
            for index, (source, target) in enumerate(pairs)
        ]

    def p_load(number):
        at = lax.div(number, PAIRS)
        pair = lax.rem(number, PAIRS)
        slot = lax.rem(number, 2 * PAIRS)
        return pltpu.make_async_copy(
            p_hbm.at[base + at, pl.ds(2 * pair, 2)], p_s.at[slot], p_sems.at[slot]
        )

    @pl.when(clip == 0)
    def _():
        for pair in range(PAIRS):
            p_load(pair).start()

    for copy in loads():
        copy.start()

    @pl.when(clip == 0)
    def _():
        own_s[rows:, :] = jnp.zeros_like(own_s[rows:, :])
        if last:
            pltpu.make_async_copy(acc_hbm, acc_s, total_sem).start()
        else:

            def clear(number, carry):
                at = pl.ds(pl.multiple_of(number * 256, 256), 256)
                acc_s[at, :] = jnp.zeros((256, PAIR), f32)
                return carry

            lax.fori_loop(0, acc_s.shape[0] // 256, clear, 0)

    def attend_back(phase, carry):
        number = clip * PAIRS + phase
        slot = lax.rem(number, 2 * PAIRS)
        p_load(number).wait()
        at = pl.ds(pl.multiple_of(phase * PAIR, PAIR), PAIR)
        query = q_ref[0, :, at] * jnp.asarray(HEAD**-0.5, bf16)
        key = k_ref[0, :, at]
        value = jnp.concatenate([v_ref[0, :, at], jnp.ones((LEN, PAIR), bf16)], axis=1)
        grad = gs_ref[:, at]
        extra = extra_ref[...]
        queries, keys, values = [], [], []
        for head in range(2):
            first = 3 * (2 * phase + head)
            inner = jnp.logical_and(lane >= first, lane < first + 3)
            left = jnp.concatenate(
                [
                    jnp.where(own_lanes(head), grad, jnp.zeros_like(grad)),
                    jnp.where(inner, extra, jnp.zeros_like(extra)),
                ],
                axis=1,
            )
            weights = p_s[slot, head]
            grad_scores = (weights.astype(f32) * dot_rt(left, value)).astype(bf16)
            queries.append(dot(grad_scores, key))
            keys.append(dot_lt(grad_scores, query))
            values.append(dot_lt(weights, grad))
        side = own_lanes(0)
        dq_s[:, at] = (jnp.where(side, queries[0], queries[1]) * (HEAD**-0.5)).astype(bf16)
        dkv_s[:, at] = jnp.where(side, keys[0], keys[1]).astype(bf16)
        at = pl.ds(pl.multiple_of(phase * PAIR + D, PAIR), PAIR)
        dkv_s[:, at] = jnp.where(side, values[0], values[1]).astype(bf16)
        return carry

    lax.fori_loop(0, PAIRS, attend_back, 0, unroll=UNROLL_B)

    @pl.when(clip + 1 < count)
    def _():
        for pair in range(PAIRS):
            p_load(PAIRS * (clip + 1) + pair).start()

    for copy in loads():
        copy.wait()
    if last:

        @pl.when(clip == 0)
        def _():
            pltpu.make_async_copy(acc_hbm, acc_s, total_sem).wait()

    if True:

        normed = normed_s[...]
        grad_q = dq_s[...]
        grad_kv = dkv_s[...]
        gn_s[...] = dot_rt(grad_kv, w_qkv_ref[:, D:])
        gn_s[:rows, :] += dot_rt(grad_q, w_qkv_ref[:, :D])
        part_q = dot_lt(normed[:rows], grad_q)
        part_kv = dot_lt(normed, grad_kv)
        for index in range(PAIRS):
            acc_s[index * D : (index + 1) * D, :] += part_q[:, index * PAIR : (index + 1) * PAIR]
        for index in range(2 * PAIRS):
            first = (PAIRS + index) * D
            acc_s[first : first + D, :] += part_kv[:, index * PAIR : (index + 1) * PAIR]
        ones = jnp.ones((8, LEN), bf16)
        sum_q = dot(ones[:, :rows], grad_q)[:1]
        sum_v = dot(ones, grad_kv[:, D:])[:1]

        def norm_rows(number, carry, with_own):
            at = pl.ds(pl.multiple_of(number * STEP, STEP), STEP)
            sum_gain, sum_bias, sum_emb = carry
            value = gn_s[at, :]
            xhat = xhat_s[at, :].astype(f32)
            sum_bias = sum_bias + column_sums(value)
            sum_gain = sum_gain + column_sums(value * xhat)
            scaled = value * gain1_ref[...][None, :]
            grad = rstd_s[at, :] * (
                scaled - lane_mean(scaled) - xhat * lane_mean(scaled * xhat)
            )
            if with_own:
                grad = grad + own_s[at, :]
            sum_emb = sum_emb + column_sums(grad)
            high = grad.astype(bf16)
            high_s[at, :] = high
            low_s[at, :] = (grad - high.astype(f32)).astype(bf16)
            return sum_gain, sum_bias, sum_emb

        zero = jnp.zeros((1, D), f32)
        own_steps = own_s.shape[0] // STEP
        carry = lax.fori_loop(
            0, own_steps, functools.partial(norm_rows, with_own=True), (zero, zero, zero), unroll=True
        )
        sum_gain, sum_bias, sum_emb = lax.fori_loop(
            own_steps, LEN // STEP, functools.partial(norm_rows, with_own=False), carry, unroll=True
        )
        row = lax.broadcasted_iota(jnp.int32, (LEN, 1), 0)
        onehot = (row == pos_ref[0]).astype(f32).astype(bf16)
        grad_proj = dot_lt(onehot, high_s[...]) + dot_lt(onehot, low_s[...])
        proj_s[...] = grad_proj
        bit = start_ref[1]
        part = SLOT // 2
        proj_kept_ref[0] = proj_s[pl.ds(pl.multiple_of(bit * part, 8), part), :]
        proj_sent_ref[0] = proj_s[
            pl.ds(pl.multiple_of((1 - bit) * part, 8), part), :
        ].astype(bf16)
        sum_proj = column_sums(grad_proj)
        vectors = [sum_proj, sum_emb - sum_proj, sum_gain, sum_bias, sum_q, sum_v]
        weight = dot_lt(x_ref[0], grad_proj[: x_ref.shape[1]].astype(bf16))
        for index in range(D // PAIR):
            lanes = slice(index * PAIR, (index + 1) * PAIR)
            first = 3 * PAIRS * D + index * DIN
            acc_s[first : first + DIN, :] += weight[:, lanes]
            first = 3 * PAIRS * D + PAIRS * DIN + 8 * index
            for number, vector in enumerate(vectors):
                acc_s[first + number : first + number + 1, :] += vector[:, lanes]

    if last:

        @pl.when(clip == count - 1)
        def _():
            bit = start_ref[1]
            half = kept_ref.shape[0]

            def hand_over(number, carry):
                at = pl.ds(pl.multiple_of(number * 256, 256), 256)
                kept_at = pl.ds(pl.multiple_of(bit * half + number * 256, 256), 256)
                sent_at = pl.ds(pl.multiple_of((1 - bit) * half + number * 256, 256), 256)
                kept_ref[at, :] = acc_s[kept_at, :]
                sent_ref[at, :] = acc_s[sent_at, :].astype(bf16)
                return carry

            lax.fori_loop(0, half // 256, hand_over, 0)


def place(target, lanes, source, where, total):
    size = target.shape[0]
    step = 96

    def move(number, total):
        first = pl.multiple_of(number * step, 16)
        value = source[pl.ds(pl.multiple_of(where + first, 16), step), :].astype(f32)
        target[pl.ds(first, step), lanes] = value
        return total + jnp.sum((value * value).reshape(step // 8, 8, PAIR), axis=0)

    return lax.fori_loop(0, size // step, move, total, unroll=2)


def lanes_of(index):
    return slice(index * PAIR, (index + 1) * PAIR)


def whole_mean(total, size):
    value = jnp.sum(jnp.sum(total, axis=1, keepdims=True), axis=0, keepdims=True)
    return value / size


def assemble_fc_kernel(
    start_ref,
    mine_hbm,
    other_hbm,
    w_out_ref,
    w_fc1_ref,
    w_fc2_ref,
    b_out_ref,
    gain_ref,
    bias_ref,
    b_fc1_ref,
    b_fc2_ref,
    mean_ref,
    full_s,
    sems,
):
    half = mine_hbm.shape[0]
    bit = start_ref[1]
    copies = [
        pltpu.make_async_copy(
            source, full_s.at[pl.ds(pl.multiple_of(side * half, 16), half)], sems.at[index]
        )
        for index, (source, side) in enumerate([(mine_hbm, bit), (other_hbm, 1 - bit)])
    ]
    for copy in copies:
        copy.start()
    for copy in copies:
        copy.wait()

    total = jnp.zeros((8, PAIR), f32)
    for index in range(PAIRS):
        total = place(w_out_ref, lanes_of(index), full_s, 2 * FF * PAIRS + index * D, total)
    mean_out = whole_mean(total, D * D)
    total = jnp.zeros((8, PAIR), f32)
    for index in range(FF // PAIR):
        total = place(w_fc1_ref, lanes_of(index), full_s, index * D, total)
    mean_fc1 = whole_mean(total, D * FF)
    total = jnp.zeros((8, PAIR), f32)
    for index in range(PAIRS):
        total = place(w_fc2_ref, lanes_of(index), full_s, FF * PAIRS + index * FF, total)
    mean_fc2 = whole_mean(total, FF * D)
    first = 2 * FF * PAIRS + PAIRS * D
    vectors = full_s[first : first + 24, :].astype(f32)
    for index in range(PAIRS):
        lanes = lanes_of(index)
        for number in range(4):
            b_fc1_ref[number * D + index * PAIR : number * D + (index + 1) * PAIR] = vectors[
                8 * index + number
            ]
        for number, target in enumerate([b_fc2_ref, gain_ref, bias_ref, b_out_ref]):
            target[lanes] = vectors[8 * index + 4 + number]
    row = lax.broadcasted_iota(jnp.int32, (8, PAIR), 0)
    mean_ref[...] = jnp.where(
        row == 1, mean_out, jnp.where(row == 2, mean_fc1, mean_fc2)
    )


def assemble_qkv_kernel(
    start_ref,
    *refs,
    far,
    chunk,
):
    planes = refs[:8]
    (
        norms_ref,
        mean_ref,
        w_proj_ref,
        w_qkv_ref,
        b_proj_ref,
        mask_ref,
        gain_ref,
        bias_ref,
        q_bias_ref,
        v_bias_ref,
        trust_ref,
        trust_qkv_ref,
        full_s,
        sems,
    ) = refs[8:]
    half = 4 * far * chunk
    bit = start_ref[1]
    copies = []
    for side in range(2):
        for plane in range(4):
            for line in range(far):
                place_at = jnp.bitwise_xor(start_ref[2], plane * far + line) * chunk
                place_at = place_at + (bit if side == 0 else 1 - bit) * half
                copies.append(
                    pltpu.make_async_copy(
                        planes[4 * side + plane].at[pl.ds(line * chunk, chunk)],
                        full_s.at[pl.ds(pl.multiple_of(place_at, 16), chunk)],
                        sems.at[len(copies)],
                    )
                )
    for copy in copies:
        copy.start()
    for copy in copies:
        copy.wait()

    total = jnp.zeros((8, PAIR), f32)
    for index in range(PAIRS):
        total = place(w_proj_ref, lanes_of(index), full_s, 3 * PAIRS * D + index * DIN, total)
    mean_proj = whole_mean(total, DIN * D)
    total = jnp.zeros((8, PAIR), f32)
    for index in range(3 * PAIRS):
        total = place(w_qkv_ref, lanes_of(index), full_s, index * D, total)
    mean_qkv = whole_mean(total, D * 3 * D)
    first = 3 * PAIRS * D + PAIRS * DIN
    vectors = full_s[first : first + 24, :].astype(f32)
    targets = [b_proj_ref, mask_ref, gain_ref, bias_ref, q_bias_ref, v_bias_ref]
    for index in range(PAIRS):
        for number, target in enumerate(targets):
            target[lanes_of(index)] = vectors[8 * index + number]
    lane = lax.broadcasted_iota(jnp.int32, (1, PAIR), 1)
    means = [mean_proj, mean_ref[1:2], mean_ref[2:3], mean_ref[3:4], mean_qkv]
    sums = jnp.sum(norms_ref[...], axis=1, keepdims=True)
    sizes = [DIN * D, D * D, D * FF, FF * D, D * 3 * D]
    grads = jnp.ones((1, PAIR), f32)
    weights = jnp.ones((1, PAIR), f32)
    for index, (mean, size) in enumerate(zip(means, sizes)):
        grads = jnp.where(lane == index, mean, grads)
        weights = jnp.where(lane == index, sums[index : index + 1] / size, weights)
    ratios = jnp.sqrt(weights) / jnp.sqrt(grads + 1e-06)
    trust_ref[...] = ratios[0, :4]
    trust_qkv_ref[...] = ratios[0, 4:5]


def whole(shape):
    return pl.BlockSpec(shape, lambda i, s: (0,) * len(shape), pipeline_mode=pl.Buffered(1))


def shape_of(shape, dtype):
    return jax.ShapeDtypeStruct(shape, dtype)


def kernel_call(kernel, grid, in_specs, out_specs, out_shape, scratch, name, cost, args):
    return pl.pallas_call(
        kernel,
        grid_spec=pltpu.PrefetchScalarGridSpec(
            num_scalar_prefetch=1,
            grid=grid,
            in_specs=in_specs,
            out_specs=out_specs,
            scratch_shapes=scratch,
        ),
        out_shape=out_shape,
        compiler_params=pltpu.CompilerParams(
            dimension_semantics=("arbitrary",), vmem_limit_bytes=VMEM
        ),
        cost_estimate=pl.CostEstimate(
            flops=cost[0], bytes_accessed=cost[1], transcendentals=cost[2]
        ),
        name=name,
    )(*args)


def run_forward(start, x_vis, padded_pos, table, params, cotangent, rows, half):
    clips, visible, _ = x_vis.shape
    (
        w_proj,
        b_proj,
        mask_token,
        ln1_gain,
        ln1_bias,
        w_qkv,
        q_bias,
        v_bias,
        w_out,
        b_out,
        ln2_gain,
        ln2_bias,
        w_fc1,
        b_fc1,
        w_fc2,
        b_fc2,
    ) = params
    tokens = clips * rows
    any_space = pl.BlockSpec(memory_space=pl.ANY)
    vector = whole((D,))

    def clip_at(i):
        return jnp.minimum(i, clips - 1)

    in_specs = [
        pl.BlockSpec((1, visible, DIN), lambda i, s: (clip_at(i), 0, 0)),
        pl.BlockSpec((1, 1, SLOT), lambda i, s: (clip_at(i), 0, 0)),
        pl.BlockSpec(
            (pl.Element(LEN // 8), pl.Element(8), pl.Element(D)),
            lambda i, s: (s[0], 0, 0),
            pipeline_mode=pl.Buffered(1),
        ),
        whole((DIN, D)),
        vector,
        vector,
        vector,
        vector,
        whole((D, 3 * D)),
        vector,
        vector,
        vector,
        vector,
        vector,
        whole((FF,)),
        vector,
    ] + [any_space] * 4
    out_specs = [whole((tokens, D)), whole((tokens, PAIR)), whole((8, PAIR))] + [any_space] * 11
    out_shape = [
        shape_of((tokens, D), bf16),
        shape_of((tokens, PAIR), bf16),
        shape_of((8, PAIR), f32),
        shape_of((tokens, D), bf16),
        shape_of((tokens, D), f32),
        shape_of((half, PAIR), bf16),
        shape_of((half, PAIR), bf16),
        shape_of((clips, HEADS, rows, LEN), bf16),
        shape_of((clips, rows, D), bf16),
        shape_of((clips, LEN, D), bf16),
        shape_of((clips, LEN, D), bf16),
        shape_of((clips, LEN, D), bf16),
        shape_of((clips, LEN, D), bf16),
        shape_of((clips, LEN, 1), f32),
    ]
    scratch = [
        pltpu.VMEM((SLOTS, 2, rows, LEN), bf16),
        pltpu.VMEM((rows, D), bf16),
        pltpu.VMEM((LEN, D), bf16),
        pltpu.VMEM((LEN, D), bf16),
        pltpu.VMEM((LEN, D), bf16),
        pltpu.VMEM((LEN, D), bf16),
        pltpu.VMEM((LEN, 1), f32),
        pltpu.VMEM((LEN, D), f32),
        pltpu.VMEM((tokens, D), f32),
        pltpu.VMEM((tokens, D), f32),
        pltpu.VMEM((tokens, D), f32),
        pltpu.VMEM((tokens, D), bf16),
        pltpu.VMEM((tokens, D), f32),
        pltpu.VMEM((tokens, 1), f32),
        pltpu.VMEM((tokens, D), bf16),
        pltpu.VMEM((tokens, D), f32),
        pltpu.VMEM((24, PAIR), f32),
        pltpu.VMEM((2 * half, PAIR), bf16),
        pltpu.VMEM((tokens, D), bf16),
        pltpu.VMEM((D, D), bf16),
        pltpu.VMEM((D, FF), bf16),
        pltpu.VMEM((FF, D), bf16),
        pltpu.VMEM((tokens, D), bf16),
        pltpu.VMEM((1, FF), f32),
        pltpu.SemaphoreType.DMA((6,)),
        pltpu.SemaphoreType.DMA((SLOTS,)),
        pltpu.SemaphoreType.DMA((4,)),
        pltpu.SemaphoreType.DMA((4,)),
    ]
    return kernel_call(
        functools.partial(forward_kernel, rows=rows, clips=clips),
        (clips + 1,),
        in_specs,
        out_specs,
        out_shape,
        scratch,
        "forward",
        (40_000_000_000, 60_000_000, 13_000_000),
        (
            start,
            x_vis,
            padded_pos,
            table,
            w_proj,
            b_proj,
            mask_token,
            ln1_gain,
            ln1_bias,
            w_qkv,
            q_bias,
            v_bias,
            b_out,
            ln2_gain,
            ln2_bias,
            b_fc1,
            b_fc2,
            w_out,
            w_fc1,
            w_fc2,
            cotangent.reshape(tokens, D),
        ),
    )


def run_backward(start, saved, x_vis, padded_pos, w_qkv, ln1_gain, rows, half, base, count, acc):
    query, key, value, grads, extra, weights, normed, xhat, rstd, gmid = saved
    _, visible, _ = x_vis.shape
    last = acc is not None
    own_rows = -(-rows // STEP) * STEP
    any_space = pl.BlockSpec(memory_space=pl.ANY)

    def at(i):
        return base + i

    def block(*shape):
        return pl.BlockSpec((1,) + shape, lambda i, s: (at(i),) + (0,) * len(shape))

    proj_spec = pl.BlockSpec((1, SLOT // 2, D), lambda i, s: (i, 0, 0))
    proj_shapes = [
        shape_of((count, SLOT // 2, D), f32),
        shape_of((count, SLOT // 2, D), bf16),
    ]
    in_specs = [
        block(rows, D),
        block(LEN, D),
        block(LEN, D),
        pl.BlockSpec((rows, D), lambda i, s: (at(i), 0)),
        pl.BlockSpec((rows, PAIR), lambda i, s: (at(i), 0)),
        block(visible, DIN),
        block(1, SLOT),
        whole((D, 3 * D)),
        whole((D,)),
    ] + [any_space] * 5
    args = [
        start,
        query,
        key,
        value,
        grads,
        extra,
        x_vis,
        padded_pos,
        w_qkv,
        ln1_gain,
        weights,
        normed,
        xhat,
        rstd,
        gmid,
    ]
    scratch = [
        pltpu.VMEM((2 * PAIRS, 2, rows, LEN), bf16),
        pltpu.VMEM((LEN, D), bf16),
        pltpu.VMEM((LEN, D), bf16),
        pltpu.VMEM((LEN, 1), f32),
        pltpu.VMEM((own_rows, D), f32),
        pltpu.VMEM((rows, D), bf16),
        pltpu.VMEM((LEN, 2 * D), bf16),
        pltpu.VMEM((LEN, D), f32),
        pltpu.VMEM((LEN, D), bf16),
        pltpu.VMEM((LEN, D), bf16),
        pltpu.VMEM((SLOT, D), f32),
        pltpu.SemaphoreType.DMA((4,)),
        pltpu.SemaphoreType.DMA((2 * PAIRS,)),
    ]
    if last:
        in_specs.append(any_space)
        args.append(acc)
        out_specs = [whole((half, PAIR)), whole((half, PAIR)), proj_spec, proj_spec]
        out_shape = [shape_of((half, PAIR), f32), shape_of((half, PAIR), bf16)] + proj_shapes
        scratch = [pltpu.VMEM((2 * half, PAIR), f32), pltpu.SemaphoreType.DMA] + scratch
    else:
        out_specs = [whole((2 * half, PAIR)), proj_spec, proj_spec]
        out_shape = [shape_of((2 * half, PAIR), f32)] + proj_shapes
    return kernel_call(
        functools.partial(backward_kernel, rows=rows, base=base, count=count, last=last),
        (count,),
        in_specs,
        out_specs,
        out_shape,
        scratch,
        "backward",
        (16_000_000_000 * count, 20_000_000 * count, 0),
        tuple(args),
    )


def run_assemble_fc(start, mine, other):
    half = mine.shape[0]
    shapes = [(D, D), (D, FF), (FF, D), (D,), (D,), (D,), (FF,), (D,), (8, PAIR)]
    return kernel_call(
        assemble_fc_kernel,
        (1,),
        [pl.BlockSpec(memory_space=pl.ANY)] * 2,
        [whole(size) for size in shapes],
        [shape_of(size, f32) for size in shapes],
        [pltpu.VMEM((2 * half, PAIR), bf16), pltpu.SemaphoreType.DMA((2,))],
        "assemble_fc",
        (10_000_000, 8_000_000, 0),
        (start, mine, other),
    )


def run_assemble_qkv(start, planes, norms, means, far, chunk):
    any_space = pl.BlockSpec(memory_space=pl.ANY)
    shapes = [(DIN, D), (D, 3 * D), (D,), (D,), (D,), (D,), (D,), (D,), (4,), (1,)]
    return kernel_call(
        functools.partial(assemble_qkv_kernel, far=far, chunk=chunk),
        (1,),
        [any_space] * 8 + [whole((8, PAIR)), whole((8, PAIR))],
        [whole(size) for size in shapes],
        [shape_of(size, f32) for size in shapes],
        [
            pltpu.VMEM((8 * far * chunk, PAIR), bf16),
            pltpu.SemaphoreType.DMA((8 * far,)),
        ],
        "assemble_qkv",
        (10_000_000, 5_000_000, 0),
        (start, *planes, norms, means),
    )


def add_received(kept, received):
    return kept.astype(f32) + received.astype(f32)


def shards(x_vis, vis_pos, *rest):
    params, cotangent = rest[:-1], rest[-1]
    w_proj, ln1_gain, w_qkv = params[0], params[3], params[5]
    seq_size = lax.axis_size("seq")
    clip_size = lax.axis_size("clip")
    groups = seq_size * clip_size // 2
    rows = LEN // seq_size
    clips, visible, _ = x_vis.shape
    far = clip_size // 2
    members = [
        [
            s * clip_size + 2 * high + low
            for s in range(core, seq_size, 2)
            for low in range(2)
            for high in range(far)
        ]
        for core in range(2)
    ]

    def chunk_rows(used):
        return -(-used // (32 * groups)) * 16

    core_pairs = [(s, s ^ 1) for s in range(seq_size)]
    chip_pairs = [(s, s ^ 2) for s in range(seq_size)]

    def across_core(value):
        return lax.ppermute(value, "seq", core_pairs)

    def swap(value):
        chunks = value.reshape(groups, -1, PAIR)
        return lax.all_to_all(chunks, AXES, 0, 0, axis_index_groups=members)

    def total_of(chunks):
        return jnp.sum(chunks.astype(f32), axis=0).astype(bf16)

    def spread(chunk, size):
        return jnp.broadcast_to(chunk[None], (size,) + chunk.shape)

    def across(value, seq_change, low_change, high_change):
        pairs = []
        for s in range(seq_size):
            for c in range(clip_size):
                other = (s ^ (2 * seq_change)) * clip_size + (c ^ (2 * high_change + low_change))
                pairs.append((s * clip_size + c, other))
        return lax.ppermute(value, AXES, pairs)

    def gather(chunk):
        size = 1
        while size < far:
            count = min(4, far // size)
            chunk = jnp.concatenate(
                [chunk] + [across(chunk, 0, 0, size * k) for k in range(1, count)]
            )
            size *= count
        return [chunk] + [across(chunk, k >> 1, k & 1, 0) for k in (1, 2, 3)]

    fc_chunk = chunk_rows(FC_USED)
    qkv_chunk = chunk_rows(QKV_USED)
    qkv_half = qkv_chunk * groups
    seq_index = lax.axis_index("seq")
    bit = seq_index & 1
    first = seq_index * rows
    local_pos = jnp.where(vis_pos >= first, vis_pos - first, vis_pos - first + LEN)
    padded_pos = jnp.pad(local_pos, ((0, 0), (0, SLOT - visible)), constant_values=-1)[:, None, :]
    table = sinusoid_table(LEN, D)
    table = jnp.asarray(np.concatenate([table, table[: LEN - rows]]).reshape(-1, 8, D))
    clip_index = lax.axis_index("clip")
    number = ((seq_index >> 1) * 2 + (clip_index & 1)) * far + (clip_index >> 1)
    start = jnp.stack([first // 8, bit, number]).astype(jnp.int32)

    (
        grads,
        extra,
        norms,
        output,
        gmid,
        kept,
        sent,
        weights,
        query,
        key,
        value,
        normed,
        xhat,
        rstd,
    ) = run_forward(start, x_vis, padded_pos, table, params, cotangent, rows, fc_chunk * groups)
    fc = add_received(kept, across_core(sent)).astype(bf16)
    fc, query = lax.optimization_barrier((fc, query))
    fc = swap(fc)
    saved = (query, key, value, grads, extra, weights, normed, xhat, rstd, gmid)
    acc, proj_kept0, proj_sent0 = run_backward(
        start, saved, x_vis, padded_pos, w_qkv, ln1_gain, rows, qkv_half, 0, clips - 1, None
    )
    fc, acc = lax.optimization_barrier((spread(total_of(fc), groups), acc))
    fc = swap(fc).reshape(groups * fc_chunk, PAIR)
    kept, sent, proj_kept1, proj_sent1 = run_backward(
        start, saved, x_vis, padded_pos, w_qkv, ln1_gain, rows, qkv_half, clips - 1, 1, acc
    )
    qkv = add_received(kept, across_core(sent)).astype(bf16)
    fc, qkv = lax.optimization_barrier((fc, qkv))
    qkv = swap(qkv)
    w_out_g, w_fc1_g, w_fc2_g, b_out_g, gain2_g, bias2_g, b_fc1_g, b_fc2_g, means = (
        run_assemble_fc(start, fc, across_core(fc))
    )
    qkv, means = lax.optimization_barrier((total_of(qkv), means))
    planes = gather(qkv)
    planes += [across_core(plane) for plane in planes]
    proj_kept = jnp.concatenate([proj_kept0, proj_kept1])
    proj_sent = jnp.concatenate([proj_sent0, proj_sent1])
    part = add_received(proj_kept, across_core(proj_sent)).astype(bf16)
    part = add_received(part, lax.ppermute(part, "seq", chip_pairs)).astype(bf16)
    other = across_core(part)
    grad_projected = jnp.where(
        bit == 0,
        jnp.concatenate([part, other], axis=1),
        jnp.concatenate([other, part], axis=1),
    )[:, :visible]
    grad_x = lax.dot_general(
        grad_projected, w_proj, (((2,), (1,)), ((), ())), preferred_element_type=f32
    )
    (
        w_proj_g,
        w_qkv_g,
        b_proj_g,
        mask_g,
        gain1_g,
        bias1_g,
        q_bias_g,
        v_bias_g,
        trust,
        trust_qkv,
    ) = run_assemble_qkv(start, planes, norms, means, far, qkv_chunk)
    return (
        output.reshape(clips, rows, D),
        grad_x,
        w_proj_g,
        b_proj_g,
        mask_g,
        gain1_g,
        bias1_g,
        w_qkv_g,
        q_bias_g,
        v_bias_g,
        w_out_g,
        b_out_g,
        gain2_g,
        bias2_g,
        w_fc1_g,
        b_fc1_g,
        w_fc2_g,
        b_fc2_g,
        trust,
        trust_qkv,
    )


def solution(mesh):
    return jax.shard_map(
        shards,
        mesh=mesh,
        in_specs=(P("clip", None, None), P("clip", None))
        + (P(),) * 16
        + (P("clip", "seq", None),),
        out_specs=(P("clip", "seq", None), P("clip", None, None)) + (P(),) * 18,
        check_vma=False,
    )
```

```python
import functools

import jax
import jax.numpy as jnp
import numpy as np
from jax import lax
from jax.experimental import pallas as pl
from jax.experimental.pallas import tpu as pltpu
from jax.sharding import PartitionSpec as P

D = 384
HEADS = 6
HEAD = 64
PAIRS = 3
PAIR = 128
FF = 1536
DIN = 768
SLOT = 160
LEN = 1568
STEP = 112
BLOCK = 256
BLOCKS = FF // BLOCK
SLOTS = 4
UNROLL_F = False
UNROLL_M = False
FC_USED = 10392
QKV_USED = 5784
AXES = ("seq", "clip")
VMEM = 60 * 1024 * 1024

bf16 = jnp.bfloat16
f32 = jnp.float32


def dot(left, right):
    return lax.dot_general(
        left, right, (((1,), (0,)), ((), ())), preferred_element_type=f32
    )


def dot_rt(left, right):
    return lax.dot_general(
        left, right, (((1,), (1,)), ((), ())), preferred_element_type=f32
    )


def dot_lt(left, right):
    return lax.dot_general(
        left, right, (((0,), (0,)), ((), ())), preferred_element_type=f32
    )


def split3(value):
    high = value.astype(bf16)
    rest = value - high.astype(f32)
    middle = rest.astype(bf16)
    low = (rest - middle.astype(f32)).astype(bf16)
    return high, middle, low


def sinusoid_table(length, columns):
    positions = np.arange(length, dtype=np.float64)[:, None]
    column = np.arange(columns)
    angles = positions / np.power(10000.0, (2 * (column // 2)) / columns)[None, :]
    return np.where((column % 2)[None, :] == 0, np.sin(angles), np.cos(angles)).astype(np.float32)


def row_loop(total, body, carry, unroll=False):
    full = total // STEP

    def at_step(number, carry):
        return body(pl.ds(pl.multiple_of(number * STEP, STEP), STEP), carry)

    carry = lax.fori_loop(0, full, at_step, carry, unroll=unroll)
    if total % STEP:
        carry = body(pl.ds(full * STEP, total % STEP), carry)
    return carry


def own_lanes(head):
    lane = lax.broadcasted_iota(jnp.int32, (1, PAIR), 1)
    return (lane < HEAD) if head == 0 else (lane >= HEAD)


def column_sums(value):
    return jnp.sum(value, axis=0, keepdims=True)


def square_sum(ref):
    rows, columns = ref.shape
    size = 64

    def add(number, total):
        piece = ref[pl.ds(pl.multiple_of(number * size, size), size), :].astype(f32)
        sums = column_sums(piece * piece)
        for first in range(0, columns, PAIR):
            total = total + sums[:, first : first + PAIR]
        return total

    return lax.fori_loop(0, rows // size, add, jnp.zeros((1, PAIR), f32))


def lane_mean(value):
    return jnp.mean(value, axis=1, keepdims=True)


def forward_kernel(
    start_ref,
    x_ref,
    pos_ref,
    table_ref,
    w_proj_ref,
    b_proj_ref,
    mask_ref,
    gain1_ref,
    bias1_ref,
    w_qkv_ref,
    q_bias_ref,
    v_bias_ref,
    b_out_ref,
    gain2_ref,
    bias2_ref,
    b_fc1_ref,
    b_fc2_ref,
    w_out_hbm,
    w_fc1_hbm,
    w_fc2_hbm,
    cot_hbm,
    gs_ref,
    extra_ref,
    norms_ref,
    out_hbm,
    gmid_hbm,
    kept_hbm,
    sent_hbm,
    p_hbm,
    q_hbm,
    k_hbm,
    v_hbm,
    normed_hbm,
    xhat_hbm,
    rstd_hbm,
    p_s,
    q_s,
    k_s,
    v_s,
    normed_s,
    xhat_s,
    rstd_s,
    emb_s,
    middle_s,
    att_s,
    linv_s,
    attended_s,
    xhat2_s,
    rstd2_s,
    normed2_s,
    gn_s,
    vec_s,
    flat_s,
    out_s,
    w_out_s,
    w_fc1_s,
    w_fc2_s,
    cot_s,
    b_fc1_s,
    save_sems,
    p_sems,
    load_sems,
    end_sems,
    *,
    rows,
    clips,
):
    step = pl.program_id(0)
    half = kept_hbm.shape[0]

    def loads():
        pairs = [
            (w_out_hbm, w_out_s),
            (w_fc1_hbm, w_fc1_s),
            (w_fc2_hbm, w_fc2_s),
            (cot_hbm, cot_s),
        ]
        return [
            pltpu.make_async_copy(source, target, load_sems.at[index])
            for index, (source, target) in enumerate(pairs)
        ]

    def saves(number):
        pairs = [
            (q_s, q_hbm),
            (k_s, k_hbm),
            (v_s, v_hbm),
            (normed_s, normed_hbm),
            (xhat_s, xhat_hbm),
            (rstd_s, rstd_hbm),
        ]
        return [
            pltpu.make_async_copy(source, target.at[number], save_sems.at[index])
            for index, (source, target) in enumerate(pairs)
        ]

    def p_save(number):
        slot = lax.rem(number, SLOTS)
        at = lax.div(number, PAIRS)
        pair = lax.rem(number, PAIRS)
        return pltpu.make_async_copy(
            p_s.at[slot], p_hbm.at[at, pl.ds(2 * pair, 2)], p_sems.at[slot]
        )

    @pl.when(step == 0)
    def _():
        for copy in loads():
            copy.start()

    @pl.when(jnp.logical_and(step > 0, step < clips))
    def _():
        for copy in saves(step - 1):
            copy.wait()
        for number in range(PAIRS - 1):
            p_save(PAIRS * (step - 1) + number).wait()

    @pl.when(jnp.logical_and(step > 1, step < clips))
    def _():
        p_save(PAIRS * (step - 1) - 1).wait()

    @pl.when(step < clips)
    def _():
        projected = dot(x_ref[0], w_proj_ref[...]) + b_proj_ref[...][None, :]
        high, middle, low = split3(projected - mask_ref[...][None, :])
        row = lax.broadcasted_iota(jnp.int32, (LEN, 1), 0)
        onehot = (row == pos_ref[0]).astype(f32).astype(bf16)[:, : x_ref.shape[1]]
        emb_s[...] = (
            (table_ref[...].reshape(LEN, D) + mask_ref[...][None, :])
            + dot(onehot, low)
            + dot(onehot, middle)
        ) + dot(onehot, high)
        for number in range(LEN // STEP):
            at = slice(number * STEP, (number + 1) * STEP)
            value = emb_s[at, :]
            centered = value - lane_mean(value)
            rstd = lax.rsqrt(lane_mean(centered * centered) + 1e-05)
            xhat = centered * rstd
            xhat_s[at, :] = xhat.astype(bf16)
            normed_s[at, :] = (xhat * gain1_ref[...][None, :] + bias1_ref[...][None, :]).astype(
                bf16
            )
            rstd_s[at, :] = rstd
        group = pl.ds(pl.multiple_of(step * rows, 8), rows)
        middle_s[group, :] = emb_s[:rows, :]
        normed = normed_s[...]
        k_s[...] = dot(normed, w_qkv_ref[:, D : 2 * D]).astype(bf16)
        v_s[...] = (dot(normed, w_qkv_ref[:, 2 * D :]) + v_bias_ref[...][None, :]).astype(bf16)
        q_s[...] = (dot(normed[:rows], w_qkv_ref[:, :D]) + q_bias_ref[...][None, :]).astype(bf16)
        for copy in saves(step):
            copy.start()

        def attend(pair, carry):
            number = step * PAIRS + pair
            slot = lax.rem(number, SLOTS)
            at = pl.ds(pl.multiple_of(pair * PAIR, PAIR), PAIR)
            query = q_s[:, at]
            key = k_s[:, at]
            value = jnp.concatenate([v_s[:, at], jnp.ones((LEN, PAIR), bf16)], axis=1)
            first = own_lanes(0)
            none = jnp.zeros_like(query)
            both = [
                dot_rt(jnp.where(first, query, none), key),
                dot_rt(jnp.where(first, none, query), key),
            ]
            weights = []
            for head, scores in enumerate(both):
                largest = jnp.max(scores, axis=1, keepdims=True)
                scaled = (scores - largest) * (HEAD**-0.5 * np.log2(np.e))
                weights.append(jnp.exp2(scaled).astype(bf16))
                p_s[slot, head] = weights[head]
            parts = [dot(weight, value) for weight in weights]
            inverse = 1.0 / jnp.where(first, parts[0][:, PAIR:], parts[1][:, PAIR:])
            linv_s[group, at] = inverse
            att_s[group, at] = jnp.where(first, parts[0][:, :PAIR], parts[1][:, :PAIR]) * inverse
            p_save(number).start()
            return carry

        lax.fori_loop(0, PAIRS, attend, 0, unroll=UNROLL_F)

    @pl.when(step == 0)
    def _():
        norms_ref[...] = jnp.zeros_like(norms_ref)
        norms_ref[0:1, :] = square_sum(w_proj_ref)
        norms_ref[4:5, :] = square_sum(w_qkv_ref)
        b_fc1_s[...] = b_fc1_ref[...][None, :]

    @pl.when(step == clips)
    def _():
        for copy in loads():
            copy.wait()
        attended_s[...] = att_s[...].astype(bf16)
        gn_s[...] = dot(attended_s[...], w_out_s[...])

        def norm_middle(at, carry):
            middle = middle_s[at, :] + (gn_s[at, :] + b_out_ref[...][None, :])
            centered = middle - lane_mean(middle)
            rstd = lax.rsqrt(lane_mean(centered * centered) + 1e-05)
            xhat = centered * rstd
            xhat2_s[at, :] = xhat
            rstd2_s[at, :] = rstd
            normed2_s[at, :] = (
                xhat * gain2_ref[...][None, :] + bias2_ref[...][None, :]
            ).astype(bf16)
            middle_s[at, :] = middle + b_fc2_ref[...][None, :]
            gn_s[at, :] = jnp.zeros(middle.shape, f32)
            return carry

        row_loop(clips * rows, norm_middle, 0, unroll=True)
        norms_ref[1:2, :] = square_sum(w_out_s)
        norms_ref[2:3, :] = square_sum(w_fc1_s)
        norms_ref[3:4, :] = square_sum(w_fc2_s)
        flat_s[FC_USED - 24 :, :] = jnp.zeros_like(flat_s[FC_USED - 24 :, :])

        def hidden_block(block, carry):
            normed2 = normed2_s[...]
            cot = cot_s[...]
            at = pl.ds(pl.multiple_of(block * BLOCK, BLOCK), BLOCK)
            w_fc1 = w_fc1_s[:, at]
            w_fc2 = w_fc2_s[at, :]
            pre = dot(normed2, w_fc1) + b_fc1_s[:, at]
            grad_hidden = dot_rt(cot, w_fc2)
            cdf = 0.5 + 0.5 * lax.erf(pre * np.float32(0.5**0.5))
            hidden = (pre * cdf).astype(bf16)
            slope = cdf + pre * (
                jnp.exp2(pre * pre * (-0.5 * np.log2(np.e))) * ((2 * np.pi) ** -0.5)
            )
            grad_pre = grad_hidden * slope
            grad_pre_b = grad_pre.astype(bf16)
            middle_s[...] += dot(hidden, w_fc2)
            gn_s[...] += dot_rt(grad_pre_b, w_fc1)
            grad_w2 = dot_lt(hidden, cot).astype(bf16)
            for column in range(D // PAIR):
                first = FF * PAIRS + column * FF + block * BLOCK
                flat_s[pl.ds(pl.multiple_of(first, 16), BLOCK), :] = grad_w2[
                    :, column * PAIR : (column + 1) * PAIR
                ]
            grad_w1 = dot_lt(normed2, grad_pre_b).astype(bf16)
            sums = column_sums(grad_pre_b.astype(f32))
            for piece in range(BLOCK // PAIR):
                lanes = slice(piece * PAIR, (piece + 1) * PAIR)
                number = block * (BLOCK // PAIR) + piece
                flat_s[pl.ds(pl.multiple_of(number * D, 16), D), :] = grad_w1[:, lanes]
                row = 8 * lax.rem(number, PAIRS) + lax.div(number, PAIRS)
                vec_s[pl.ds(row, 1), :] = sums[:, lanes]
            return carry

        lax.fori_loop(0, BLOCKS, hidden_block, 0, unroll=UNROLL_M)
        out_s[...] = middle_s[...].astype(bf16)
        ends = [pltpu.make_async_copy(out_s, out_hbm, end_sems.at[0])]
        ends[0].start()

        def norm_back(at, carry):
            cot_f = cot_s[at, :].astype(f32)
            grad_normed = gn_s[at, :]
            xhat = xhat2_s[at, :]
            scaled = grad_normed * gain2_ref[...][None, :]
            grad_middle = cot_f + rstd2_s[at, :] * (
                scaled - lane_mean(scaled) - xhat * lane_mean(scaled * xhat)
            )
            middle_s[at, :] = grad_middle
            grad_branch = grad_middle.astype(bf16)
            normed2_s[at, :] = grad_branch
            terms = [cot_f, grad_normed * xhat, grad_normed, grad_branch.astype(f32)]
            return tuple(total + column_sums(term) for total, term in zip(carry, terms))

        zero = jnp.zeros((1, D), f32)
        vectors = row_loop(clips * rows, norm_back, (zero,) * 4, unroll=True)
        ends.append(pltpu.make_async_copy(middle_s, gmid_hbm, end_sems.at[1]))
        ends[1].start()
        grad_branch = normed2_s[...]
        grad_out = dot_lt(attended_s[...], grad_branch).astype(bf16)
        for column in range(D // PAIR):
            lanes = slice(column * PAIR, (column + 1) * PAIR)
            first = 2 * FF * PAIRS + column * D
            flat_s[first : first + D, :] = grad_out[:, lanes]
            for number, vector in enumerate(vectors):
                row = 8 * column + 4 + number
                vec_s[row : row + 1, :] = vector[:, lanes]
        flat_s[FC_USED - 24 : FC_USED, :] = vec_s[...].astype(bf16)
        bit = start_ref[1]
        for index, (side, target) in enumerate([(bit, kept_hbm), (1 - bit, sent_hbm)]):
            copy = pltpu.make_async_copy(
                flat_s.at[pl.ds(pl.multiple_of(side * half, 16), half)],
                target,
                end_sems.at[2 + index],
            )
            copy.start()
            ends.append(copy)
        gn_s[...] = dot_rt(grad_branch, w_out_s[...])

        def inner_products(at, carry):
            grad_att = gn_s[at, :].astype(bf16).astype(f32)
            grad_s = (grad_att * linv_s[at, :]).astype(bf16)
            gs_ref[at, :] = grad_s
            product = grad_s.astype(f32) * att_s[at, :]
            lane = lax.broadcasted_iota(jnp.int32, (1, PAIR), 1)
            packed = jnp.zeros((product.shape[0], PAIR), f32)
            for pair in range(PAIRS):
                piece = product[:, pair * PAIR : (pair + 1) * PAIR]
                for head in range(2):
                    inner = -jnp.sum(
                        jnp.where(own_lanes(head), piece, 0.0), axis=1, keepdims=True
                    )
                    for index, term in enumerate(split3(inner)):
                        where = 3 * (2 * pair + head) + index
                        packed = jnp.where(lane == where, term.astype(f32), packed)
            extra_ref[at, :] = packed.astype(bf16)
            return carry

        row_loop(clips * rows, inner_products, 0, unroll=True)
        for copy in ends + saves(clips - 1):
            copy.wait()
        for number in range(PAIRS * clips - PAIRS - 1, PAIRS * clips):
            p_save(number).wait()


def backward_kernel(
    start_ref,
    q_ref,
    k_ref,
    v_ref,
    gs_ref,
    extra_ref,
    pos_ref,
    gain1_ref,
    w_qkv_hbm,
    x_hbm,
    p_hbm,
    normed_hbm,
    xhat_hbm,
    rstd_hbm,
    gmid_hbm,
    *rest,
    rows,
    base,
    count,
    last,
):
    if last:
        acc_hbm, dq_hbm, dkv_hbm, kept_ref, sent_ref, proj_kept_ref, proj_sent_ref = rest[:7]
        scratch = rest[7:]
    else:
        proj_kept_ref, proj_sent_ref, acc_hbm, dq_hbm, dkv_hbm = rest[:5]
        scratch = rest[5:]
    (p_s, normed_s, xhat_s, rstd_s, own_s, dq_s, dkv_s, gn_s, high_s, low_s, proj_s) = scratch[:-7]
    w_qkv_s, x_s, acc_s, hand_sems, w_sem, sems, p_sems = scratch[-7:]
    step = pl.program_id(0)
    lane = lax.broadcasted_iota(jnp.int32, (1, PAIR), 1)
    first_post = base - 1 if last else base

    def loads():
        at = first_post + step
        pairs = [
            (normed_hbm.at[at], normed_s),
            (xhat_hbm.at[at], xhat_s),
            (rstd_hbm.at[at], rstd_s),
            (x_hbm.at[at], x_s),
            (gmid_hbm.at[pl.ds(pl.multiple_of(at * rows, 8), rows)], own_s.at[pl.ds(0, rows)]),
        ]
        return [
            pltpu.make_async_copy(source, target, sems.at[index])
            for index, (source, target) in enumerate(pairs)
        ]

    def hand(number):
        pairs = [(acc_s, acc_hbm), (dq_s, dq_hbm), (dkv_s, dkv_hbm)]
        inside, outside = pairs[number]
        if last:
            return pltpu.make_async_copy(outside, inside, hand_sems.at[number])
        return pltpu.make_async_copy(inside, outside, hand_sems.at[number])

    def p_load(number):
        at = lax.div(number, PAIRS)
        pair = lax.rem(number, PAIRS)
        slot = lax.rem(number, 2 * PAIRS)
        return pltpu.make_async_copy(
            p_hbm.at[base + at, pl.ds(2 * pair, 2)], p_s.at[slot], p_sems.at[slot]
        )

    w_load = pltpu.make_async_copy(w_qkv_hbm, w_qkv_s, w_sem)
    has_post = True if last else step < count - 1

    if last:
        for number in (2, 1):
            pl.when(step == 0)(hand(number).start)

    @pl.when(step == 0)
    def _():
        if not last:
            for pair in range(PAIRS):
                p_load(pair).start()
        w_load.start()

    @pl.when(has_post)
    def _():
        for copy in loads():
            copy.start()

    @pl.when(step == 0)
    def _():
        own_s[rows:, :] = jnp.zeros_like(own_s[rows:, :])
        if last:
            hand(0).start()
            for pair in range(PAIRS):
                p_load(pair).start()
        else:

            def clear(number, carry):
                at = pl.ds(pl.multiple_of(number * 256, 256), 256)
                acc_s[at, :] = jnp.zeros((256, PAIR), f32)
                return carry

            lax.fori_loop(0, acc_s.shape[0] // 256, clear, 0)

    def attend_back(phase, carry):
        number = phase if last else step * PAIRS + phase
        slot = lax.rem(number, 2 * PAIRS)
        p_load(number).wait()
        at = pl.ds(pl.multiple_of(phase * PAIR, PAIR), PAIR)
        query = q_ref[0, :, at] * jnp.asarray(HEAD**-0.5, bf16)
        key = k_ref[0, :, at]
        value = jnp.concatenate([v_ref[0, :, at], jnp.ones((LEN, PAIR), bf16)], axis=1)
        grad = gs_ref[:, at]
        extra = extra_ref[...]
        products = []
        for head in range(2):
            first = 3 * (2 * phase + head)
            inner = jnp.logical_and(lane >= first, lane < first + 3)
            left = jnp.concatenate(
                [
                    jnp.where(own_lanes(head), grad, jnp.zeros_like(grad)),
                    jnp.where(inner, extra, jnp.zeros_like(extra)),
                ],
                axis=1,
            )
            products.append(dot_rt(left, value))
        weights = [p_s[slot, head] for head in range(2)]
        scores = [
            (weight.astype(f32) * product).astype(bf16)
            for weight, product in zip(weights, products)
        ]
        values = [dot_lt(weight, grad) for weight in weights]
        keys = [dot_lt(score, query) for score in scores]
        queries = [dot(score, key) for score in scores]
        side = own_lanes(0)
        dq_s[:, at] = (jnp.where(side, queries[0], queries[1]) * (HEAD**-0.5)).astype(bf16)
        dkv_s[:, at] = jnp.where(side, keys[0], keys[1]).astype(bf16)
        at = pl.ds(pl.multiple_of(phase * PAIR + D, PAIR), PAIR)
        dkv_s[:, at] = jnp.where(side, values[0], values[1]).astype(bf16)
        return carry

    if last:

        @pl.when(step == 1)
        def _():
            lax.fori_loop(0, PAIRS, attend_back, 0)

    else:
        lax.fori_loop(0, PAIRS, attend_back, 0)

        @pl.when(step + 1 < count)
        def _():
            for pair in range(PAIRS):
                p_load(PAIRS * (step + 1) + pair).start()

    @pl.when(step == 0)
    def _():
        w_load.wait()
        if last:
            for number in range(3):
                hand(number).wait()

    @pl.when(has_post)
    def _():
        for copy in loads():
            copy.wait()
        normed = normed_s[...]
        grad_q = dq_s[...]
        grad_kv = dkv_s[...]
        gn_s[...] = dot_rt(grad_kv, w_qkv_s[:, D:])
        gn_s[:rows, :] += dot_rt(grad_q, w_qkv_s[:, :D])
        part_q = dot_lt(normed[:rows], grad_q)
        part_kv = dot_lt(normed, grad_kv)
        for index in range(PAIRS):
            acc_s[index * D : (index + 1) * D, :] += part_q[:, index * PAIR : (index + 1) * PAIR]
        for index in range(2 * PAIRS):
            first = (PAIRS + index) * D
            acc_s[first : first + D, :] += part_kv[:, index * PAIR : (index + 1) * PAIR]
        ones = jnp.ones((8, LEN), bf16)
        sum_q = dot(ones[:, :rows], grad_q)[:1]
        sum_v = dot(ones, grad_kv[:, D:])[:1]

        def norm_rows(number, carry, with_own):
            at = pl.ds(pl.multiple_of(number * STEP, STEP), STEP)
            sum_gain, sum_bias, sum_emb = carry
            value = gn_s[at, :]
            xhat = xhat_s[at, :].astype(f32)
            sum_bias = sum_bias + column_sums(value)
            sum_gain = sum_gain + column_sums(value * xhat)
            scaled = value * gain1_ref[...][None, :]
            grad = rstd_s[at, :] * (
                scaled - lane_mean(scaled) - xhat * lane_mean(scaled * xhat)
            )
            if with_own:
                grad = grad + own_s[at, :]
            sum_emb = sum_emb + column_sums(grad)
            high = grad.astype(bf16)
            high_s[at, :] = high
            low_s[at, :] = (grad - high.astype(f32)).astype(bf16)
            return sum_gain, sum_bias, sum_emb

        zero = jnp.zeros((1, D), f32)
        own_steps = own_s.shape[0] // STEP
        carry = lax.fori_loop(
            0, own_steps, functools.partial(norm_rows, with_own=True), (zero, zero, zero), unroll=True
        )
        sum_gain, sum_bias, sum_emb = lax.fori_loop(
            own_steps, LEN // STEP, functools.partial(norm_rows, with_own=False), carry, unroll=True
        )
        row = lax.broadcasted_iota(jnp.int32, (LEN, 1), 0)
        onehot = (row == pos_ref[0]).astype(f32).astype(bf16)
        grad_proj = dot_lt(onehot, high_s[...]) + dot_lt(onehot, low_s[...])
        proj_s[...] = grad_proj
        bit = start_ref[1]
        part = SLOT // 2
        proj_kept_ref[0] = proj_s[pl.ds(pl.multiple_of(bit * part, 8), part), :]
        proj_sent_ref[0] = proj_s[
            pl.ds(pl.multiple_of((1 - bit) * part, 8), part), :
        ].astype(bf16)
        sum_proj = column_sums(grad_proj)
        vectors = [sum_proj, sum_emb - sum_proj, sum_gain, sum_bias, sum_q, sum_v]
        weight = dot_lt(x_s[...], grad_proj[: x_s.shape[0]].astype(bf16))
        for index in range(D // PAIR):
            lanes = slice(index * PAIR, (index + 1) * PAIR)
            first = 3 * PAIRS * D + index * DIN
            acc_s[first : first + DIN, :] += weight[:, lanes]
            first = 3 * PAIRS * D + PAIRS * DIN + 8 * index
            for number, vector in enumerate(vectors):
                acc_s[first + number : first + number + 1, :] += vector[:, lanes]

    if last:

        @pl.when(step == 1)
        def _():
            bit = start_ref[1]
            half = kept_ref.shape[0]

            def hand_over(number, carry):
                at = pl.ds(pl.multiple_of(number * 256, 256), 256)
                kept_at = pl.ds(pl.multiple_of(bit * half + number * 256, 256), 256)
                sent_at = pl.ds(pl.multiple_of((1 - bit) * half + number * 256, 256), 256)
                kept_ref[at, :] = acc_s[kept_at, :]
                sent_ref[at, :] = acc_s[sent_at, :].astype(bf16)
                return carry

            lax.fori_loop(0, half // 256, hand_over, 0)

    else:
        pl.when(step == count - 2)(hand(0).start)

        @pl.when(step == count - 1)
        def _():
            hand(1).start()
            hand(2).start()
            for number in range(3):
                hand(number).wait()


def place(target, lanes, source, where, total):
    size = target.shape[0]
    step = 96

    def move(number, total):
        first = pl.multiple_of(number * step, 16)
        value = source[pl.ds(pl.multiple_of(where + first, 16), step), :].astype(f32)
        target[pl.ds(first, step), lanes] = value
        return total + jnp.sum((value * value).reshape(step // 8, 8, PAIR), axis=0)

    return lax.fori_loop(0, size // step, move, total, unroll=2)


def lanes_of(index):
    return slice(index * PAIR, (index + 1) * PAIR)


def whole_mean(total, size):
    value = jnp.sum(jnp.sum(total, axis=1, keepdims=True), axis=0, keepdims=True)
    return value / size


def assemble_fc_kernel(
    start_ref,
    mine_hbm,
    other_hbm,
    w_out_ref,
    w_fc1_ref,
    w_fc2_ref,
    b_out_ref,
    gain_ref,
    bias_ref,
    b_fc1_ref,
    b_fc2_ref,
    mean_ref,
    full_s,
    sems,
):
    half = mine_hbm.shape[0]
    bit = start_ref[1]
    copies = [
        pltpu.make_async_copy(
            source, full_s.at[pl.ds(pl.multiple_of(side * half, 16), half)], sems.at[index]
        )
        for index, (source, side) in enumerate([(mine_hbm, bit), (other_hbm, 1 - bit)])
    ]
    for copy in copies:
        copy.start()
    for copy in copies:
        copy.wait()

    total = jnp.zeros((8, PAIR), f32)
    for index in range(PAIRS):
        total = place(w_out_ref, lanes_of(index), full_s, 2 * FF * PAIRS + index * D, total)
    mean_out = whole_mean(total, D * D)
    total = jnp.zeros((8, PAIR), f32)
    for index in range(FF // PAIR):
        total = place(w_fc1_ref, lanes_of(index), full_s, index * D, total)
    mean_fc1 = whole_mean(total, D * FF)
    total = jnp.zeros((8, PAIR), f32)
    for index in range(PAIRS):
        total = place(w_fc2_ref, lanes_of(index), full_s, FF * PAIRS + index * FF, total)
    mean_fc2 = whole_mean(total, FF * D)
    first = 2 * FF * PAIRS + PAIRS * D
    vectors = full_s[first : first + 24, :].astype(f32)
    for index in range(PAIRS):
        lanes = lanes_of(index)
        for number in range(4):
            b_fc1_ref[number * D + index * PAIR : number * D + (index + 1) * PAIR] = vectors[
                8 * index + number
            ]
        for number, target in enumerate([b_fc2_ref, gain_ref, bias_ref, b_out_ref]):
            target[lanes] = vectors[8 * index + 4 + number]
    row = lax.broadcasted_iota(jnp.int32, (8, PAIR), 0)
    mean_ref[...] = jnp.where(
        row == 1, mean_out, jnp.where(row == 2, mean_fc1, mean_fc2)
    )


def assemble_qkv_kernel(
    start_ref,
    *refs,
    far,
    chunk,
):
    planes = refs[:8]
    (
        norms_ref,
        mean_ref,
        w_proj_ref,
        w_qkv_ref,
        b_proj_ref,
        mask_ref,
        gain_ref,
        bias_ref,
        q_bias_ref,
        v_bias_ref,
        trust_ref,
        trust_qkv_ref,
        full_s,
        sems,
    ) = refs[8:]
    half = 4 * far * chunk
    bit = start_ref[1]
    copies = []
    for side in range(2):
        for plane in range(4):
            for line in range(far):
                place_at = jnp.bitwise_xor(start_ref[2], plane * far + line) * chunk
                place_at = place_at + (bit if side == 0 else 1 - bit) * half
                copies.append(
                    pltpu.make_async_copy(
                        planes[4 * side + plane].at[pl.ds(line * chunk, chunk)],
                        full_s.at[pl.ds(pl.multiple_of(place_at, 16), chunk)],
                        sems.at[len(copies)],
                    )
                )
    for copy in copies:
        copy.start()
    for copy in copies:
        copy.wait()

    total = jnp.zeros((8, PAIR), f32)
    for index in range(PAIRS):
        total = place(w_proj_ref, lanes_of(index), full_s, 3 * PAIRS * D + index * DIN, total)
    mean_proj = whole_mean(total, DIN * D)
    total = jnp.zeros((8, PAIR), f32)
    for index in range(3 * PAIRS):
        total = place(w_qkv_ref, lanes_of(index), full_s, index * D, total)
    mean_qkv = whole_mean(total, D * 3 * D)
    first = 3 * PAIRS * D + PAIRS * DIN
    vectors = full_s[first : first + 24, :].astype(f32)
    targets = [b_proj_ref, mask_ref, gain_ref, bias_ref, q_bias_ref, v_bias_ref]
    for index in range(PAIRS):
        for number, target in enumerate(targets):
            target[lanes_of(index)] = vectors[8 * index + number]
    lane = lax.broadcasted_iota(jnp.int32, (1, PAIR), 1)
    means = [mean_proj, mean_ref[1:2], mean_ref[2:3], mean_ref[3:4], mean_qkv]
    sums = jnp.sum(norms_ref[...], axis=1, keepdims=True)
    sizes = [DIN * D, D * D, D * FF, FF * D, D * 3 * D]
    grads = jnp.ones((1, PAIR), f32)
    weights = jnp.ones((1, PAIR), f32)
    for index, (mean, size) in enumerate(zip(means, sizes)):
        grads = jnp.where(lane == index, mean, grads)
        weights = jnp.where(lane == index, sums[index : index + 1] / size, weights)
    ratios = jnp.sqrt(weights) / jnp.sqrt(grads + 1e-06)
    trust_ref[...] = ratios[0, :4]
    trust_qkv_ref[...] = ratios[0, 4:5]


def whole(shape):
    return pl.BlockSpec(shape, lambda i, s: (0,) * len(shape), pipeline_mode=pl.Buffered(1))


def shape_of(shape, dtype):
    return jax.ShapeDtypeStruct(shape, dtype)


def kernel_call(kernel, grid, in_specs, out_specs, out_shape, scratch, name, cost, args):
    return pl.pallas_call(
        kernel,
        grid_spec=pltpu.PrefetchScalarGridSpec(
            num_scalar_prefetch=1,
            grid=grid,
            in_specs=in_specs,
            out_specs=out_specs,
            scratch_shapes=scratch,
        ),
        out_shape=out_shape,
        compiler_params=pltpu.CompilerParams(
            dimension_semantics=("arbitrary",), vmem_limit_bytes=VMEM
        ),
        cost_estimate=pl.CostEstimate(
            flops=cost[0], bytes_accessed=cost[1], transcendentals=cost[2]
        ),
        name=name,
    )(*args)


def run_forward(start, x_vis, padded_pos, table, params, cotangent, rows, half):
    clips, visible, _ = x_vis.shape
    (
        w_proj,
        b_proj,
        mask_token,
        ln1_gain,
        ln1_bias,
        w_qkv,
        q_bias,
        v_bias,
        w_out,
        b_out,
        ln2_gain,
        ln2_bias,
        w_fc1,
        b_fc1,
        w_fc2,
        b_fc2,
    ) = params
    tokens = clips * rows
    any_space = pl.BlockSpec(memory_space=pl.ANY)
    vector = whole((D,))

    def clip_at(i):
        return jnp.minimum(i, clips - 1)

    in_specs = [
        pl.BlockSpec((1, visible, DIN), lambda i, s: (clip_at(i), 0, 0)),
        pl.BlockSpec((1, 1, SLOT), lambda i, s: (clip_at(i), 0, 0)),
        pl.BlockSpec(
            (pl.Element(LEN // 8), pl.Element(8), pl.Element(D)),
            lambda i, s: (s[0], 0, 0),
            pipeline_mode=pl.Buffered(1),
        ),
        whole((DIN, D)),
        vector,
        vector,
        vector,
        vector,
        whole((D, 3 * D)),
        vector,
        vector,
        vector,
        vector,
        vector,
        whole((FF,)),
        vector,
    ] + [any_space] * 4
    out_specs = [whole((tokens, D)), whole((tokens, PAIR)), whole((8, PAIR))] + [any_space] * 11
    out_shape = [
        shape_of((tokens, D), bf16),
        shape_of((tokens, PAIR), bf16),
        shape_of((8, PAIR), f32),
        shape_of((tokens, D), bf16),
        shape_of((tokens, D), f32),
        shape_of((half, PAIR), bf16),
        shape_of((half, PAIR), bf16),
        shape_of((clips, HEADS, rows, LEN), bf16),
        shape_of((clips, rows, D), bf16),
        shape_of((clips, LEN, D), bf16),
        shape_of((clips, LEN, D), bf16),
        shape_of((clips, LEN, D), bf16),
        shape_of((clips, LEN, D), bf16),
        shape_of((clips, LEN, 1), f32),
    ]
    scratch = [
        pltpu.VMEM((SLOTS, 2, rows, LEN), bf16),
        pltpu.VMEM((rows, D), bf16),
        pltpu.VMEM((LEN, D), bf16),
        pltpu.VMEM((LEN, D), bf16),
        pltpu.VMEM((LEN, D), bf16),
        pltpu.VMEM((LEN, D), bf16),
        pltpu.VMEM((LEN, 1), f32),
        pltpu.VMEM((LEN, D), f32),
        pltpu.VMEM((tokens, D), f32),
        pltpu.VMEM((tokens, D), f32),
        pltpu.VMEM((tokens, D), f32),
        pltpu.VMEM((tokens, D), bf16),
        pltpu.VMEM((tokens, D), f32),
        pltpu.VMEM((tokens, 1), f32),
        pltpu.VMEM((tokens, D), bf16),
        pltpu.VMEM((tokens, D), f32),
        pltpu.VMEM((24, PAIR), f32),
        pltpu.VMEM((2 * half, PAIR), bf16),
        pltpu.VMEM((tokens, D), bf16),
        pltpu.VMEM((D, D), bf16),
        pltpu.VMEM((D, FF), bf16),
        pltpu.VMEM((FF, D), bf16),
        pltpu.VMEM((tokens, D), bf16),
        pltpu.VMEM((1, FF), f32),
        pltpu.SemaphoreType.DMA((6,)),
        pltpu.SemaphoreType.DMA((SLOTS,)),
        pltpu.SemaphoreType.DMA((4,)),
        pltpu.SemaphoreType.DMA((4,)),
    ]
    return kernel_call(
        functools.partial(forward_kernel, rows=rows, clips=clips),
        (clips + 1,),
        in_specs,
        out_specs,
        out_shape,
        scratch,
        "forward",
        (40_000_000_000, 60_000_000, 13_000_000),
        (
            start,
            x_vis,
            padded_pos,
            table,
            w_proj,
            b_proj,
            mask_token,
            ln1_gain,
            ln1_bias,
            w_qkv,
            q_bias,
            v_bias,
            b_out,
            ln2_gain,
            ln2_bias,
            b_fc1,
            b_fc2,
            w_out,
            w_fc1,
            w_fc2,
            cotangent.reshape(tokens, D),
        ),
    )


def run_backward(start, saved, x_vis, padded_pos, w_qkv, ln1_gain, rows, half, base, count, handed):
    query, key, value, grads, extra, weights, normed, xhat, rstd, gmid = saved
    _, visible, _ = x_vis.shape
    last = handed is not None
    own_rows = -(-rows // STEP) * STEP
    any_space = pl.BlockSpec(memory_space=pl.ANY)
    posts = count + 1 if last else count - 1

    def at(i):
        return base if last else i

    def block(*shape):
        return pl.BlockSpec((1,) + shape, lambda i, s: (at(i),) + (0,) * len(shape))

    proj_spec = pl.BlockSpec(
        (1, SLOT // 2, D), lambda i, s: (jnp.minimum(i, posts - 1), 0, 0)
    )
    proj_shapes = [
        shape_of((posts, SLOT // 2, D), f32),
        shape_of((posts, SLOT // 2, D), bf16),
    ]
    hand_shapes = [
        shape_of((2 * half, PAIR), f32),
        shape_of((rows, D), bf16),
        shape_of((LEN, 2 * D), bf16),
    ]
    in_specs = [
        block(rows, D),
        block(LEN, D),
        block(LEN, D),
        pl.BlockSpec((rows, D), lambda i, s: (at(i), 0)),
        pl.BlockSpec((rows, PAIR), lambda i, s: (at(i), 0)),
        pl.BlockSpec((1, 1, SLOT), lambda i, s: (base - 1 + i if last else i, 0, 0)),
        whole((D,)),
    ] + [any_space] * 7
    args = [
        start,
        query,
        key,
        value,
        grads,
        extra,
        padded_pos,
        ln1_gain,
        w_qkv,
        x_vis,
        weights,
        normed,
        xhat,
        rstd,
        gmid,
    ]
    scratch = [
        pltpu.VMEM((2 * PAIRS, 2, rows, LEN), bf16),
        pltpu.VMEM((LEN, D), bf16),
        pltpu.VMEM((LEN, D), bf16),
        pltpu.VMEM((LEN, 1), f32),
        pltpu.VMEM((own_rows, D), f32),
        pltpu.VMEM((rows, D), bf16),
        pltpu.VMEM((LEN, 2 * D), bf16),
        pltpu.VMEM((LEN, D), f32),
        pltpu.VMEM((LEN, D), bf16),
        pltpu.VMEM((LEN, D), bf16),
        pltpu.VMEM((SLOT, D), f32),
        pltpu.VMEM((D, 3 * D), bf16),
        pltpu.VMEM((visible, DIN), bf16),
        pltpu.VMEM((2 * half, PAIR), f32),
        pltpu.SemaphoreType.DMA((3,)),
        pltpu.SemaphoreType.DMA,
        pltpu.SemaphoreType.DMA((5,)),
        pltpu.SemaphoreType.DMA((2 * PAIRS,)),
    ]
    if last:
        in_specs += [any_space] * 3
        args += handed
        out_specs = [whole((half, PAIR)), whole((half, PAIR)), proj_spec, proj_spec]
        out_shape = [shape_of((half, PAIR), f32), shape_of((half, PAIR), bf16)] + proj_shapes
    else:
        out_specs = [proj_spec, proj_spec] + [any_space] * 3
        out_shape = proj_shapes + hand_shapes
    return kernel_call(
        functools.partial(backward_kernel, rows=rows, base=base, count=count, last=last),
        (posts if last else count,),
        in_specs,
        out_specs,
        out_shape,
        scratch,
        "backward",
        (16_000_000_000 * count, 20_000_000 * count, 0),
        tuple(args),
    )


def run_assemble_fc(start, mine, other):
    half = mine.shape[0]
    shapes = [(D, D), (D, FF), (FF, D), (D,), (D,), (D,), (FF,), (D,), (8, PAIR)]
    return kernel_call(
        assemble_fc_kernel,
        (1,),
        [pl.BlockSpec(memory_space=pl.ANY)] * 2,
        [whole(size) for size in shapes],
        [shape_of(size, f32) for size in shapes],
        [pltpu.VMEM((2 * half, PAIR), bf16), pltpu.SemaphoreType.DMA((2,))],
        "assemble_fc",
        (10_000_000, 8_000_000, 0),
        (start, mine, other),
    )


def run_assemble_qkv(start, planes, norms, means, far, chunk):
    any_space = pl.BlockSpec(memory_space=pl.ANY)
    shapes = [(DIN, D), (D, 3 * D), (D,), (D,), (D,), (D,), (D,), (D,), (4,), (1,)]
    return kernel_call(
        functools.partial(assemble_qkv_kernel, far=far, chunk=chunk),
        (1,),
        [any_space] * 8 + [whole((8, PAIR)), whole((8, PAIR))],
        [whole(size) for size in shapes],
        [shape_of(size, f32) for size in shapes],
        [
            pltpu.VMEM((8 * far * chunk, PAIR), bf16),
            pltpu.SemaphoreType.DMA((8 * far,)),
        ],
        "assemble_qkv",
        (10_000_000, 5_000_000, 0),
        (start, *planes, norms, means),
    )


def add_received(kept, received):
    return kept.astype(f32) + received.astype(f32)


def shards(x_vis, vis_pos, *rest):
    params, cotangent = rest[:-1], rest[-1]
    w_proj, ln1_gain, w_qkv = params[0], params[3], params[5]
    seq_size = lax.axis_size("seq")
    clip_size = lax.axis_size("clip")
    groups = seq_size * clip_size // 2
    rows = LEN // seq_size
    clips, visible, _ = x_vis.shape
    far = clip_size // 2
    members = [
        [
            s * clip_size + 2 * high + low
            for s in range(core, seq_size, 2)
            for low in range(2)
            for high in range(far)
        ]
        for core in range(2)
    ]

    def chunk_rows(used):
        return -(-used // (32 * groups)) * 16

    core_pairs = [(s, s ^ 1) for s in range(seq_size)]
    chip_pairs = [(s, s ^ 2) for s in range(seq_size)]

    def across_core(value):
        return lax.ppermute(value, "seq", core_pairs)

    def swap(value):
        chunks = value.reshape(groups, -1, PAIR)
        return lax.all_to_all(chunks, AXES, 0, 0, axis_index_groups=members)

    def total_of(chunks):
        return jnp.sum(chunks.astype(f32), axis=0).astype(bf16)

    def spread(chunk, size):
        return jnp.broadcast_to(chunk[None], (size,) + chunk.shape)

    def across(value, seq_change, low_change, high_change):
        pairs = []
        for s in range(seq_size):
            for c in range(clip_size):
                other = (s ^ (2 * seq_change)) * clip_size + (c ^ (2 * high_change + low_change))
                pairs.append((s * clip_size + c, other))
        return lax.ppermute(value, AXES, pairs)

    def parts_of(arrays, index, count):
        size = arrays[0].shape[0] // count
        result = []
        for k in range(count):
            first = jnp.bitwise_xor(index, k) * size
            pieces = [lax.dynamic_slice_in_dim(value, first, size, 0) for value in arrays]
            total = pieces[0].astype(f32)
            for piece in pieces[1:]:
                total = total + piece.astype(f32)
            result.append(total if k == 0 else total.astype(bf16))
        return result

    def scatter(kept, received, beside):
        x, y, high = seq_index >> 1, clip_index & 1, clip_index >> 1
        own, *others = parts_of([kept, received], 2 * x + y, 4)
        arrays = [own] + [
            across(value, k >> 1, k & 1, 0) for k, value in enumerate(others, 1)
        ]
        arrays, beside = lax.optimization_barrier((arrays, beside))
        size = far
        while size > 1:
            count = 2 if size == 2 or (size.bit_length() % 2 == 0) else 4
            size //= count
            own, *others = parts_of(arrays, (high // size) % count, count)
            arrays = [own] + [
                across(value, 0, 0, size * k) for k, value in enumerate(others, 1)
            ]
        total = arrays[0]
        for value in arrays[1:]:
            total = total + value.astype(f32)
        return total.astype(bf16), beside

    def gather(chunk):
        size = 1
        while size < far:
            count = min(4, far // size)
            chunk = jnp.concatenate(
                [chunk] + [across(chunk, 0, 0, size * k) for k in range(1, count)]
            )
            size *= count
        return [chunk] + [across(chunk, k >> 1, k & 1, 0) for k in (1, 2, 3)]

    fc_chunk = chunk_rows(FC_USED)
    qkv_chunk = chunk_rows(QKV_USED)
    qkv_half = qkv_chunk * groups
    seq_index = lax.axis_index("seq")
    clip_index = lax.axis_index("clip")
    bit = seq_index & 1
    first = seq_index * rows
    local_pos = jnp.where(vis_pos >= first, vis_pos - first, vis_pos - first + LEN)
    padded_pos = jnp.pad(local_pos, ((0, 0), (0, SLOT - visible)), constant_values=-1)[:, None, :]
    table = sinusoid_table(LEN, D)
    table = jnp.asarray(np.concatenate([table, table[: LEN - rows]]).reshape(-1, 8, D))
    number = ((seq_index >> 1) * 2 + (clip_index & 1)) * far + (clip_index >> 1)
    start = jnp.stack([first // 8, bit, number]).astype(jnp.int32)

    (
        grads,
        extra,
        norms,
        output,
        gmid,
        kept,
        sent,
        weights,
        query,
        key,
        value,
        normed,
        xhat,
        rstd,
    ) = run_forward(start, x_vis, padded_pos, table, params, cotangent, rows, fc_chunk * groups)
    fc = add_received(kept, across_core(sent)).astype(bf16)
    fc, query = lax.optimization_barrier((fc, query))
    fc = swap(fc)
    saved = (query, key, value, grads, extra, weights, normed, xhat, rstd, gmid)
    proj_kept0, proj_sent0, *handed = run_backward(
        start, saved, x_vis, padded_pos, w_qkv, ln1_gain, rows, qkv_half, 0, clips - 1, None
    )
    fc, handed = lax.optimization_barrier((spread(total_of(fc), groups), handed))
    fc = swap(fc).reshape(groups * fc_chunk, PAIR)
    kept, sent, proj_kept1, proj_sent1 = run_backward(
        start, saved, x_vis, padded_pos, w_qkv, ln1_gain, rows, qkv_half, clips - 1, 1, handed
    )
    fc, received = lax.optimization_barrier((fc, across_core(sent)))
    w_out_g, w_fc1_g, w_fc2_g, b_out_g, gain2_g, bias2_g, b_fc1_g, b_fc2_g, means = (
        run_assemble_fc(start, fc, across_core(fc))
    )
    qkv, means = scatter(kept, received, means)
    planes = gather(qkv)
    planes += [across_core(plane) for plane in planes]
    proj_kept = jnp.concatenate([proj_kept0, proj_kept1])
    proj_sent = jnp.concatenate([proj_sent0, proj_sent1])
    part = add_received(proj_kept, across_core(proj_sent)).astype(bf16)
    part = add_received(part, lax.ppermute(part, "seq", chip_pairs)).astype(bf16)
    other = across_core(part)
    grad_projected = jnp.where(
        bit == 0,
        jnp.concatenate([part, other], axis=1),
        jnp.concatenate([other, part], axis=1),
    )[:, :visible]
    grad_x = lax.dot_general(
        grad_projected, w_proj, (((2,), (1,)), ((), ())), preferred_element_type=f32
    )
    (
        w_proj_g,
        w_qkv_g,
        b_proj_g,
        mask_g,
        gain1_g,
        bias1_g,
        q_bias_g,
        v_bias_g,
        trust,
        trust_qkv,
    ) = run_assemble_qkv(start, planes, norms, means, far, qkv_chunk)
    return (
        output.reshape(clips, rows, D),
        grad_x,
        w_proj_g,
        b_proj_g,
        mask_g,
        gain1_g,
        bias1_g,
        w_qkv_g,
        q_bias_g,
        v_bias_g,
        w_out_g,
        b_out_g,
        gain2_g,
        bias2_g,
        w_fc1_g,
        b_fc1_g,
        w_fc2_g,
        b_fc2_g,
        trust,
        trust_qkv,
    )


def solution(mesh):
    return jax.shard_map(
        shards,
        mesh=mesh,
        in_specs=(P("clip", None, None), P("clip", None))
        + (P(),) * 16
        + (P("clip", "seq", None),),
        out_specs=(P("clip", "seq", None), P("clip", None, None)) + (P(),) * 18,
        check_vma=False,
    )
```

```python
import functools

import jax
import jax.numpy as jnp
import numpy as np
from jax import lax
from jax.experimental import pallas as pl
from jax.experimental.pallas import tpu as pltpu
from jax.sharding import PartitionSpec as P

D = 384
HEADS = 6
HEAD = 64
PAIRS = 3
PAIR = 128
FF = 1536
DIN = 768
SLOT = 160
LEN = 1568
STEP = 112
BLOCK = 256
BLOCKS = FF // BLOCK
SLOTS = 4
UNROLL_F = False
UNROLL_M = False
FC_USED = 10392
QKV_USED = 5784
AXES = ("seq", "clip")
VMEM = 60 * 1024 * 1024

bf16 = jnp.bfloat16
f32 = jnp.float32


def dot(left, right):
    return lax.dot_general(
        left, right, (((1,), (0,)), ((), ())), preferred_element_type=f32
    )


def dot_rt(left, right):
    return lax.dot_general(
        left, right, (((1,), (1,)), ((), ())), preferred_element_type=f32
    )


def dot_lt(left, right):
    return lax.dot_general(
        left, right, (((0,), (0,)), ((), ())), preferred_element_type=f32
    )


def split3(value):
    high = value.astype(bf16)
    rest = value - high.astype(f32)
    middle = rest.astype(bf16)
    low = (rest - middle.astype(f32)).astype(bf16)
    return high, middle, low


def sinusoid_table(length, columns):
    positions = np.arange(length, dtype=np.float64)[:, None]
    column = np.arange(columns)
    angles = positions / np.power(10000.0, (2 * (column // 2)) / columns)[None, :]
    return np.where((column % 2)[None, :] == 0, np.sin(angles), np.cos(angles)).astype(np.float32)


def row_loop(total, body, carry, unroll=False):
    full = total // STEP

    def at_step(number, carry):
        return body(pl.ds(pl.multiple_of(number * STEP, STEP), STEP), carry)

    carry = lax.fori_loop(0, full, at_step, carry, unroll=unroll)
    if total % STEP:
        carry = body(pl.ds(full * STEP, total % STEP), carry)
    return carry


def own_lanes(head):
    lane = lax.broadcasted_iota(jnp.int32, (1, PAIR), 1)
    return (lane < HEAD) if head == 0 else (lane >= HEAD)


def column_sums(value):
    return jnp.sum(value, axis=0, keepdims=True)


def square_sum(ref):
    rows, columns = ref.shape
    size = 64

    def add(number, total):
        piece = ref[pl.ds(pl.multiple_of(number * size, size), size), :].astype(f32)
        sums = column_sums(piece * piece)
        for first in range(0, columns, PAIR):
            total = total + sums[:, first : first + PAIR]
        return total

    return lax.fori_loop(0, rows // size, add, jnp.zeros((1, PAIR), f32))


def lane_mean(value):
    return jnp.mean(value, axis=1, keepdims=True)


def forward_kernel(
    start_ref,
    x_ref,
    pos_ref,
    table_ref,
    w_proj_ref,
    b_proj_ref,
    mask_ref,
    gain1_ref,
    bias1_ref,
    w_qkv_ref,
    q_bias_ref,
    v_bias_ref,
    b_out_ref,
    gain2_ref,
    bias2_ref,
    b_fc1_ref,
    b_fc2_ref,
    w_out_hbm,
    w_fc1_hbm,
    w_fc2_hbm,
    cot_hbm,
    gs_ref,
    extra_ref,
    norms_ref,
    out_hbm,
    gmid_hbm,
    kept_hbm,
    sent_hbm,
    p_hbm,
    q_hbm,
    k_hbm,
    v_hbm,
    normed_hbm,
    xhat_hbm,
    rstd_hbm,
    p_s,
    q_s,
    k_s,
    v_s,
    normed_s,
    xhat_s,
    rstd_s,
    emb_s,
    middle_s,
    att_s,
    linv_s,
    attended_s,
    xhat2_s,
    rstd2_s,
    normed2_s,
    gn_s,
    vec_s,
    flat_s,
    out_s,
    w_out_s,
    w_fc1_s,
    w_fc2_s,
    cot_s,
    b_fc1_s,
    save_sems,
    p_sems,
    load_sems,
    end_sems,
    *,
    rows,
    clips,
):
    step = pl.program_id(0)
    half = kept_hbm.shape[0]

    def loads():
        pairs = [
            (w_out_hbm, w_out_s),
            (w_fc1_hbm, w_fc1_s),
            (w_fc2_hbm, w_fc2_s),
            (cot_hbm, cot_s),
        ]
        return [
            pltpu.make_async_copy(source, target, load_sems.at[index])
            for index, (source, target) in enumerate(pairs)
        ]

    def saves(number):
        pairs = [
            (q_s, q_hbm),
            (k_s, k_hbm),
            (v_s, v_hbm),
            (normed_s, normed_hbm),
            (xhat_s, xhat_hbm),
            (rstd_s, rstd_hbm),
        ]
        return [
            pltpu.make_async_copy(source, target.at[number], save_sems.at[index])
            for index, (source, target) in enumerate(pairs)
        ]

    def p_save(number):
        slot = lax.rem(number, SLOTS)
        at = lax.div(number, PAIRS)
        pair = lax.rem(number, PAIRS)
        return pltpu.make_async_copy(
            p_s.at[slot], p_hbm.at[at, pl.ds(2 * pair, 2)], p_sems.at[slot]
        )

    @pl.when(step == 0)
    def _():
        for copy in loads():
            copy.start()

    @pl.when(jnp.logical_and(step > 0, step < clips))
    def _():
        for copy in saves(step - 1):
            copy.wait()
        for number in range(PAIRS - 1):
            p_save(PAIRS * (step - 1) + number).wait()

    @pl.when(jnp.logical_and(step > 1, step < clips))
    def _():
        p_save(PAIRS * (step - 1) - 1).wait()

    @pl.when(step < clips)
    def _():
        projected = dot(x_ref[0], w_proj_ref[...]) + b_proj_ref[...][None, :]
        high, middle, low = split3(projected - mask_ref[...][None, :])
        row = lax.broadcasted_iota(jnp.int32, (LEN, 1), 0)
        onehot = (row == pos_ref[0]).astype(f32).astype(bf16)[:, : x_ref.shape[1]]
        emb_s[...] = (
            (table_ref[...].reshape(LEN, D) + mask_ref[...][None, :])
            + dot(onehot, low)
            + dot(onehot, middle)
        ) + dot(onehot, high)
        for number in range(LEN // STEP):
            at = slice(number * STEP, (number + 1) * STEP)
            value = emb_s[at, :]
            centered = value - lane_mean(value)
            rstd = lax.rsqrt(lane_mean(centered * centered) + 1e-05)
            xhat = centered * rstd
            xhat_s[at, :] = xhat.astype(bf16)
            normed_s[at, :] = (xhat * gain1_ref[...][None, :] + bias1_ref[...][None, :]).astype(
                bf16
            )
            rstd_s[at, :] = rstd
        group = pl.ds(pl.multiple_of(step * rows, 8), rows)
        middle_s[group, :] = emb_s[:rows, :]
        normed = normed_s[...]
        k_s[...] = dot(normed, w_qkv_ref[:, D : 2 * D]).astype(bf16)
        v_s[...] = (dot(normed, w_qkv_ref[:, 2 * D :]) + v_bias_ref[...][None, :]).astype(bf16)
        q_s[...] = (dot(normed[:rows], w_qkv_ref[:, :D]) + q_bias_ref[...][None, :]).astype(bf16)
        for copy in saves(step):
            copy.start()

        def attend(pair, carry):
            number = step * PAIRS + pair
            slot = lax.rem(number, SLOTS)
            at = pl.ds(pl.multiple_of(pair * PAIR, PAIR), PAIR)
            query = q_s[:, at]
            key = k_s[:, at]
            value = jnp.concatenate([v_s[:, at], jnp.ones((LEN, PAIR), bf16)], axis=1)
            first = own_lanes(0)
            none = jnp.zeros_like(query)
            both = [
                dot_rt(jnp.where(first, query, none), key),
                dot_rt(jnp.where(first, none, query), key),
            ]
            weights = []
            for head, scores in enumerate(both):
                largest = jnp.max(scores, axis=1, keepdims=True)
                scaled = (scores - largest) * (HEAD**-0.5 * np.log2(np.e))
                weights.append(jnp.exp2(scaled).astype(bf16))
                p_s[slot, head] = weights[head]
            parts = [dot(weight, value) for weight in weights]
            inverse = 1.0 / jnp.where(first, parts[0][:, PAIR:], parts[1][:, PAIR:])
            linv_s[group, at] = inverse
            att_s[group, at] = jnp.where(first, parts[0][:, :PAIR], parts[1][:, :PAIR]) * inverse
            p_save(number).start()
            return carry

        lax.fori_loop(0, PAIRS, attend, 0, unroll=UNROLL_F)

    @pl.when(step == 0)
    def _():
        norms_ref[...] = jnp.zeros_like(norms_ref)
        norms_ref[0:1, :] = square_sum(w_proj_ref)
        norms_ref[4:5, :] = square_sum(w_qkv_ref)
        b_fc1_s[...] = b_fc1_ref[...][None, :]

    @pl.when(step == clips)
    def _():
        for copy in loads():
            copy.wait()
        attended_s[...] = att_s[...].astype(bf16)
        gn_s[...] = dot(attended_s[...], w_out_s[...])

        def norm_middle(at, carry):
            middle = middle_s[at, :] + (gn_s[at, :] + b_out_ref[...][None, :])
            centered = middle - lane_mean(middle)
            rstd = lax.rsqrt(lane_mean(centered * centered) + 1e-05)
            xhat = centered * rstd
            xhat2_s[at, :] = xhat
            rstd2_s[at, :] = rstd
            normed2_s[at, :] = (
                xhat * gain2_ref[...][None, :] + bias2_ref[...][None, :]
            ).astype(bf16)
            middle_s[at, :] = middle + b_fc2_ref[...][None, :]
            gn_s[at, :] = jnp.zeros(middle.shape, f32)
            return carry

        row_loop(clips * rows, norm_middle, 0, unroll=True)
        norms_ref[1:2, :] = square_sum(w_out_s)
        norms_ref[2:3, :] = square_sum(w_fc1_s)
        norms_ref[3:4, :] = square_sum(w_fc2_s)
        flat_s[FC_USED - 24 :, :] = jnp.zeros_like(flat_s[FC_USED - 24 :, :])

        def hidden_block(block, carry):
            normed2 = normed2_s[...]
            cot = cot_s[...]
            at = pl.ds(pl.multiple_of(block * BLOCK, BLOCK), BLOCK)
            w_fc1 = w_fc1_s[:, at]
            w_fc2 = w_fc2_s[at, :]
            pre = dot(normed2, w_fc1) + b_fc1_s[:, at]
            grad_hidden = dot_rt(cot, w_fc2)
            cdf = 0.5 + 0.5 * lax.erf(pre * np.float32(0.5**0.5))
            hidden = (pre * cdf).astype(bf16)
            slope = cdf + pre * (
                jnp.exp2(pre * pre * (-0.5 * np.log2(np.e))) * ((2 * np.pi) ** -0.5)
            )
            grad_pre = grad_hidden * slope
            grad_pre_b = grad_pre.astype(bf16)
            middle_s[...] += dot(hidden, w_fc2)
            gn_s[...] += dot_rt(grad_pre_b, w_fc1)
            grad_w2 = dot_lt(hidden, cot).astype(bf16)
            for column in range(D // PAIR):
                first = FF * PAIRS + column * FF + block * BLOCK
                flat_s[pl.ds(pl.multiple_of(first, 16), BLOCK), :] = grad_w2[
                    :, column * PAIR : (column + 1) * PAIR
                ]
            grad_w1 = dot_lt(normed2, grad_pre_b).astype(bf16)
            sums = column_sums(grad_pre_b.astype(f32))
            for piece in range(BLOCK // PAIR):
                lanes = slice(piece * PAIR, (piece + 1) * PAIR)
                number = block * (BLOCK // PAIR) + piece
                flat_s[pl.ds(pl.multiple_of(number * D, 16), D), :] = grad_w1[:, lanes]
                row = 8 * lax.rem(number, PAIRS) + lax.div(number, PAIRS)
                vec_s[pl.ds(row, 1), :] = sums[:, lanes]
            return carry

        lax.fori_loop(0, BLOCKS, hidden_block, 0, unroll=UNROLL_M)
        out_s[...] = middle_s[...].astype(bf16)
        ends = [pltpu.make_async_copy(out_s, out_hbm, end_sems.at[0])]
        ends[0].start()

        def norm_back(at, carry):
            cot_f = cot_s[at, :].astype(f32)
            grad_normed = gn_s[at, :]
            xhat = xhat2_s[at, :]
            scaled = grad_normed * gain2_ref[...][None, :]
            grad_middle = cot_f + rstd2_s[at, :] * (
                scaled - lane_mean(scaled) - xhat * lane_mean(scaled * xhat)
            )
            middle_s[at, :] = grad_middle
            grad_branch = grad_middle.astype(bf16)
            normed2_s[at, :] = grad_branch
            terms = [cot_f, grad_normed * xhat, grad_normed, grad_branch.astype(f32)]
            return tuple(total + column_sums(term) for total, term in zip(carry, terms))

        zero = jnp.zeros((1, D), f32)
        vectors = row_loop(clips * rows, norm_back, (zero,) * 4, unroll=True)
        ends.append(pltpu.make_async_copy(middle_s, gmid_hbm, end_sems.at[1]))
        ends[1].start()
        grad_branch = normed2_s[...]
        grad_out = dot_lt(attended_s[...], grad_branch).astype(bf16)
        for column in range(D // PAIR):
            lanes = slice(column * PAIR, (column + 1) * PAIR)
            first = 2 * FF * PAIRS + column * D
            flat_s[first : first + D, :] = grad_out[:, lanes]
            for number, vector in enumerate(vectors):
                row = 8 * column + 4 + number
                vec_s[row : row + 1, :] = vector[:, lanes]
        flat_s[FC_USED - 24 : FC_USED, :] = vec_s[...].astype(bf16)
        bit = start_ref[1]
        for index, (side, target) in enumerate([(bit, kept_hbm), (1 - bit, sent_hbm)]):
            copy = pltpu.make_async_copy(
                flat_s.at[pl.ds(pl.multiple_of(side * half, 16), half)],
                target,
                end_sems.at[2 + index],
            )
            copy.start()
            ends.append(copy)
        gn_s[...] = dot_rt(grad_branch, w_out_s[...])

        def inner_products(at, carry):
            grad_att = gn_s[at, :].astype(bf16).astype(f32)
            grad_s = (grad_att * linv_s[at, :]).astype(bf16)
            gs_ref[at, :] = grad_s
            product = grad_s.astype(f32) * att_s[at, :]
            lane = lax.broadcasted_iota(jnp.int32, (1, PAIR), 1)
            packed = jnp.zeros((product.shape[0], PAIR), f32)
            for pair in range(PAIRS):
                piece = product[:, pair * PAIR : (pair + 1) * PAIR]
                for head in range(2):
                    inner = -jnp.sum(
                        jnp.where(own_lanes(head), piece, 0.0), axis=1, keepdims=True
                    )
                    for index, term in enumerate(split3(inner)):
                        where = 3 * (2 * pair + head) + index
                        packed = jnp.where(lane == where, term.astype(f32), packed)
            extra_ref[at, :] = packed.astype(bf16)
            return carry

        row_loop(clips * rows, inner_products, 0, unroll=True)
        for copy in ends + saves(clips - 1):
            copy.wait()
        for number in range(PAIRS * clips - PAIRS - 1, PAIRS * clips):
            p_save(number).wait()


def backward_kernel(
    start_ref,
    q_ref,
    k_ref,
    v_ref,
    gs_ref,
    extra_ref,
    pos_ref,
    gain1_ref,
    w_qkv_hbm,
    x_hbm,
    p_hbm,
    normed_hbm,
    xhat_hbm,
    rstd_hbm,
    gmid_hbm,
    *rest,
    rows,
    base,
    count,
    last,
):
    if last:
        acc_hbm, dq_hbm, dkv_hbm, kept_ref, sent_ref, proj_kept_ref, proj_sent_ref = rest[:7]
        scratch = rest[7:]
    else:
        proj_kept_ref, proj_sent_ref, acc_hbm, dq_hbm, dkv_hbm = rest[:5]
        scratch = rest[5:]
    (p_s, normed_s, xhat_s, rstd_s, own_s, dq_s, dkv_s, gn_s, high_s, low_s, proj_s) = scratch[-18:-7]
    w_qkv_s, x_s, acc_s, hand_sems, w_sem, sems, p_sems = scratch[-7:]
    if last:
        q_s, k_s, v_s, late_sems = scratch[:4]
        late = [
            pltpu.make_async_copy(source.at[pl.ds(base, 1)], target, late_sems.at[index])
            for index, (source, target) in enumerate(
                [(q_ref, q_s), (k_ref, k_s), (v_ref, v_s)]
            )
        ]
        q_ref, k_ref, v_ref = q_s, k_s, v_s
    step = pl.program_id(0)
    lane = lax.broadcasted_iota(jnp.int32, (1, PAIR), 1)
    first_post = base - 1 if last else base

    def loads():
        at = first_post + step
        pairs = [
            (normed_hbm.at[at], normed_s),
            (xhat_hbm.at[at], xhat_s),
            (rstd_hbm.at[at], rstd_s),
            (x_hbm.at[at], x_s),
            (gmid_hbm.at[pl.ds(pl.multiple_of(at * rows, 8), rows)], own_s.at[pl.ds(0, rows)]),
        ]
        return [
            pltpu.make_async_copy(source, target, sems.at[index])
            for index, (source, target) in enumerate(pairs)
        ]

    def hand(number):
        pairs = [(acc_s, acc_hbm), (dq_s, dq_hbm), (dkv_s, dkv_hbm)]
        inside, outside = pairs[number]
        if last:
            return pltpu.make_async_copy(outside, inside, hand_sems.at[number])
        return pltpu.make_async_copy(inside, outside, hand_sems.at[number])

    def p_load(number):
        at = lax.div(number, PAIRS)
        pair = lax.rem(number, PAIRS)
        slot = lax.rem(number, 2 * PAIRS)
        return pltpu.make_async_copy(
            p_hbm.at[base + at, pl.ds(2 * pair, 2)], p_s.at[slot], p_sems.at[slot]
        )

    w_load = pltpu.make_async_copy(w_qkv_hbm, w_qkv_s, w_sem)
    has_post = True if last else step < count - 1

    if last:
        for number in (2, 1):
            pl.when(step == 0)(hand(number).start)

    @pl.when(step == 0)
    def _():
        if not last:
            for pair in range(PAIRS):
                p_load(pair).start()
        w_load.start()

    @pl.when(has_post)
    def _():
        for copy in loads():
            copy.start()

    @pl.when(step == 0)
    def _():
        own_s[rows:, :] = jnp.zeros_like(own_s[rows:, :])
        if last:
            hand(0).start()
            for copy in late:
                copy.start()
            for pair in range(PAIRS):
                p_load(pair).start()
        else:

            def clear(number, carry):
                at = pl.ds(pl.multiple_of(number * 256, 256), 256)
                acc_s[at, :] = jnp.zeros((256, PAIR), f32)
                return carry

            lax.fori_loop(0, acc_s.shape[0] // 256, clear, 0)

    def attend_back(phase, carry):
        number = phase if last else step * PAIRS + phase
        slot = lax.rem(number, 2 * PAIRS)
        p_load(number).wait()
        at = pl.ds(pl.multiple_of(phase * PAIR, PAIR), PAIR)
        query = q_ref[0, :, at] * jnp.asarray(HEAD**-0.5, bf16)
        key = k_ref[0, :, at]
        value = jnp.concatenate([v_ref[0, :, at], jnp.ones((LEN, PAIR), bf16)], axis=1)
        grad = gs_ref[:, at]
        extra = extra_ref[...]
        products = []
        for head in range(2):
            first = 3 * (2 * phase + head)
            inner = jnp.logical_and(lane >= first, lane < first + 3)
            left = jnp.concatenate(
                [
                    jnp.where(own_lanes(head), grad, jnp.zeros_like(grad)),
                    jnp.where(inner, extra, jnp.zeros_like(extra)),
                ],
                axis=1,
            )
            products.append(dot_rt(left, value))
        weights = [p_s[slot, head] for head in range(2)]
        scores = [
            (weight.astype(f32) * product).astype(bf16)
            for weight, product in zip(weights, products)
        ]
        values = [dot_lt(weight, grad) for weight in weights]
        keys = [dot_lt(score, query) for score in scores]
        queries = [dot(score, key) for score in scores]
        side = own_lanes(0)
        dq_s[:, at] = (jnp.where(side, queries[0], queries[1]) * (HEAD**-0.5)).astype(bf16)
        dkv_s[:, at] = jnp.where(side, keys[0], keys[1]).astype(bf16)
        at = pl.ds(pl.multiple_of(phase * PAIR + D, PAIR), PAIR)
        dkv_s[:, at] = jnp.where(side, values[0], values[1]).astype(bf16)
        return carry

    if last:

        @pl.when(step == 1)
        def _():
            for copy in late:
                copy.wait()
            lax.fori_loop(0, PAIRS, attend_back, 0)

    else:
        lax.fori_loop(0, PAIRS, attend_back, 0)

        @pl.when(step + 1 < count)
        def _():
            for pair in range(PAIRS):
                p_load(PAIRS * (step + 1) + pair).start()

    @pl.when(step == 0)
    def _():
        w_load.wait()
        if last:
            hand(1).wait()
            hand(2).wait()

    @pl.when(has_post)
    def _():
        grad_q = dq_s[...]
        grad_kv = dkv_s[...]
        gn_s[...] = dot_rt(grad_kv, w_qkv_s[:, D:])
        gn_s[:rows, :] += dot_rt(grad_q, w_qkv_s[:, :D])
        for copy in loads():
            copy.wait()
        if last:

            @pl.when(step == 0)
            def _():
                hand(0).wait()

        normed = normed_s[...]
        part_q = dot_lt(normed[:rows], grad_q)
        part_kv = dot_lt(normed, grad_kv)
        for index in range(PAIRS):
            acc_s[index * D : (index + 1) * D, :] += part_q[:, index * PAIR : (index + 1) * PAIR]
        for index in range(2 * PAIRS):
            first = (PAIRS + index) * D
            acc_s[first : first + D, :] += part_kv[:, index * PAIR : (index + 1) * PAIR]
        ones = jnp.ones((8, LEN), bf16)
        sum_q = dot(ones[:, :rows], grad_q)[:1]
        sum_v = dot(ones, grad_kv[:, D:])[:1]

        def norm_rows(number, carry, with_own):
            at = pl.ds(pl.multiple_of(number * STEP, STEP), STEP)
            sum_gain, sum_bias, sum_emb = carry
            value = gn_s[at, :]
            xhat = xhat_s[at, :].astype(f32)
            sum_bias = sum_bias + column_sums(value)
            sum_gain = sum_gain + column_sums(value * xhat)
            scaled = value * gain1_ref[...][None, :]
            grad = rstd_s[at, :] * (
                scaled - lane_mean(scaled) - xhat * lane_mean(scaled * xhat)
            )
            if with_own:
                grad = grad + own_s[at, :]
            sum_emb = sum_emb + column_sums(grad)
            high = grad.astype(bf16)
            high_s[at, :] = high
            low_s[at, :] = (grad - high.astype(f32)).astype(bf16)
            return sum_gain, sum_bias, sum_emb

        zero = jnp.zeros((1, D), f32)
        own_steps = own_s.shape[0] // STEP
        carry = lax.fori_loop(
            0, own_steps, functools.partial(norm_rows, with_own=True), (zero, zero, zero), unroll=True
        )
        sum_gain, sum_bias, sum_emb = lax.fori_loop(
            own_steps, LEN // STEP, functools.partial(norm_rows, with_own=False), carry, unroll=True
        )
        row = lax.broadcasted_iota(jnp.int32, (LEN, 1), 0)
        onehot = (row == pos_ref[0]).astype(f32).astype(bf16)
        grad_proj = dot_lt(onehot, high_s[...]) + dot_lt(onehot, low_s[...])
        proj_s[...] = grad_proj
        bit = start_ref[1]
        part = SLOT // 2
        proj_kept_ref[0] = proj_s[pl.ds(pl.multiple_of(bit * part, 8), part), :]
        proj_sent_ref[0] = proj_s[
            pl.ds(pl.multiple_of((1 - bit) * part, 8), part), :
        ].astype(bf16)
        sum_proj = column_sums(grad_proj)
        vectors = [sum_proj, sum_emb - sum_proj, sum_gain, sum_bias, sum_q, sum_v]
        weight = dot_lt(x_s[...], grad_proj[: x_s.shape[0]].astype(bf16))
        for index in range(D // PAIR):
            lanes = slice(index * PAIR, (index + 1) * PAIR)
            first = 3 * PAIRS * D + index * DIN
            acc_s[first : first + DIN, :] += weight[:, lanes]
            first = 3 * PAIRS * D + PAIRS * DIN + 8 * index
            for number, vector in enumerate(vectors):
                acc_s[first + number : first + number + 1, :] += vector[:, lanes]

    if last:

        @pl.when(step == 1)
        def _():
            bit = start_ref[1]
            half = kept_ref.shape[0]

            def hand_over(number, carry):
                at = pl.ds(pl.multiple_of(number * 256, 256), 256)
                kept_at = pl.ds(pl.multiple_of(bit * half + number * 256, 256), 256)
                sent_at = pl.ds(pl.multiple_of((1 - bit) * half + number * 256, 256), 256)
                kept_ref[at, :] = acc_s[kept_at, :]
                sent_ref[at, :] = acc_s[sent_at, :].astype(bf16)
                return carry

            lax.fori_loop(0, half // 256, hand_over, 0)

    else:
        pl.when(step == count - 2)(hand(0).start)

        @pl.when(step == count - 1)
        def _():
            hand(1).start()
            hand(2).start()
            for number in range(3):
                hand(number).wait()


def place(target, lanes, source, where, total):
    size = target.shape[0]
    step = 96

    def move(number, total):
        first = pl.multiple_of(number * step, 16)
        value = source[pl.ds(pl.multiple_of(where + first, 16), step), :].astype(f32)
        target[pl.ds(first, step), lanes] = value
        return total + jnp.sum((value * value).reshape(step // 8, 8, PAIR), axis=0)

    return lax.fori_loop(0, size // step, move, total, unroll=2)


def lanes_of(index):
    return slice(index * PAIR, (index + 1) * PAIR)


def whole_mean(total, size):
    value = jnp.sum(jnp.sum(total, axis=1, keepdims=True), axis=0, keepdims=True)
    return value / size


def assemble_fc_kernel(
    start_ref,
    mine_hbm,
    other_hbm,
    w_out_ref,
    w_fc1_ref,
    w_fc2_ref,
    b_out_ref,
    gain_ref,
    bias_ref,
    b_fc1_ref,
    b_fc2_ref,
    mean_ref,
    full_s,
    sems,
):
    half = mine_hbm.shape[0]
    bit = start_ref[1]
    copies = [
        pltpu.make_async_copy(
            source, full_s.at[pl.ds(pl.multiple_of(side * half, 16), half)], sems.at[index]
        )
        for index, (source, side) in enumerate([(mine_hbm, bit), (other_hbm, 1 - bit)])
    ]
    for copy in copies:
        copy.start()
    for copy in copies:
        copy.wait()

    total = jnp.zeros((8, PAIR), f32)
    for index in range(PAIRS):
        total = place(w_out_ref, lanes_of(index), full_s, 2 * FF * PAIRS + index * D, total)
    mean_out = whole_mean(total, D * D)
    total = jnp.zeros((8, PAIR), f32)
    for index in range(FF // PAIR):
        total = place(w_fc1_ref, lanes_of(index), full_s, index * D, total)
    mean_fc1 = whole_mean(total, D * FF)
    total = jnp.zeros((8, PAIR), f32)
    for index in range(PAIRS):
        total = place(w_fc2_ref, lanes_of(index), full_s, FF * PAIRS + index * FF, total)
    mean_fc2 = whole_mean(total, FF * D)
    first = 2 * FF * PAIRS + PAIRS * D
    vectors = full_s[first : first + 24, :].astype(f32)
    for index in range(PAIRS):
        lanes = lanes_of(index)
        for number in range(4):
            b_fc1_ref[number * D + index * PAIR : number * D + (index + 1) * PAIR] = vectors[
                8 * index + number
            ]
        for number, target in enumerate([b_fc2_ref, gain_ref, bias_ref, b_out_ref]):
            target[lanes] = vectors[8 * index + 4 + number]
    row = lax.broadcasted_iota(jnp.int32, (8, PAIR), 0)
    mean_ref[...] = jnp.where(
        row == 1, mean_out, jnp.where(row == 2, mean_fc1, mean_fc2)
    )


def assemble_qkv_kernel(
    start_ref,
    *refs,
    far,
    chunk,
):
    planes = refs[:8]
    (
        norms_ref,
        mean_ref,
        w_proj_ref,
        w_qkv_ref,
        b_proj_ref,
        mask_ref,
        gain_ref,
        bias_ref,
        q_bias_ref,
        v_bias_ref,
        trust_ref,
        trust_qkv_ref,
        full_s,
        sems,
    ) = refs[8:]
    half = 4 * far * chunk
    bit = start_ref[1]
    copies = []
    for side in range(2):
        for plane in range(4):
            for line in range(far):
                place_at = jnp.bitwise_xor(start_ref[2], plane * far + line) * chunk
                place_at = place_at + (bit if side == 0 else 1 - bit) * half
                copies.append(
                    pltpu.make_async_copy(
                        planes[4 * side + plane].at[pl.ds(line * chunk, chunk)],
                        full_s.at[pl.ds(pl.multiple_of(place_at, 16), chunk)],
                        sems.at[len(copies)],
                    )
                )
    for copy in copies:
        copy.start()
    for copy in copies:
        copy.wait()

    total = jnp.zeros((8, PAIR), f32)
    for index in range(PAIRS):
        total = place(w_proj_ref, lanes_of(index), full_s, 3 * PAIRS * D + index * DIN, total)
    mean_proj = whole_mean(total, DIN * D)
    total = jnp.zeros((8, PAIR), f32)
    for index in range(3 * PAIRS):
        total = place(w_qkv_ref, lanes_of(index), full_s, index * D, total)
    mean_qkv = whole_mean(total, D * 3 * D)
    first = 3 * PAIRS * D + PAIRS * DIN
    vectors = full_s[first : first + 24, :].astype(f32)
    targets = [b_proj_ref, mask_ref, gain_ref, bias_ref, q_bias_ref, v_bias_ref]
    for index in range(PAIRS):
        for number, target in enumerate(targets):
            target[lanes_of(index)] = vectors[8 * index + number]
    lane = lax.broadcasted_iota(jnp.int32, (1, PAIR), 1)
    means = [mean_proj, mean_ref[1:2], mean_ref[2:3], mean_ref[3:4], mean_qkv]
    sums = jnp.sum(norms_ref[...], axis=1, keepdims=True)
    sizes = [DIN * D, D * D, D * FF, FF * D, D * 3 * D]
    grads = jnp.ones((1, PAIR), f32)
    weights = jnp.ones((1, PAIR), f32)
    for index, (mean, size) in enumerate(zip(means, sizes)):
        grads = jnp.where(lane == index, mean, grads)
        weights = jnp.where(lane == index, sums[index : index + 1] / size, weights)
    ratios = jnp.sqrt(weights) / jnp.sqrt(grads + 1e-06)
    trust_ref[...] = ratios[0, :4]
    trust_qkv_ref[...] = ratios[0, 4:5]


def whole(shape):
    return pl.BlockSpec(shape, lambda i, s: (0,) * len(shape), pipeline_mode=pl.Buffered(1))


def shape_of(shape, dtype):
    return jax.ShapeDtypeStruct(shape, dtype)


def kernel_call(kernel, grid, in_specs, out_specs, out_shape, scratch, name, cost, args):
    return pl.pallas_call(
        kernel,
        grid_spec=pltpu.PrefetchScalarGridSpec(
            num_scalar_prefetch=1,
            grid=grid,
            in_specs=in_specs,
            out_specs=out_specs,
            scratch_shapes=scratch,
        ),
        out_shape=out_shape,
        compiler_params=pltpu.CompilerParams(
            dimension_semantics=("arbitrary",), vmem_limit_bytes=VMEM
        ),
        cost_estimate=pl.CostEstimate(
            flops=cost[0], bytes_accessed=cost[1], transcendentals=cost[2]
        ),
        name=name,
    )(*args)


def run_forward(start, x_vis, padded_pos, table, params, cotangent, rows, half):
    clips, visible, _ = x_vis.shape
    (
        w_proj,
        b_proj,
        mask_token,
        ln1_gain,
        ln1_bias,
        w_qkv,
        q_bias,
        v_bias,
        w_out,
        b_out,
        ln2_gain,
        ln2_bias,
        w_fc1,
        b_fc1,
        w_fc2,
        b_fc2,
    ) = params
    tokens = clips * rows
    any_space = pl.BlockSpec(memory_space=pl.ANY)
    vector = whole((D,))

    def clip_at(i):
        return jnp.minimum(i, clips - 1)

    in_specs = [
        pl.BlockSpec((1, visible, DIN), lambda i, s: (clip_at(i), 0, 0)),
        pl.BlockSpec((1, 1, SLOT), lambda i, s: (clip_at(i), 0, 0)),
        pl.BlockSpec(
            (pl.Element(LEN // 8), pl.Element(8), pl.Element(D)),
            lambda i, s: (s[0], 0, 0),
            pipeline_mode=pl.Buffered(1),
        ),
        whole((DIN, D)),
        vector,
        vector,
        vector,
        vector,
        whole((D, 3 * D)),
        vector,
        vector,
        vector,
        vector,
        vector,
        whole((FF,)),
        vector,
    ] + [any_space] * 4
    out_specs = [whole((tokens, D)), whole((tokens, PAIR)), whole((8, PAIR))] + [any_space] * 11
    out_shape = [
        shape_of((tokens, D), bf16),
        shape_of((tokens, PAIR), bf16),
        shape_of((8, PAIR), f32),
        shape_of((tokens, D), bf16),
        shape_of((tokens, D), f32),
        shape_of((half, PAIR), bf16),
        shape_of((half, PAIR), bf16),
        shape_of((clips, HEADS, rows, LEN), bf16),
        shape_of((clips, rows, D), bf16),
        shape_of((clips, LEN, D), bf16),
        shape_of((clips, LEN, D), bf16),
        shape_of((clips, LEN, D), bf16),
        shape_of((clips, LEN, D), bf16),
        shape_of((clips, LEN, 1), f32),
    ]
    scratch = [
        pltpu.VMEM((SLOTS, 2, rows, LEN), bf16),
        pltpu.VMEM((rows, D), bf16),
        pltpu.VMEM((LEN, D), bf16),
        pltpu.VMEM((LEN, D), bf16),
        pltpu.VMEM((LEN, D), bf16),
        pltpu.VMEM((LEN, D), bf16),
        pltpu.VMEM((LEN, 1), f32),
        pltpu.VMEM((LEN, D), f32),
        pltpu.VMEM((tokens, D), f32),
        pltpu.VMEM((tokens, D), f32),
        pltpu.VMEM((tokens, D), f32),
        pltpu.VMEM((tokens, D), bf16),
        pltpu.VMEM((tokens, D), f32),
        pltpu.VMEM((tokens, 1), f32),
        pltpu.VMEM((tokens, D), bf16),
        pltpu.VMEM((tokens, D), f32),
        pltpu.VMEM((24, PAIR), f32),
        pltpu.VMEM((2 * half, PAIR), bf16),
        pltpu.VMEM((tokens, D), bf16),
        pltpu.VMEM((D, D), bf16),
        pltpu.VMEM((D, FF), bf16),
        pltpu.VMEM((FF, D), bf16),
        pltpu.VMEM((tokens, D), bf16),
        pltpu.VMEM((1, FF), f32),
        pltpu.SemaphoreType.DMA((6,)),
        pltpu.SemaphoreType.DMA((SLOTS,)),
        pltpu.SemaphoreType.DMA((4,)),
        pltpu.SemaphoreType.DMA((4,)),
    ]
    return kernel_call(
        functools.partial(forward_kernel, rows=rows, clips=clips),
        (clips + 1,),
        in_specs,
        out_specs,
        out_shape,
        scratch,
        "forward",
        (40_000_000_000, 60_000_000, 13_000_000),
        (
            start,
            x_vis,
            padded_pos,
            table,
            w_proj,
            b_proj,
            mask_token,
            ln1_gain,
            ln1_bias,
            w_qkv,
            q_bias,
            v_bias,
            b_out,
            ln2_gain,
            ln2_bias,
            b_fc1,
            b_fc2,
            w_out,
            w_fc1,
            w_fc2,
            cotangent.reshape(tokens, D),
        ),
    )


def run_backward(start, saved, x_vis, padded_pos, w_qkv, ln1_gain, rows, half, base, count, handed):
    query, key, value, grads, extra, weights, normed, xhat, rstd, gmid = saved
    _, visible, _ = x_vis.shape
    last = handed is not None
    own_rows = -(-rows // STEP) * STEP
    any_space = pl.BlockSpec(memory_space=pl.ANY)
    posts = count + 1 if last else count - 1

    def at(i):
        return base if last else i

    def block(*shape):
        return pl.BlockSpec((1,) + shape, lambda i, s: (at(i),) + (0,) * len(shape))

    proj_spec = pl.BlockSpec(
        (1, SLOT // 2, D), lambda i, s: (jnp.minimum(i, posts - 1), 0, 0)
    )
    proj_shapes = [
        shape_of((posts, SLOT // 2, D), f32),
        shape_of((posts, SLOT // 2, D), bf16),
    ]
    hand_shapes = [
        shape_of((2 * half, PAIR), f32),
        shape_of((rows, D), bf16),
        shape_of((LEN, 2 * D), bf16),
    ]
    in_specs = [
        block(rows, D),
        block(LEN, D),
        block(LEN, D),
        pl.BlockSpec((rows, D), lambda i, s: (at(i), 0)),
        pl.BlockSpec((rows, PAIR), lambda i, s: (at(i), 0)),
        pl.BlockSpec((1, 1, SLOT), lambda i, s: (base - 1 + i if last else i, 0, 0)),
        whole((D,)),
    ] + [any_space] * 7
    args = [
        start,
        query,
        key,
        value,
        grads,
        extra,
        padded_pos,
        ln1_gain,
        w_qkv,
        x_vis,
        weights,
        normed,
        xhat,
        rstd,
        gmid,
    ]
    scratch = [
        pltpu.VMEM((2 * PAIRS, 2, rows, LEN), bf16),
        pltpu.VMEM((LEN, D), bf16),
        pltpu.VMEM((LEN, D), bf16),
        pltpu.VMEM((LEN, 1), f32),
        pltpu.VMEM((own_rows, D), f32),
        pltpu.VMEM((rows, D), bf16),
        pltpu.VMEM((LEN, 2 * D), bf16),
        pltpu.VMEM((LEN, D), f32),
        pltpu.VMEM((LEN, D), bf16),
        pltpu.VMEM((LEN, D), bf16),
        pltpu.VMEM((SLOT, D), f32),
        pltpu.VMEM((D, 3 * D), bf16),
        pltpu.VMEM((visible, DIN), bf16),
        pltpu.VMEM((2 * half, PAIR), f32),
        pltpu.SemaphoreType.DMA((3,)),
        pltpu.SemaphoreType.DMA,
        pltpu.SemaphoreType.DMA((5,)),
        pltpu.SemaphoreType.DMA((2 * PAIRS,)),
    ]
    if last:
        in_specs[:3] = [any_space] * 3
        scratch = [
            pltpu.VMEM((1, rows, D), bf16),
            pltpu.VMEM((1, LEN, D), bf16),
            pltpu.VMEM((1, LEN, D), bf16),
            pltpu.SemaphoreType.DMA((3,)),
        ] + scratch
        in_specs += [any_space] * 3
        args += handed
        out_specs = [whole((half, PAIR)), whole((half, PAIR)), proj_spec, proj_spec]
        out_shape = [shape_of((half, PAIR), f32), shape_of((half, PAIR), bf16)] + proj_shapes
    else:
        out_specs = [proj_spec, proj_spec] + [any_space] * 3
        out_shape = proj_shapes + hand_shapes
    return kernel_call(
        functools.partial(backward_kernel, rows=rows, base=base, count=count, last=last),
        (posts if last else count,),
        in_specs,
        out_specs,
        out_shape,
        scratch,
        "backward",
        (16_000_000_000 * count, 20_000_000 * count, 0),
        tuple(args),
    )


def run_assemble_fc(start, mine, other):
    half = mine.shape[0]
    shapes = [(D, D), (D, FF), (FF, D), (D,), (D,), (D,), (FF,), (D,), (8, PAIR)]
    return kernel_call(
        assemble_fc_kernel,
        (1,),
        [pl.BlockSpec(memory_space=pl.ANY)] * 2,
        [whole(size) for size in shapes],
        [shape_of(size, f32) for size in shapes],
        [pltpu.VMEM((2 * half, PAIR), bf16), pltpu.SemaphoreType.DMA((2,))],
        "assemble_fc",
        (10_000_000, 8_000_000, 0),
        (start, mine, other),
    )


def run_assemble_qkv(start, planes, norms, means, far, chunk):
    any_space = pl.BlockSpec(memory_space=pl.ANY)
    shapes = [(DIN, D), (D, 3 * D), (D,), (D,), (D,), (D,), (D,), (D,), (4,), (1,)]
    return kernel_call(
        functools.partial(assemble_qkv_kernel, far=far, chunk=chunk),
        (1,),
        [any_space] * 8 + [whole((8, PAIR)), whole((8, PAIR))],
        [whole(size) for size in shapes],
        [shape_of(size, f32) for size in shapes],
        [
            pltpu.VMEM((8 * far * chunk, PAIR), bf16),
            pltpu.SemaphoreType.DMA((8 * far,)),
        ],
        "assemble_qkv",
        (10_000_000, 5_000_000, 0),
        (start, *planes, norms, means),
    )


def add_received(kept, received):
    return kept.astype(f32) + received.astype(f32)


def shards(x_vis, vis_pos, *rest):
    params, cotangent = rest[:-1], rest[-1]
    w_proj, ln1_gain, w_qkv = params[0], params[3], params[5]
    seq_size = lax.axis_size("seq")
    clip_size = lax.axis_size("clip")
    groups = seq_size * clip_size // 2
    rows = LEN // seq_size
    clips, visible, _ = x_vis.shape
    far = clip_size // 2
    members = [
        [
            s * clip_size + 2 * high + low
            for s in range(core, seq_size, 2)
            for low in range(2)
            for high in range(far)
        ]
        for core in range(2)
    ]

    def chunk_rows(used):
        return -(-used // (32 * groups)) * 16

    core_pairs = [(s, s ^ 1) for s in range(seq_size)]
    chip_pairs = [(s, s ^ 2) for s in range(seq_size)]

    def across_core(value):
        return lax.ppermute(value, "seq", core_pairs)

    def swap(value):
        chunks = value.reshape(groups, -1, PAIR)
        return lax.all_to_all(chunks, AXES, 0, 0, axis_index_groups=members)

    def total_of(chunks):
        return jnp.sum(chunks.astype(f32), axis=0).astype(bf16)

    def spread(chunk, size):
        return jnp.broadcast_to(chunk[None], (size,) + chunk.shape)

    def across(value, seq_change, low_change, high_change):
        pairs = []
        for s in range(seq_size):
            for c in range(clip_size):
                other = (s ^ (2 * seq_change)) * clip_size + (c ^ (2 * high_change + low_change))
                pairs.append((s * clip_size + c, other))
        return lax.ppermute(value, AXES, pairs)

    def parts_of(arrays, index, count):
        size = arrays[0].shape[0] // count
        result = []
        for k in range(count):
            first = jnp.bitwise_xor(index, k) * size
            pieces = [lax.dynamic_slice_in_dim(value, first, size, 0) for value in arrays]
            total = pieces[0].astype(f32)
            for piece in pieces[1:]:
                total = total + piece.astype(f32)
            result.append(total if k == 0 else total.astype(bf16))
        return result

    def scatter(kept, received, beside):
        x, y, high = seq_index >> 1, clip_index & 1, clip_index >> 1
        own, *others = parts_of([kept, received], 2 * x + y, 4)
        arrays = [own] + [
            across(value, k >> 1, k & 1, 0) for k, value in enumerate(others, 1)
        ]
        arrays, beside = lax.optimization_barrier((arrays, beside))
        size = far
        while size > 1:
            count = 2 if size == 2 or (size.bit_length() % 2 == 0) else 4
            size //= count
            own, *others = parts_of(arrays, (high // size) % count, count)
            arrays = [own] + [
                across(value, 0, 0, size * k) for k, value in enumerate(others, 1)
            ]
        total = arrays[0]
        for value in arrays[1:]:
            total = total + value.astype(f32)
        return total.astype(bf16), beside

    def gather(chunk):
        size = 1
        while size < far:
            count = min(4, far // size)
            chunk = jnp.concatenate(
                [chunk] + [across(chunk, 0, 0, size * k) for k in range(1, count)]
            )
            size *= count
        return [chunk] + [across(chunk, k >> 1, k & 1, 0) for k in (1, 2, 3)]

    fc_chunk = chunk_rows(FC_USED)
    qkv_chunk = chunk_rows(QKV_USED)
    qkv_half = qkv_chunk * groups
    seq_index = lax.axis_index("seq")
    clip_index = lax.axis_index("clip")
    bit = seq_index & 1
    first = seq_index * rows
    local_pos = jnp.where(vis_pos >= first, vis_pos - first, vis_pos - first + LEN)
    padded_pos = jnp.pad(local_pos, ((0, 0), (0, SLOT - visible)), constant_values=-1)[:, None, :]
    table = sinusoid_table(LEN, D)
    table = jnp.asarray(np.concatenate([table, table[: LEN - rows]]).reshape(-1, 8, D))
    number = ((seq_index >> 1) * 2 + (clip_index & 1)) * far + (clip_index >> 1)
    start = jnp.stack([first // 8, bit, number]).astype(jnp.int32)

    (
        grads,
        extra,
        norms,
        output,
        gmid,
        kept,
        sent,
        weights,
        query,
        key,
        value,
        normed,
        xhat,
        rstd,
    ) = run_forward(start, x_vis, padded_pos, table, params, cotangent, rows, fc_chunk * groups)
    fc = add_received(kept, across_core(sent)).astype(bf16)
    fc, query = lax.optimization_barrier((fc, query))
    fc = swap(fc)
    saved = (query, key, value, grads, extra, weights, normed, xhat, rstd, gmid)
    proj_kept0, proj_sent0, *handed = run_backward(
        start, saved, x_vis, padded_pos, w_qkv, ln1_gain, rows, qkv_half, 0, clips - 1, None
    )
    fc, handed = lax.optimization_barrier((spread(total_of(fc), groups), handed))
    fc = swap(fc).reshape(groups * fc_chunk, PAIR)
    kept, sent, proj_kept1, proj_sent1 = run_backward(
        start, saved, x_vis, padded_pos, w_qkv, ln1_gain, rows, qkv_half, clips - 1, 1, handed
    )
    fc, received = lax.optimization_barrier((fc, across_core(sent)))
    w_out_g, w_fc1_g, w_fc2_g, b_out_g, gain2_g, bias2_g, b_fc1_g, b_fc2_g, means = (
        run_assemble_fc(start, fc, across_core(fc))
    )
    qkv, means = scatter(kept, received, means)
    planes = gather(qkv)
    planes += [across_core(plane) for plane in planes]
    proj_kept = jnp.concatenate([proj_kept0, proj_kept1])
    proj_sent = jnp.concatenate([proj_sent0, proj_sent1])
    part = add_received(proj_kept, across_core(proj_sent)).astype(bf16)
    part = add_received(part, lax.ppermute(part, "seq", chip_pairs)).astype(bf16)
    other = across_core(part)
    grad_projected = jnp.where(
        bit == 0,
        jnp.concatenate([part, other], axis=1),
        jnp.concatenate([other, part], axis=1),
    )[:, :visible]
    grad_x = lax.dot_general(
        grad_projected, w_proj, (((2,), (1,)), ((), ())), preferred_element_type=f32
    )
    (
        w_proj_g,
        w_qkv_g,
        b_proj_g,
        mask_g,
        gain1_g,
        bias1_g,
        q_bias_g,
        v_bias_g,
        trust,
        trust_qkv,
    ) = run_assemble_qkv(start, planes, norms, means, far, qkv_chunk)
    return (
        output.reshape(clips, rows, D),
        grad_x,
        w_proj_g,
        b_proj_g,
        mask_g,
        gain1_g,
        bias1_g,
        w_qkv_g,
        q_bias_g,
        v_bias_g,
        w_out_g,
        b_out_g,
        gain2_g,
        bias2_g,
        w_fc1_g,
        b_fc1_g,
        w_fc2_g,
        b_fc2_g,
        trust,
        trust_qkv,
    )


def solution(mesh):
    return jax.shard_map(
        shards,
        mesh=mesh,
        in_specs=(P("clip", None, None), P("clip", None))
        + (P(),) * 16
        + (P("clip", "seq", None),),
        out_specs=(P("clip", "seq", None), P("clip", None, None)) + (P(),) * 18,
        check_vma=False,
    )
```

```python
import functools

import jax
import jax.numpy as jnp
import numpy as np
from jax import lax
from jax.experimental import pallas as pl
from jax.experimental.pallas import tpu as pltpu
from jax.sharding import PartitionSpec as P

D = 384
HEADS = 6
HEAD = 64
PAIRS = 3
PAIR = 128
FF = 1536
DIN = 768
SLOT = 160
LEN = 1568
STEP = 112
BLOCK = 256
BLOCKS = FF // BLOCK
SLOTS = 4
UNROLL_F = False
UNROLL_M = False
FC_USED = 10392
QKV_USED = 5784
AXES = ("seq", "clip")
VMEM = 60 * 1024 * 1024

bf16 = jnp.bfloat16
f32 = jnp.float32


def dot(left, right):
    return lax.dot_general(
        left, right, (((1,), (0,)), ((), ())), preferred_element_type=f32
    )


def dot_rt(left, right):
    return lax.dot_general(
        left, right, (((1,), (1,)), ((), ())), preferred_element_type=f32
    )


def dot_lt(left, right):
    return lax.dot_general(
        left, right, (((0,), (0,)), ((), ())), preferred_element_type=f32
    )


def split3(value):
    high = value.astype(bf16)
    rest = value - high.astype(f32)
    middle = rest.astype(bf16)
    low = (rest - middle.astype(f32)).astype(bf16)
    return high, middle, low


def sinusoid_table(length, columns):
    positions = np.arange(length, dtype=np.float64)[:, None]
    column = np.arange(columns)
    angles = positions / np.power(10000.0, (2 * (column // 2)) / columns)[None, :]
    return np.where((column % 2)[None, :] == 0, np.sin(angles), np.cos(angles)).astype(np.float32)


def row_loop(total, body, carry, unroll=False):
    full = total // STEP

    def at_step(number, carry):
        return body(pl.ds(pl.multiple_of(number * STEP, STEP), STEP), carry)

    carry = lax.fori_loop(0, full, at_step, carry, unroll=unroll)
    if total % STEP:
        carry = body(pl.ds(full * STEP, total % STEP), carry)
    return carry


def own_lanes(head):
    lane = lax.broadcasted_iota(jnp.int32, (1, PAIR), 1)
    return (lane < HEAD) if head == 0 else (lane >= HEAD)


def column_sums(value):
    return jnp.sum(value, axis=0, keepdims=True)


def square_sum(ref):
    rows, columns = ref.shape
    size = 64

    def add(number, total):
        piece = ref[pl.ds(pl.multiple_of(number * size, size), size), :].astype(f32)
        sums = column_sums(piece * piece)
        for first in range(0, columns, PAIR):
            total = total + sums[:, first : first + PAIR]
        return total

    return lax.fori_loop(0, rows // size, add, jnp.zeros((1, PAIR), f32))


def lane_mean(value):
    return jnp.mean(value, axis=1, keepdims=True)


def forward_kernel(
    start_ref,
    x_ref,
    pos_ref,
    table_ref,
    w_proj_ref,
    b_proj_ref,
    mask_ref,
    gain1_ref,
    bias1_ref,
    w_qkv_ref,
    q_bias_ref,
    v_bias_ref,
    b_out_ref,
    gain2_ref,
    bias2_ref,
    b_fc1_ref,
    b_fc2_ref,
    w_out_hbm,
    w_fc1_hbm,
    w_fc2_hbm,
    cot_hbm,
    gs_ref,
    extra_ref,
    norms_ref,
    out_hbm,
    gmid_hbm,
    kept_hbm,
    sent_hbm,
    p_hbm,
    q_hbm,
    k_hbm,
    v_hbm,
    normed_hbm,
    xhat_hbm,
    rstd_hbm,
    p_s,
    q_s,
    k_s,
    v_s,
    normed_s,
    xhat_s,
    rstd_s,
    emb_s,
    middle_s,
    att_s,
    linv_s,
    attended_s,
    xhat2_s,
    rstd2_s,
    normed2_s,
    gn_s,
    vec_s,
    flat_s,
    out_s,
    w_out_s,
    w_fc1_s,
    w_fc2_s,
    cot_s,
    b_fc1_s,
    save_sems,
    p_sems,
    load_sems,
    end_sems,
    *,
    rows,
    clips,
):
    step = pl.program_id(0)
    half = kept_hbm.shape[0]

    def loads():
        pairs = [
            (w_out_hbm, w_out_s),
            (w_fc1_hbm, w_fc1_s),
            (w_fc2_hbm, w_fc2_s),
            (cot_hbm, cot_s),
        ]
        return [
            pltpu.make_async_copy(source, target, load_sems.at[index])
            for index, (source, target) in enumerate(pairs)
        ]

    def saves(number):
        pairs = [
            (q_s, q_hbm),
            (k_s, k_hbm),
            (v_s, v_hbm),
            (normed_s, normed_hbm),
            (xhat_s, xhat_hbm),
            (rstd_s, rstd_hbm),
        ]
        return [
            pltpu.make_async_copy(source, target.at[number], save_sems.at[index])
            for index, (source, target) in enumerate(pairs)
        ]

    def p_save(number):
        slot = lax.rem(number, SLOTS)
        at = lax.div(number, PAIRS)
        pair = lax.rem(number, PAIRS)
        return pltpu.make_async_copy(
            p_s.at[slot], p_hbm.at[at, pl.ds(2 * pair, 2)], p_sems.at[slot]
        )

    @pl.when(step == 0)
    def _():
        for copy in loads():
            copy.start()

    @pl.when(jnp.logical_and(step > 0, step < clips))
    def _():
        for copy in saves(step - 1):
            copy.wait()
        for number in range(PAIRS - 1):
            p_save(PAIRS * (step - 1) + number).wait()

    @pl.when(jnp.logical_and(step > 1, step < clips))
    def _():
        p_save(PAIRS * (step - 1) - 1).wait()

    @pl.when(step < clips)
    def _():
        projected = dot(x_ref[0], w_proj_ref[...]) + b_proj_ref[...][None, :]
        high, middle, low = split3(projected - mask_ref[...][None, :])
        row = lax.broadcasted_iota(jnp.int32, (LEN, 1), 0)
        onehot = (row == pos_ref[0]).astype(f32).astype(bf16)[:, : x_ref.shape[1]]
        emb_s[...] = (
            (table_ref[...].reshape(LEN, D) + mask_ref[...][None, :])
            + dot(onehot, low)
            + dot(onehot, middle)
        ) + dot(onehot, high)
        for number in range(LEN // STEP):
            at = slice(number * STEP, (number + 1) * STEP)
            value = emb_s[at, :]
            centered = value - lane_mean(value)
            rstd = lax.rsqrt(lane_mean(centered * centered) + 1e-05)
            xhat = centered * rstd
            xhat_s[at, :] = xhat.astype(bf16)
            normed_s[at, :] = (xhat * gain1_ref[...][None, :] + bias1_ref[...][None, :]).astype(
                bf16
            )
            rstd_s[at, :] = rstd
        group = pl.ds(pl.multiple_of(step * rows, 8), rows)
        middle_s[group, :] = emb_s[:rows, :]
        normed = normed_s[...]
        k_s[...] = dot(normed, w_qkv_ref[:, D : 2 * D]).astype(bf16)
        v_s[...] = (dot(normed, w_qkv_ref[:, 2 * D :]) + v_bias_ref[...][None, :]).astype(bf16)
        q_s[...] = (dot(normed[:rows], w_qkv_ref[:, :D]) + q_bias_ref[...][None, :]).astype(bf16)
        for copy in saves(step):
            copy.start()

        def attend(pair, carry):
            number = step * PAIRS + pair
            slot = lax.rem(number, SLOTS)
            at = pl.ds(pl.multiple_of(pair * PAIR, PAIR), PAIR)
            query = q_s[:, at]
            key = k_s[:, at]
            value = jnp.concatenate([v_s[:, at], jnp.ones((LEN, PAIR), bf16)], axis=1)
            first = own_lanes(0)
            none = jnp.zeros_like(query)
            both = [
                dot_rt(jnp.where(first, query, none), key),
                dot_rt(jnp.where(first, none, query), key),
            ]
            weights = []
            for head, scores in enumerate(both):
                largest = jnp.max(scores, axis=1, keepdims=True)
                scaled = (scores - largest) * (HEAD**-0.5 * np.log2(np.e))
                weights.append(jnp.exp2(scaled).astype(bf16))
                p_s[slot, head] = weights[head]
            parts = [dot(weight, value) for weight in weights]
            inverse = 1.0 / jnp.where(first, parts[0][:, PAIR:], parts[1][:, PAIR:])
            linv_s[group, at] = inverse
            att_s[group, at] = jnp.where(first, parts[0][:, :PAIR], parts[1][:, :PAIR]) * inverse
            p_save(number).start()
            return carry

        lax.fori_loop(0, PAIRS, attend, 0, unroll=UNROLL_F)

    @pl.when(step == 0)
    def _():
        norms_ref[...] = jnp.zeros_like(norms_ref)
        norms_ref[0:1, :] = square_sum(w_proj_ref)
        norms_ref[4:5, :] = square_sum(w_qkv_ref)
        b_fc1_s[...] = b_fc1_ref[...][None, :]

    @pl.when(step == clips)
    def _():
        for copy in loads():
            copy.wait()
        attended_s[...] = att_s[...].astype(bf16)
        gn_s[...] = dot(attended_s[...], w_out_s[...])

        def norm_middle(at, carry):
            middle = middle_s[at, :] + (gn_s[at, :] + b_out_ref[...][None, :])
            centered = middle - lane_mean(middle)
            rstd = lax.rsqrt(lane_mean(centered * centered) + 1e-05)
            xhat = centered * rstd
            xhat2_s[at, :] = xhat
            rstd2_s[at, :] = rstd
            normed2_s[at, :] = (
                xhat * gain2_ref[...][None, :] + bias2_ref[...][None, :]
            ).astype(bf16)
            middle_s[at, :] = middle + b_fc2_ref[...][None, :]
            gn_s[at, :] = jnp.zeros(middle.shape, f32)
            return carry

        row_loop(clips * rows, norm_middle, 0, unroll=True)
        norms_ref[1:2, :] = square_sum(w_out_s)
        norms_ref[2:3, :] = square_sum(w_fc1_s)
        norms_ref[3:4, :] = square_sum(w_fc2_s)
        flat_s[FC_USED - 24 :, :] = jnp.zeros_like(flat_s[FC_USED - 24 :, :])

        def hidden_block(block, carry):
            normed2 = normed2_s[...]
            cot = cot_s[...]
            at = pl.ds(pl.multiple_of(block * BLOCK, BLOCK), BLOCK)
            w_fc1 = w_fc1_s[:, at]
            w_fc2 = w_fc2_s[at, :]
            pre = dot(normed2, w_fc1) + b_fc1_s[:, at]
            grad_hidden = dot_rt(cot, w_fc2)
            cdf = 0.5 + 0.5 * lax.erf(pre * np.float32(0.5**0.5))
            hidden = (pre * cdf).astype(bf16)
            slope = cdf + pre * (
                jnp.exp2(pre * pre * (-0.5 * np.log2(np.e))) * ((2 * np.pi) ** -0.5)
            )
            grad_pre = grad_hidden * slope
            grad_pre_b = grad_pre.astype(bf16)
            middle_s[...] += dot(hidden, w_fc2)
            gn_s[...] += dot_rt(grad_pre_b, w_fc1)
            grad_w2 = dot_lt(hidden, cot).astype(bf16)
            for column in range(D // PAIR):
                first = FF * PAIRS + column * FF + block * BLOCK
                flat_s[pl.ds(pl.multiple_of(first, 16), BLOCK), :] = grad_w2[
                    :, column * PAIR : (column + 1) * PAIR
                ]
            grad_w1 = dot_lt(normed2, grad_pre_b).astype(bf16)
            sums = column_sums(grad_pre_b.astype(f32))
            for piece in range(BLOCK // PAIR):
                lanes = slice(piece * PAIR, (piece + 1) * PAIR)
                number = block * (BLOCK // PAIR) + piece
                flat_s[pl.ds(pl.multiple_of(number * D, 16), D), :] = grad_w1[:, lanes]
                row = 8 * lax.rem(number, PAIRS) + lax.div(number, PAIRS)
                vec_s[pl.ds(row, 1), :] = sums[:, lanes]
            return carry

        lax.fori_loop(0, BLOCKS, hidden_block, 0, unroll=UNROLL_M)
        out_s[...] = middle_s[...].astype(bf16)
        ends = [pltpu.make_async_copy(out_s, out_hbm, end_sems.at[0])]
        ends[0].start()

        def norm_back(at, carry):
            cot_f = cot_s[at, :].astype(f32)
            grad_normed = gn_s[at, :]
            xhat = xhat2_s[at, :]
            scaled = grad_normed * gain2_ref[...][None, :]
            grad_middle = cot_f + rstd2_s[at, :] * (
                scaled - lane_mean(scaled) - xhat * lane_mean(scaled * xhat)
            )
            middle_s[at, :] = grad_middle
            grad_branch = grad_middle.astype(bf16)
            normed2_s[at, :] = grad_branch
            terms = [cot_f, grad_normed * xhat, grad_normed, grad_branch.astype(f32)]
            return tuple(total + column_sums(term) for total, term in zip(carry, terms))

        zero = jnp.zeros((1, D), f32)
        vectors = row_loop(clips * rows, norm_back, (zero,) * 4, unroll=True)
        ends.append(pltpu.make_async_copy(middle_s, gmid_hbm, end_sems.at[1]))
        ends[1].start()
        grad_branch = normed2_s[...]
        grad_out = dot_lt(attended_s[...], grad_branch).astype(bf16)
        for column in range(D // PAIR):
            lanes = slice(column * PAIR, (column + 1) * PAIR)
            first = 2 * FF * PAIRS + column * D
            flat_s[first : first + D, :] = grad_out[:, lanes]
            for number, vector in enumerate(vectors):
                row = 8 * column + 4 + number
                vec_s[row : row + 1, :] = vector[:, lanes]
        flat_s[FC_USED - 24 : FC_USED, :] = vec_s[...].astype(bf16)
        bit = start_ref[1]
        for index, (side, target) in enumerate([(bit, kept_hbm), (1 - bit, sent_hbm)]):
            copy = pltpu.make_async_copy(
                flat_s.at[pl.ds(pl.multiple_of(side * half, 16), half)],
                target,
                end_sems.at[2 + index],
            )
            copy.start()
            ends.append(copy)
        gn_s[...] = dot_rt(grad_branch, w_out_s[...])

        def inner_products(at, carry):
            grad_att = gn_s[at, :].astype(bf16).astype(f32)
            grad_s = (grad_att * linv_s[at, :]).astype(bf16)
            gs_ref[at, :] = grad_s
            product = grad_s.astype(f32) * att_s[at, :]
            lane = lax.broadcasted_iota(jnp.int32, (1, PAIR), 1)
            packed = jnp.zeros((product.shape[0], PAIR), f32)
            for pair in range(PAIRS):
                piece = product[:, pair * PAIR : (pair + 1) * PAIR]
                for head in range(2):
                    inner = -jnp.sum(
                        jnp.where(own_lanes(head), piece, 0.0), axis=1, keepdims=True
                    )
                    for index, term in enumerate(split3(inner)):
                        where = 3 * (2 * pair + head) + index
                        packed = jnp.where(lane == where, term.astype(f32), packed)
            extra_ref[at, :] = packed.astype(bf16)
            return carry

        row_loop(clips * rows, inner_products, 0, unroll=True)
        for copy in ends + saves(clips - 1):
            copy.wait()
        for number in range(PAIRS * clips - PAIRS - 1, PAIRS * clips):
            p_save(number).wait()


def backward_kernel(
    start_ref,
    q_ref,
    k_ref,
    v_ref,
    gs_ref,
    extra_ref,
    pos_ref,
    gain1_ref,
    w_qkv_hbm,
    x_hbm,
    p_hbm,
    normed_hbm,
    xhat_hbm,
    rstd_hbm,
    gmid_hbm,
    *rest,
    rows,
    base,
    count,
    last,
):
    if last:
        acc_hbm, dq_hbm, dkv_hbm, kept_ref, sent_ref, proj_kept_ref, proj_sent_ref = rest[:7]
        scratch = rest[7:]
    else:
        proj_kept_ref, proj_sent_ref, acc_hbm, dq_hbm, dkv_hbm = rest[:5]
        scratch = rest[5:]
    (p_s, normed_s, xhat_s, rstd_s, own_s, dq_s, dkv_s, gn_s, high_s, low_s, proj_s) = scratch[-18:-7]
    w_qkv_s, x_s, acc_s, hand_sems, w_sem, sems, p_sems = scratch[-7:]
    if last:
        q_s, k_s, v_s, late_sems = scratch[:4]
        late = [
            pltpu.make_async_copy(source.at[pl.ds(base, 1)], target, late_sems.at[index])
            for index, (source, target) in enumerate(
                [(q_ref, q_s), (k_ref, k_s), (v_ref, v_s)]
            )
        ]
        q_ref, k_ref, v_ref = q_s, k_s, v_s
    step = pl.program_id(0)
    lane = lax.broadcasted_iota(jnp.int32, (1, PAIR), 1)
    first_post = base - 1 if last else base

    def loads():
        at = first_post + step
        pairs = [
            (normed_hbm.at[at], normed_s),
            (xhat_hbm.at[at], xhat_s),
            (rstd_hbm.at[at], rstd_s),
            (x_hbm.at[at], x_s),
            (gmid_hbm.at[pl.ds(pl.multiple_of(at * rows, 8), rows)], own_s.at[pl.ds(0, rows)]),
        ]
        return [
            pltpu.make_async_copy(source, target, sems.at[index])
            for index, (source, target) in enumerate(pairs)
        ]

    def hand(number):
        pairs = [(acc_s, acc_hbm), (dq_s, dq_hbm), (dkv_s, dkv_hbm)]
        inside, outside = pairs[number]
        if last:
            return pltpu.make_async_copy(outside, inside, hand_sems.at[number])
        return pltpu.make_async_copy(inside, outside, hand_sems.at[number])

    def p_load(number):
        at = lax.div(number, PAIRS)
        pair = lax.rem(number, PAIRS)
        slot = lax.rem(number, 2 * PAIRS)
        return pltpu.make_async_copy(
            p_hbm.at[base + at, pl.ds(2 * pair, 2)], p_s.at[slot], p_sems.at[slot]
        )

    w_load = pltpu.make_async_copy(w_qkv_hbm, w_qkv_s, w_sem)
    has_post = True if last else step < count - 1

    if last:
        for number in (2, 1):
            pl.when(step == 0)(hand(number).start)

    @pl.when(step == 0)
    def _():
        if not last:
            for pair in range(PAIRS):
                p_load(pair).start()
        w_load.start()

    @pl.when(has_post)
    def _():
        for copy in loads():
            copy.start()

    @pl.when(step == 0)
    def _():
        own_s[rows:, :] = jnp.zeros_like(own_s[rows:, :])
        if last:
            hand(0).start()
            for copy in late:
                copy.start()
            for pair in range(PAIRS):
                p_load(pair).start()
        else:

            def clear(number, carry):
                at = pl.ds(pl.multiple_of(number * 256, 256), 256)
                acc_s[at, :] = jnp.zeros((256, PAIR), f32)
                return carry

            lax.fori_loop(0, acc_s.shape[0] // 256, clear, 0)

    def attend_back(phase, carry):
        number = phase if last else step * PAIRS + phase
        slot = lax.rem(number, 2 * PAIRS)
        p_load(number).wait()
        at = pl.ds(pl.multiple_of(phase * PAIR, PAIR), PAIR)
        query = q_ref[0, :, at] * jnp.asarray(HEAD**-0.5, bf16)
        key = k_ref[0, :, at]
        value = jnp.concatenate([v_ref[0, :, at], jnp.ones((LEN, PAIR), bf16)], axis=1)
        grad = gs_ref[:, at]
        extra = extra_ref[...]
        products = []
        for head in range(2):
            first = 3 * (2 * phase + head)
            inner = jnp.logical_and(lane >= first, lane < first + 3)
            left = jnp.concatenate(
                [
                    jnp.where(own_lanes(head), grad, jnp.zeros_like(grad)),
                    jnp.where(inner, extra, jnp.zeros_like(extra)),
                ],
                axis=1,
            )
            products.append(dot_rt(left, value))
        weights = [p_s[slot, head] for head in range(2)]
        scores = [
            (weight.astype(f32) * product).astype(bf16)
            for weight, product in zip(weights, products)
        ]
        values = [dot_lt(weight, grad) for weight in weights]
        keys = [dot_lt(score, query) for score in scores]
        queries = [dot(score, key) for score in scores]
        side = own_lanes(0)
        dq_s[:, at] = (jnp.where(side, queries[0], queries[1]) * (HEAD**-0.5)).astype(bf16)
        dkv_s[:, at] = jnp.where(side, keys[0], keys[1]).astype(bf16)
        at = pl.ds(pl.multiple_of(phase * PAIR + D, PAIR), PAIR)
        dkv_s[:, at] = jnp.where(side, values[0], values[1]).astype(bf16)
        return carry

    if last:

        @pl.when(step == 1)
        def _():
            for copy in late:
                copy.wait()
            lax.fori_loop(0, PAIRS, attend_back, 0)

    else:
        lax.fori_loop(0, PAIRS, attend_back, 0)

        @pl.when(step + 1 < count)
        def _():
            for pair in range(PAIRS):
                p_load(PAIRS * (step + 1) + pair).start()

    @pl.when(step == 0)
    def _():
        w_load.wait()
        if last:
            hand(1).wait()
            hand(2).wait()

    @pl.when(has_post)
    def _():
        grad_q = dq_s[...]
        grad_kv = dkv_s[...]
        gn_s[...] = dot_rt(grad_kv, w_qkv_s[:, D:])
        gn_s[:rows, :] += dot_rt(grad_q, w_qkv_s[:, :D])
        for copy in loads():
            copy.wait()
        if last:

            @pl.when(step == 0)
            def _():
                hand(0).wait()

        normed = normed_s[...]
        part_q = dot_lt(normed[:rows], grad_q)
        part_kv = dot_lt(normed, grad_kv)
        for index in range(PAIRS):
            acc_s[index * D : (index + 1) * D, :] += part_q[:, index * PAIR : (index + 1) * PAIR]
        for index in range(2 * PAIRS):
            first = (PAIRS + index) * D
            acc_s[first : first + D, :] += part_kv[:, index * PAIR : (index + 1) * PAIR]
        ones = jnp.ones((8, LEN), bf16)
        sum_q = dot(ones[:, :rows], grad_q)[:1]
        sum_v = dot(ones, grad_kv[:, D:])[:1]

        def norm_rows(number, carry, with_own):
            at = pl.ds(pl.multiple_of(number * STEP, STEP), STEP)
            sum_gain, sum_bias, sum_emb = carry
            value = gn_s[at, :]
            xhat = xhat_s[at, :].astype(f32)
            sum_bias = sum_bias + column_sums(value)
            sum_gain = sum_gain + column_sums(value * xhat)
            scaled = value * gain1_ref[...][None, :]
            grad = rstd_s[at, :] * (
                scaled - lane_mean(scaled) - xhat * lane_mean(scaled * xhat)
            )
            if with_own:
                grad = grad + own_s[at, :]
            sum_emb = sum_emb + column_sums(grad)
            high = grad.astype(bf16)
            high_s[at, :] = high
            low_s[at, :] = (grad - high.astype(f32)).astype(bf16)
            return sum_gain, sum_bias, sum_emb

        zero = jnp.zeros((1, D), f32)
        own_steps = own_s.shape[0] // STEP
        carry = lax.fori_loop(
            0, own_steps, functools.partial(norm_rows, with_own=True), (zero, zero, zero), unroll=True
        )
        sum_gain, sum_bias, sum_emb = lax.fori_loop(
            own_steps, LEN // STEP, functools.partial(norm_rows, with_own=False), carry, unroll=True
        )
        row = lax.broadcasted_iota(jnp.int32, (LEN, 1), 0)
        onehot = (row == pos_ref[0]).astype(f32).astype(bf16)
        grad_proj = dot_lt(onehot, high_s[...]) + dot_lt(onehot, low_s[...])
        proj_s[...] = grad_proj
        bit = start_ref[1]
        part = SLOT // 2
        proj_kept_ref[0] = proj_s[pl.ds(pl.multiple_of(bit * part, 8), part), :]
        proj_sent_ref[0] = proj_s[
            pl.ds(pl.multiple_of((1 - bit) * part, 8), part), :
        ].astype(bf16)
        sum_proj = column_sums(grad_proj)
        vectors = [sum_proj, sum_emb - sum_proj, sum_gain, sum_bias, sum_q, sum_v]
        weight = dot_lt(x_s[...], grad_proj[: x_s.shape[0]].astype(bf16))
        for index in range(D // PAIR):
            lanes = slice(index * PAIR, (index + 1) * PAIR)
            first = 3 * PAIRS * D + index * DIN
            acc_s[first : first + DIN, :] += weight[:, lanes]
            first = 3 * PAIRS * D + PAIRS * DIN + 8 * index
            for number, vector in enumerate(vectors):
                acc_s[first + number : first + number + 1, :] += vector[:, lanes]

    if last:

        @pl.when(step == 1)
        def _():
            bit = start_ref[1]
            half = kept_ref.shape[0]

            def hand_over(number, carry):
                at = pl.ds(pl.multiple_of(number * 256, 256), 256)
                kept_at = pl.ds(pl.multiple_of(bit * half + number * 256, 256), 256)
                sent_at = pl.ds(pl.multiple_of((1 - bit) * half + number * 256, 256), 256)
                kept_ref[at, :] = acc_s[kept_at, :].astype(bf16)
                sent_ref[at, :] = acc_s[sent_at, :].astype(bf16)
                return carry

            lax.fori_loop(0, half // 256, hand_over, 0)

    else:
        pl.when(step == count - 2)(hand(0).start)

        @pl.when(step == count - 1)
        def _():
            hand(1).start()
            hand(2).start()
            for number in range(3):
                hand(number).wait()


def place(target, lanes, source, where, total):
    size = target.shape[0]
    step = 96

    def move(number, total):
        first = pl.multiple_of(number * step, 16)
        value = source[pl.ds(pl.multiple_of(where + first, 16), step), :].astype(f32)
        target[pl.ds(first, step), lanes] = value
        return total + jnp.sum((value * value).reshape(step // 8, 8, PAIR), axis=0)

    return lax.fori_loop(0, size // step, move, total, unroll=2)


def lanes_of(index):
    return slice(index * PAIR, (index + 1) * PAIR)


def whole_mean(total, size):
    value = jnp.sum(jnp.sum(total, axis=1, keepdims=True), axis=0, keepdims=True)
    return value / size


def assemble_fc_kernel(
    start_ref,
    mine_hbm,
    other_hbm,
    w_out_ref,
    w_fc1_ref,
    w_fc2_ref,
    b_out_ref,
    gain_ref,
    bias_ref,
    b_fc1_ref,
    b_fc2_ref,
    mean_ref,
    full_s,
    sems,
):
    half = mine_hbm.shape[0]
    bit = start_ref[1]
    copies = [
        pltpu.make_async_copy(
            source, full_s.at[pl.ds(pl.multiple_of(side * half, 16), half)], sems.at[index]
        )
        for index, (source, side) in enumerate([(mine_hbm, bit), (other_hbm, 1 - bit)])
    ]
    for copy in copies:
        copy.start()
    for copy in copies:
        copy.wait()

    total = jnp.zeros((8, PAIR), f32)
    for index in range(PAIRS):
        total = place(w_out_ref, lanes_of(index), full_s, 2 * FF * PAIRS + index * D, total)
    mean_out = whole_mean(total, D * D)
    total = jnp.zeros((8, PAIR), f32)
    for index in range(FF // PAIR):
        total = place(w_fc1_ref, lanes_of(index), full_s, index * D, total)
    mean_fc1 = whole_mean(total, D * FF)
    total = jnp.zeros((8, PAIR), f32)
    for index in range(PAIRS):
        total = place(w_fc2_ref, lanes_of(index), full_s, FF * PAIRS + index * FF, total)
    mean_fc2 = whole_mean(total, FF * D)
    first = 2 * FF * PAIRS + PAIRS * D
    vectors = full_s[first : first + 24, :].astype(f32)
    for index in range(PAIRS):
        lanes = lanes_of(index)
        for number in range(4):
            b_fc1_ref[number * D + index * PAIR : number * D + (index + 1) * PAIR] = vectors[
                8 * index + number
            ]
        for number, target in enumerate([b_fc2_ref, gain_ref, bias_ref, b_out_ref]):
            target[lanes] = vectors[8 * index + 4 + number]
    row = lax.broadcasted_iota(jnp.int32, (8, PAIR), 0)
    mean_ref[...] = jnp.where(
        row == 1, mean_out, jnp.where(row == 2, mean_fc1, mean_fc2)
    )


def assemble_qkv_kernel(
    start_ref,
    *refs,
    far,
    chunk,
):
    planes = refs[:8]
    (
        norms_ref,
        mean_ref,
        w_proj_ref,
        w_qkv_ref,
        b_proj_ref,
        mask_ref,
        gain_ref,
        bias_ref,
        q_bias_ref,
        v_bias_ref,
        trust_ref,
        trust_qkv_ref,
        full_s,
        sems,
    ) = refs[8:]
    half = 4 * far * chunk
    bit = start_ref[1]
    copies = []
    for side in range(2):
        for plane in range(4):
            for line in range(far):
                place_at = jnp.bitwise_xor(start_ref[2], plane * far + line) * chunk
                place_at = place_at + (bit if side == 0 else 1 - bit) * half
                copies.append(
                    pltpu.make_async_copy(
                        planes[4 * side + plane].at[pl.ds(line * chunk, chunk)],
                        full_s.at[pl.ds(pl.multiple_of(place_at, 16), chunk)],
                        sems.at[len(copies)],
                    )
                )
    for copy in copies:
        copy.start()
    for copy in copies:
        copy.wait()

    total = jnp.zeros((8, PAIR), f32)
    for index in range(PAIRS):
        total = place(w_proj_ref, lanes_of(index), full_s, 3 * PAIRS * D + index * DIN, total)
    mean_proj = whole_mean(total, DIN * D)
    total = jnp.zeros((8, PAIR), f32)
    for index in range(3 * PAIRS):
        total = place(w_qkv_ref, lanes_of(index), full_s, index * D, total)
    mean_qkv = whole_mean(total, D * 3 * D)
    first = 3 * PAIRS * D + PAIRS * DIN
    vectors = full_s[first : first + 24, :].astype(f32)
    targets = [b_proj_ref, mask_ref, gain_ref, bias_ref, q_bias_ref, v_bias_ref]
    for index in range(PAIRS):
        for number, target in enumerate(targets):
            target[lanes_of(index)] = vectors[8 * index + number]
    lane = lax.broadcasted_iota(jnp.int32, (1, PAIR), 1)
    means = [mean_proj, mean_ref[1:2], mean_ref[2:3], mean_ref[3:4], mean_qkv]
    sums = jnp.sum(norms_ref[...], axis=1, keepdims=True)
    sizes = [DIN * D, D * D, D * FF, FF * D, D * 3 * D]
    grads = jnp.ones((1, PAIR), f32)
    weights = jnp.ones((1, PAIR), f32)
    for index, (mean, size) in enumerate(zip(means, sizes)):
        grads = jnp.where(lane == index, mean, grads)
        weights = jnp.where(lane == index, sums[index : index + 1] / size, weights)
    ratios = jnp.sqrt(weights) / jnp.sqrt(grads + 1e-06)
    trust_ref[...] = ratios[0, :4]
    trust_qkv_ref[...] = ratios[0, 4:5]


def whole(shape):
    return pl.BlockSpec(shape, lambda i, s: (0,) * len(shape), pipeline_mode=pl.Buffered(1))


def shape_of(shape, dtype):
    return jax.ShapeDtypeStruct(shape, dtype)


def kernel_call(kernel, grid, in_specs, out_specs, out_shape, scratch, name, cost, args):
    return pl.pallas_call(
        kernel,
        grid_spec=pltpu.PrefetchScalarGridSpec(
            num_scalar_prefetch=1,
            grid=grid,
            in_specs=in_specs,
            out_specs=out_specs,
            scratch_shapes=scratch,
        ),
        out_shape=out_shape,
        compiler_params=pltpu.CompilerParams(
            dimension_semantics=("arbitrary",), vmem_limit_bytes=VMEM
        ),
        cost_estimate=pl.CostEstimate(
            flops=cost[0], bytes_accessed=cost[1], transcendentals=cost[2]
        ),
        name=name,
    )(*args)


def run_forward(start, x_vis, padded_pos, table, params, cotangent, rows, half):
    clips, visible, _ = x_vis.shape
    (
        w_proj,
        b_proj,
        mask_token,
        ln1_gain,
        ln1_bias,
        w_qkv,
        q_bias,
        v_bias,
        w_out,
        b_out,
        ln2_gain,
        ln2_bias,
        w_fc1,
        b_fc1,
        w_fc2,
        b_fc2,
    ) = params
    tokens = clips * rows
    any_space = pl.BlockSpec(memory_space=pl.ANY)
    vector = whole((D,))

    def clip_at(i):
        return jnp.minimum(i, clips - 1)

    in_specs = [
        pl.BlockSpec((1, visible, DIN), lambda i, s: (clip_at(i), 0, 0)),
        pl.BlockSpec((1, 1, SLOT), lambda i, s: (clip_at(i), 0, 0)),
        pl.BlockSpec(
            (pl.Element(LEN // 8), pl.Element(8), pl.Element(D)),
            lambda i, s: (s[0], 0, 0),
            pipeline_mode=pl.Buffered(1),
        ),
        whole((DIN, D)),
        vector,
        vector,
        vector,
        vector,
        whole((D, 3 * D)),
        vector,
        vector,
        vector,
        vector,
        vector,
        whole((FF,)),
        vector,
    ] + [any_space] * 4
    out_specs = [whole((tokens, D)), whole((tokens, PAIR)), whole((8, PAIR))] + [any_space] * 11
    out_shape = [
        shape_of((tokens, D), bf16),
        shape_of((tokens, PAIR), bf16),
        shape_of((8, PAIR), f32),
        shape_of((tokens, D), bf16),
        shape_of((tokens, D), f32),
        shape_of((half, PAIR), bf16),
        shape_of((half, PAIR), bf16),
        shape_of((clips, HEADS, rows, LEN), bf16),
        shape_of((clips, rows, D), bf16),
        shape_of((clips, LEN, D), bf16),
        shape_of((clips, LEN, D), bf16),
        shape_of((clips, LEN, D), bf16),
        shape_of((clips, LEN, D), bf16),
        shape_of((clips, LEN, 1), f32),
    ]
    scratch = [
        pltpu.VMEM((SLOTS, 2, rows, LEN), bf16),
        pltpu.VMEM((rows, D), bf16),
        pltpu.VMEM((LEN, D), bf16),
        pltpu.VMEM((LEN, D), bf16),
        pltpu.VMEM((LEN, D), bf16),
        pltpu.VMEM((LEN, D), bf16),
        pltpu.VMEM((LEN, 1), f32),
        pltpu.VMEM((LEN, D), f32),
        pltpu.VMEM((tokens, D), f32),
        pltpu.VMEM((tokens, D), f32),
        pltpu.VMEM((tokens, D), f32),
        pltpu.VMEM((tokens, D), bf16),
        pltpu.VMEM((tokens, D), f32),
        pltpu.VMEM((tokens, 1), f32),
        pltpu.VMEM((tokens, D), bf16),
        pltpu.VMEM((tokens, D), f32),
        pltpu.VMEM((24, PAIR), f32),
        pltpu.VMEM((2 * half, PAIR), bf16),
        pltpu.VMEM((tokens, D), bf16),
        pltpu.VMEM((D, D), bf16),
        pltpu.VMEM((D, FF), bf16),
        pltpu.VMEM((FF, D), bf16),
        pltpu.VMEM((tokens, D), bf16),
        pltpu.VMEM((1, FF), f32),
        pltpu.SemaphoreType.DMA((6,)),
        pltpu.SemaphoreType.DMA((SLOTS,)),
        pltpu.SemaphoreType.DMA((4,)),
        pltpu.SemaphoreType.DMA((4,)),
    ]
    return kernel_call(
        functools.partial(forward_kernel, rows=rows, clips=clips),
        (clips + 1,),
        in_specs,
        out_specs,
        out_shape,
        scratch,
        "forward",
        (40_000_000_000, 60_000_000, 13_000_000),
        (
            start,
            x_vis,
            padded_pos,
            table,
            w_proj,
            b_proj,
            mask_token,
            ln1_gain,
            ln1_bias,
            w_qkv,
            q_bias,
            v_bias,
            b_out,
            ln2_gain,
            ln2_bias,
            b_fc1,
            b_fc2,
            w_out,
            w_fc1,
            w_fc2,
            cotangent.reshape(tokens, D),
        ),
    )


def run_backward(start, saved, x_vis, padded_pos, w_qkv, ln1_gain, rows, half, base, count, handed):
    query, key, value, grads, extra, weights, normed, xhat, rstd, gmid = saved
    _, visible, _ = x_vis.shape
    last = handed is not None
    own_rows = -(-rows // STEP) * STEP
    any_space = pl.BlockSpec(memory_space=pl.ANY)
    posts = count + 1 if last else count - 1

    def at(i):
        return base if last else i

    def block(*shape):
        return pl.BlockSpec((1,) + shape, lambda i, s: (at(i),) + (0,) * len(shape))

    proj_spec = pl.BlockSpec(
        (1, SLOT // 2, D), lambda i, s: (jnp.minimum(i, posts - 1), 0, 0)
    )
    proj_shapes = [
        shape_of((posts, SLOT // 2, D), f32),
        shape_of((posts, SLOT // 2, D), bf16),
    ]
    hand_shapes = [
        shape_of((2 * half, PAIR), f32),
        shape_of((rows, D), bf16),
        shape_of((LEN, 2 * D), bf16),
    ]
    in_specs = [
        block(rows, D),
        block(LEN, D),
        block(LEN, D),
        pl.BlockSpec((rows, D), lambda i, s: (at(i), 0)),
        pl.BlockSpec((rows, PAIR), lambda i, s: (at(i), 0)),
        pl.BlockSpec((1, 1, SLOT), lambda i, s: (base - 1 + i if last else i, 0, 0)),
        whole((D,)),
    ] + [any_space] * 7
    args = [
        start,
        query,
        key,
        value,
        grads,
        extra,
        padded_pos,
        ln1_gain,
        w_qkv,
        x_vis,
        weights,
        normed,
        xhat,
        rstd,
        gmid,
    ]
    scratch = [
        pltpu.VMEM((2 * PAIRS, 2, rows, LEN), bf16),
        pltpu.VMEM((LEN, D), bf16),
        pltpu.VMEM((LEN, D), bf16),
        pltpu.VMEM((LEN, 1), f32),
        pltpu.VMEM((own_rows, D), f32),
        pltpu.VMEM((rows, D), bf16),
        pltpu.VMEM((LEN, 2 * D), bf16),
        pltpu.VMEM((LEN, D), f32),
        pltpu.VMEM((LEN, D), bf16),
        pltpu.VMEM((LEN, D), bf16),
        pltpu.VMEM((SLOT, D), f32),
        pltpu.VMEM((D, 3 * D), bf16),
        pltpu.VMEM((visible, DIN), bf16),
        pltpu.VMEM((2 * half, PAIR), f32),
        pltpu.SemaphoreType.DMA((3,)),
        pltpu.SemaphoreType.DMA,
        pltpu.SemaphoreType.DMA((5,)),
        pltpu.SemaphoreType.DMA((2 * PAIRS,)),
    ]
    if last:
        in_specs[:3] = [any_space] * 3
        scratch = [
            pltpu.VMEM((1, rows, D), bf16),
            pltpu.VMEM((1, LEN, D), bf16),
            pltpu.VMEM((1, LEN, D), bf16),
            pltpu.SemaphoreType.DMA((3,)),
        ] + scratch
        in_specs += [any_space] * 3
        args += handed
        out_specs = [whole((half, PAIR)), whole((half, PAIR)), proj_spec, proj_spec]
        out_shape = [shape_of((half, PAIR), bf16), shape_of((half, PAIR), bf16)] + proj_shapes
    else:
        out_specs = [proj_spec, proj_spec] + [any_space] * 3
        out_shape = proj_shapes + hand_shapes
    return kernel_call(
        functools.partial(backward_kernel, rows=rows, base=base, count=count, last=last),
        (posts if last else count,),
        in_specs,
        out_specs,
        out_shape,
        scratch,
        "backward",
        (16_000_000_000 * count, 20_000_000 * count, 0),
        tuple(args),
    )


def run_assemble_fc(start, mine, other):
    half = mine.shape[0]
    shapes = [(D, D), (D, FF), (FF, D), (D,), (D,), (D,), (FF,), (D,), (8, PAIR)]
    return kernel_call(
        assemble_fc_kernel,
        (1,),
        [pl.BlockSpec(memory_space=pl.ANY)] * 2,
        [whole(size) for size in shapes],
        [shape_of(size, f32) for size in shapes],
        [pltpu.VMEM((2 * half, PAIR), bf16), pltpu.SemaphoreType.DMA((2,))],
        "assemble_fc",
        (10_000_000, 8_000_000, 0),
        (start, mine, other),
    )


def run_assemble_qkv(start, planes, norms, means, far, chunk):
    any_space = pl.BlockSpec(memory_space=pl.ANY)
    shapes = [(DIN, D), (D, 3 * D), (D,), (D,), (D,), (D,), (D,), (D,), (4,), (1,)]
    return kernel_call(
        functools.partial(assemble_qkv_kernel, far=far, chunk=chunk),
        (1,),
        [any_space] * 8 + [whole((8, PAIR)), whole((8, PAIR))],
        [whole(size) for size in shapes],
        [shape_of(size, f32) for size in shapes],
        [
            pltpu.VMEM((8 * far * chunk, PAIR), bf16),
            pltpu.SemaphoreType.DMA((8 * far,)),
        ],
        "assemble_qkv",
        (10_000_000, 5_000_000, 0),
        (start, *planes, norms, means),
    )


def add_received(kept, received):
    return kept.astype(f32) + received.astype(f32)


def shards(x_vis, vis_pos, *rest):
    params, cotangent = rest[:-1], rest[-1]
    w_proj, ln1_gain, w_qkv = params[0], params[3], params[5]
    seq_size = lax.axis_size("seq")
    clip_size = lax.axis_size("clip")
    groups = seq_size * clip_size // 2
    rows = LEN // seq_size
    clips, visible, _ = x_vis.shape
    far = clip_size // 2
    members = [
        [
            s * clip_size + 2 * high + low
            for s in range(core, seq_size, 2)
            for low in range(2)
            for high in range(far)
        ]
        for core in range(2)
    ]

    def chunk_rows(used):
        return -(-used // (32 * groups)) * 16

    core_pairs = [(s, s ^ 1) for s in range(seq_size)]
    chip_pairs = [(s, s ^ 2) for s in range(seq_size)]

    def across_core(value):
        return lax.ppermute(value, "seq", core_pairs)

    def swap(value):
        chunks = value.reshape(groups, -1, PAIR)
        return lax.all_to_all(chunks, AXES, 0, 0, axis_index_groups=members)

    def total_of(chunks):
        return jnp.sum(chunks.astype(f32), axis=0).astype(bf16)

    def spread(chunk, size):
        return jnp.broadcast_to(chunk[None], (size,) + chunk.shape)

    def across(value, seq_change, low_change, high_change):
        pairs = []
        for s in range(seq_size):
            for c in range(clip_size):
                other = (s ^ (2 * seq_change)) * clip_size + (c ^ (2 * high_change + low_change))
                pairs.append((s * clip_size + c, other))
        return lax.ppermute(value, AXES, pairs)

    def parts_of(arrays, index, count):
        size = arrays[0].shape[0] // count
        result = []
        for k in range(count):
            first = jnp.bitwise_xor(index, k) * size
            pieces = [lax.dynamic_slice_in_dim(value, first, size, 0) for value in arrays]
            total = pieces[0].astype(f32)
            for piece in pieces[1:]:
                total = total + piece.astype(f32)
            result.append(total if k == 0 else total.astype(bf16))
        return result

    def scatter(kept, received, beside):
        x, y, high = seq_index >> 1, clip_index & 1, clip_index >> 1
        own, *others = parts_of([kept, received], 2 * x + y, 4)
        arrays = [own] + [
            across(value, k >> 1, k & 1, 0) for k, value in enumerate(others, 1)
        ]
        arrays, beside = lax.optimization_barrier((arrays, beside))
        size = far
        while size > 1:
            count = 2 if size == 2 or (size.bit_length() % 2 == 0) else 4
            size //= count
            own, *others = parts_of(arrays, (high // size) % count, count)
            arrays = [own] + [
                across(value, 0, 0, size * k) for k, value in enumerate(others, 1)
            ]
        total = arrays[0]
        for value in arrays[1:]:
            total = total + value.astype(f32)
        return total.astype(bf16), beside

    def gather(chunk):
        size = 1
        while size < far:
            count = min(4, far // size)
            chunk = jnp.concatenate(
                [chunk] + [across(chunk, 0, 0, size * k) for k in range(1, count)]
            )
            size *= count
        return [chunk] + [across(chunk, k >> 1, k & 1, 0) for k in (1, 2, 3)]

    fc_chunk = chunk_rows(FC_USED)
    qkv_chunk = chunk_rows(QKV_USED)
    qkv_half = qkv_chunk * groups
    seq_index = lax.axis_index("seq")
    clip_index = lax.axis_index("clip")
    bit = seq_index & 1
    first = seq_index * rows
    local_pos = jnp.where(vis_pos >= first, vis_pos - first, vis_pos - first + LEN)
    padded_pos = jnp.pad(local_pos, ((0, 0), (0, SLOT - visible)), constant_values=-1)[:, None, :]
    table = sinusoid_table(LEN, D)
    table = jnp.asarray(np.concatenate([table, table[: LEN - rows]]).reshape(-1, 8, D))
    number = ((seq_index >> 1) * 2 + (clip_index & 1)) * far + (clip_index >> 1)
    start = jnp.stack([first // 8, bit, number]).astype(jnp.int32)

    (
        grads,
        extra,
        norms,
        output,
        gmid,
        kept,
        sent,
        weights,
        query,
        key,
        value,
        normed,
        xhat,
        rstd,
    ) = run_forward(start, x_vis, padded_pos, table, params, cotangent, rows, fc_chunk * groups)
    fc = add_received(kept, across_core(sent)).astype(bf16)
    fc, query = lax.optimization_barrier((fc, query))
    fc = swap(fc)
    saved = (query, key, value, grads, extra, weights, normed, xhat, rstd, gmid)
    proj_kept0, proj_sent0, *handed = run_backward(
        start, saved, x_vis, padded_pos, w_qkv, ln1_gain, rows, qkv_half, 0, clips - 1, None
    )
    fc, handed = lax.optimization_barrier((spread(total_of(fc), groups), handed))
    fc = swap(fc).reshape(groups * fc_chunk, PAIR)
    kept, sent, proj_kept1, proj_sent1 = run_backward(
        start, saved, x_vis, padded_pos, w_qkv, ln1_gain, rows, qkv_half, clips - 1, 1, handed
    )
    fc, received = lax.optimization_barrier((fc, across_core(sent)))
    w_out_g, w_fc1_g, w_fc2_g, b_out_g, gain2_g, bias2_g, b_fc1_g, b_fc2_g, means = (
        run_assemble_fc(start, fc, across_core(fc))
    )
    qkv, means = scatter(kept, received, means)
    planes = gather(qkv)
    planes += [across_core(plane) for plane in planes]
    proj_kept = jnp.concatenate([proj_kept0, proj_kept1])
    proj_sent = jnp.concatenate([proj_sent0, proj_sent1])
    part = add_received(proj_kept, across_core(proj_sent)).astype(bf16)
    part = add_received(part, lax.ppermute(part, "seq", chip_pairs)).astype(bf16)
    other = across_core(part)
    grad_projected = jnp.where(
        bit == 0,
        jnp.concatenate([part, other], axis=1),
        jnp.concatenate([other, part], axis=1),
    )[:, :visible]
    grad_x = lax.dot_general(
        grad_projected, w_proj, (((2,), (1,)), ((), ())), preferred_element_type=f32
    )
    (
        w_proj_g,
        w_qkv_g,
        b_proj_g,
        mask_g,
        gain1_g,
        bias1_g,
        q_bias_g,
        v_bias_g,
        trust,
        trust_qkv,
    ) = run_assemble_qkv(start, planes, norms, means, far, qkv_chunk)
    return (
        output.reshape(clips, rows, D),
        grad_x,
        w_proj_g,
        b_proj_g,
        mask_g,
        gain1_g,
        bias1_g,
        w_qkv_g,
        q_bias_g,
        v_bias_g,
        w_out_g,
        b_out_g,
        gain2_g,
        bias2_g,
        w_fc1_g,
        b_fc1_g,
        w_fc2_g,
        b_fc2_g,
        trust,
        trust_qkv,
    )


def solution(mesh):
    return jax.shard_map(
        shards,
        mesh=mesh,
        in_specs=(P("clip", None, None), P("clip", None))
        + (P(),) * 16
        + (P("clip", "seq", None),),
        out_specs=(P("clip", "seq", None), P("clip", None, None)) + (P(),) * 18,
        check_vma=False,
    )
```
